256 devices in a mesh: lon: 32 (over y, z), lat: 8 (over x, core).
Axes of the slice: x: 4, y: 4, z: 8, core: 2. Of those that a mesh axis runs over, the one named last changes fastest.
Arguments:
- forcing: float32 [512, 8192], P('lat', 'lon'), may hold values from -27 to 27
- surface_term: float32 [512, 8192], P('lat', 'lon'), may hold values from 0.001 to 0.025
- sea_cells: int32 [512, 8192], P('lat', 'lon'), may hold values from 0 to 1, as said below
- levels: int32 [512, 8192], P('lat', 'lon'), may hold values from 4 to 60
Outputs:
- solution: float32 [512, 8192], P('lat', 'lon')
- residual: float32 [512, 8192], P('lat', 'lon')
The draws below stay inside these ranges and needn't reach their ends.
Inputs may be any that keep to these rules, and one draw needn't show every extreme that they name: `sea_cells`: land (0) lies only at cells whose row and longitude index, counted from 0, are both even.
All inputs are finite; a program needn't handle non-finite values.
Results may differ from the reference program's by a relative error of at most 0.0003.
Values sent between devices are 32-bit elements; how exact they have to be, the bound alone decides.
A program may use at most 64 MiB of HBM per device.

```python
import math
import jax
import jax.numpy as jnp

LEVELS = 3
SWEEPS = 2
BOTTOM_ITERS = 6
VLEV = 60
NX = 8192
NY = 512


LOG_THREE = math.log(3.0)


def draw_forcing(key, part):
    base = jax.random.fold_in(key, 101)
    keys = jax.random.split(base, 3)
    cols = jnp.arange(NX, dtype=jnp.float32)[None, :] / NX
    row_scale = jnp.exp(jax.random.uniform(keys[1], (NY, 1), jnp.float32, -1.15, 1.15))
    col_scale = jnp.exp(jax.random.uniform(keys[2], (1, NX), jnp.float32, -1.15, 1.15))
    rough = jnp.clip(jax.random.normal(keys[0], (NY, NX), jnp.float32), -4.0, 4.0)
    trend = jnp.exp(0.5 * LOG_THREE * (cols - 0.5))
    return 0.5 * rough * row_scale * col_scale * trend


def draw_surface_term(key, part):
    base = jax.random.fold_in(key, 202)
    keys = jax.random.split(base, 2)
    cols = jnp.arange(NX, dtype=jnp.float32)[None, :] / NX
    rows = jnp.arange(NY, dtype=jnp.float32)[:, None] / NY
    phases = jax.random.uniform(keys[1], (2,), jnp.float32, 0.0, 2.0 * math.pi)
    region = jnp.cos(6.0 * math.pi * cols + phases[0]) * jnp.cos(math.pi * rows + phases[1])
    single = jax.random.uniform(keys[0], (NY, NX), jnp.float32, -1.0, 1.0)
    return 0.006 * jnp.exp(0.8 * single + 0.6 * region)


def draw_sea_cells(key, part):
    base = jax.random.fold_in(key, 303)
    rows = jnp.arange(NY, dtype=jnp.int32)[:, None]
    cols = jnp.arange(NX, dtype=jnp.int32)[None, :]
    lattice = (rows % 2 == 0) & (cols % 2 == 0)
    picked = jax.random.randint(base, (NY, NX), 0, 5)
    land = lattice & (picked < 4)
    return jnp.where(land, 0, 1).astype(jnp.int32)


def place_ends(result, own_key, least, high):
    dims = result.shape
    place = [jax.random.randint(jax.random.fold_in(own_key, axis), (), 0, dims[axis]) for axis in range(len(dims))]
    result = result.at[tuple(place)].set(least)
    longest = dims.index(max(dims))
    place[longest] = (place[longest] + 1) % dims[longest]
    return result.at[tuple(place)].set(high)


def setup_inputs(seed: int = 0) -> dict:
    key_of = jax.random.split(jax.random.key(seed), 5)
    forcing = draw_forcing(jax.random.fold_in(key_of[4], 71), 0)
    surface_term = draw_surface_term(jax.random.fold_in(key_of[4], 71), 0)
    sea_cells = draw_sea_cells(jax.random.fold_in(key_of[4], 71), 0)
    levels = place_ends(jax.random.randint(key_of[3], (NY, NX), 4, VLEV + 1), jax.random.fold_in(key_of[3], 1), 4, VLEV).astype(jnp.int32)
    return dict(forcing=forcing, surface_term=surface_term, sea_cells=sea_cells, levels=levels)


DAMPING = 0.8
ROW_STEP = 150.0 / 8640.0
BAND_SOUTH = -50.0


def depth_of(levels, sea_mask):
    layers = levels.astype(jnp.float32)
    return sea_mask * ((layers + layers * (layers - 1.0) / 20.0) / 200.0)


def metric(first_row, row_count):
    row_index = first_row + jnp.arange(row_count, dtype=jnp.float32)[:, None]
    center = jnp.cos(jnp.deg2rad(BAND_SOUTH + ROW_STEP * (row_index + 0.5)))
    northern = jnp.cos(jnp.deg2rad(BAND_SOUTH + ROW_STEP * (row_index + 1.0)))
    return center, northern


def stencil(field, east_val, west_val, north_val, south_val, coeffs):
    return coeffs[4] * field - (coeffs[0] * east_val + coeffs[1] * west_val + coeffs[2] * north_val + coeffs[3] * south_val)


def coarsen(east_face, north_face, source_term, sea_mask):
    east_next = east_face[0::2, 1::2] + east_face[1::2, 1::2]
    north_next = north_face[1::2, 0::2] + north_face[1::2, 1::2]
    source_next = source_term[0::2, 0::2] + source_term[1::2, 0::2] + source_term[0::2, 1::2] + source_term[1::2, 1::2]
    mask_next = jnp.maximum(jnp.maximum(sea_mask[0::2, 0::2], sea_mask[1::2, 0::2]), jnp.maximum(sea_mask[0::2, 1::2], sea_mask[1::2, 1::2]))
    return east_next, north_next, source_next, mask_next


def restrict(field):
    return field[0::2, 0::2] + field[1::2, 0::2] + field[0::2, 1::2] + field[1::2, 1::2]


def prolong(field, sea_mask):
    return jnp.repeat(jnp.repeat(field, 2, axis=0), 2, axis=1) * sea_mask


def with_diagonal(east_face, west_face, north_face, south_face, source_term, sea_mask):
    diagonal = sea_mask * (source_term + east_face + west_face + north_face + south_face) + (1.0 - sea_mask)
    return (east_face, west_face, north_face, south_face, diagonal, 1.0 / diagonal)


def shifted(field):
    zero_row = jnp.zeros_like(field[:1])
    east_val = jnp.roll(field, -1, axis=1)
    west_val = jnp.roll(field, 1, axis=1)
    north_val = jnp.concatenate([field[1:], zero_row], axis=0)
    south_val = jnp.concatenate([zero_row, field[:-1]], axis=0)
    return east_val, west_val, north_val, south_val


def apply_op(field, coeffs):
    east_val, west_val, north_val, south_val = shifted(field)
    return stencil(field, east_val, west_val, north_val, south_val, coeffs)


def finish(east_face, north_face, source_term, sea_mask):
    west_face = jnp.roll(east_face, 1, axis=1)
    south_face = jnp.concatenate([jnp.zeros_like(north_face[:1]), north_face[:-1]], axis=0)
    return with_diagonal(east_face, west_face, north_face, south_face, source_term, sea_mask)


def smooth(field, source, coeffs):
    return field + DAMPING * coeffs[5] * (source - apply_op(field, coeffs))


def reference(forcing, surface_term, sea_cells, levels):
    sea_mask = sea_cells.astype(jnp.float32)
    depth = depth_of(levels, sea_mask)
    center, northern = metric(0.0, NY)
    east_depth, west_depth, north_depth, south_depth = shifted(depth)
    east_face = jnp.minimum(depth, east_depth) / center
    north_face = jnp.minimum(depth, north_depth) * northern
    source_term = surface_term * center * sea_mask
    coeff_list = []
    mask_list = []
    for level_index in range(LEVELS + 1):
        coeff_list.append(finish(east_face, north_face, source_term, sea_mask))
        mask_list.append(sea_mask)
        if level_index < LEVELS:
            east_face, north_face, source_term, sea_mask = coarsen(east_face, north_face, source_term, sea_mask)
    source = forcing * mask_list[0]
    first_source = source
    sources = []
    iterates = []
    for level_index in range(LEVELS):
        coeffs = coeff_list[level_index]
        field = DAMPING * coeffs[5] * source
        for sweep_index in range(SWEEPS - 1):
            field = smooth(field, source, coeffs)
        sources.append(source)
        iterates.append(field)
        source = restrict(source - apply_op(field, coeffs))
    coeffs = coeff_list[LEVELS]
    iterate = jnp.zeros_like(source)
    remain = source
    direction = source
    norm_now = jnp.sum(remain * remain)
    for sweep_index in range(BOTTOM_ITERS):
        image = apply_op(direction, coeffs)
        step_size = norm_now / jnp.sum(direction * image)
        iterate = iterate + step_size * direction
        remain = remain - step_size * image
        norm_next = jnp.sum(remain * remain)
        direction = remain + (norm_next / norm_now) * direction
        norm_now = norm_next
    correction = iterate
    for level_index in range(LEVELS - 1, -1, -1):
        coeffs = coeff_list[level_index]
        field = iterates[level_index] + prolong(correction, mask_list[level_index])
        for sweep_index in range(SWEEPS):
            field = smooth(field, sources[level_index], coeffs)
        correction = field
    residual = first_source - apply_op(correction, coeff_list[0])
    return correction, residual
```

```python
import functools
import math

import jax
import jax.numpy as jnp
from jax import lax
from jax.experimental import pallas as pl
from jax.experimental.pallas import tpu as pltpu
from jax.sharding import PartitionSpec as P

MESH = pl.DeviceIdType.MESH
DAMPING = 0.8
ROW_STEP = 150.0 / 8640.0
BAND_SOUTH = -50.0
BAND_ROWS = 512
BOTTOM_ITERS = 6
CORES = 2
RING = 8

ROWS, COLS = 64, 256
RIM = 32
PAD = 8
LANES = 128
CHUNK = 32


def lane_of(rows):
    return lax.broadcasted_iota(jnp.int32, (rows, LANES), 1)


def east_of(cols, shift, lane):
    count = len(cols)
    return [
        pltpu.roll(jnp.where(lane < shift, cols[(c + 1) % count], cols[c]), LANES - shift, 1)
        for c in range(count)
    ]


def west_of(cols, shift, lane):
    count = len(cols)
    return [
        pltpu.roll(jnp.where(lane >= LANES - shift, cols[(c - 1) % count], cols[c]), shift, 1)
        for c in range(count)
    ]


def pair_sum(value, shift, lane):
    upper = (lane & shift) != 0
    return value + jnp.where(upper, pltpu.roll(value, shift, 1), pltpu.roll(value, LANES - shift, 1))


def upper_of(value, shift, lane):
    return jnp.where((lane & shift) != 0, value, pltpu.roll(value, LANES - shift, 1))


def cosines(row):
    middle = math.radians(BAND_SOUTH + ROW_STEP * (BAND_ROWS / 2))
    off = (row - BAND_ROWS / 2) * math.radians(ROW_STEP)
    sq = off * off
    cos_off = 1.0 - sq * (1.0 / 2 - sq * (1.0 / 24 - sq * (1.0 / 720)))
    sin_off = off * (1.0 - sq * (1.0 / 6 - sq * (1.0 / 120 - sq * (1.0 / 5040))))
    return math.cos(middle) * cos_off - math.sin(middle) * sin_off


class Level:
    def __init__(self, index, refs):
        self.index = index
        self.shift = 1 << index
        self.rows = (ROWS + 2 * RIM) >> index
        self.rim = RIM >> index
        self.east, self.west, self.north, self.source, self.diag, self.scale, self.rhs, self.va, self.vb, self.tmp = refs
        self.chunk = min(CHUNK, self.rows)

    def chunks(self):
        return range(0, self.rows, self.chunk)

    def load(self, ref, col, row, count):
        return ref[col, pl.ds(PAD + row, count), :]

    def apply(self, ref, row, count, cols=3):
        lane = lane_of(count)
        value = [self.load(ref, c, row, count) for c in range(3)]
        east = east_of(value, self.shift, lane)
        west = west_of(value, self.shift, lane)
        out = []
        for c in range(cols):
            around = (
                self.load(self.east, c, row, count) * east[c]
                + self.load(self.west, c, row, count) * west[c]
                + self.load(self.north, c, row, count) * self.load(ref, c, row + 1, count)
                + self.load(self.north, c, row - 1, count) * self.load(ref, c, row - 1, count)
            )
            out.append(self.load(self.diag, c, row, count) * value[c] - around)
        return value, out

    def smooth(self, source_ref, target_ref):
        for row in self.chunks():
            value, image = self.apply(source_ref, row, self.chunk)
            for c in range(3):
                rest = self.load(self.rhs, c, row, self.chunk) - image[c]
                target_ref[c, pl.ds(PAD + row, self.chunk), :] = (
                    value[c] + self.load(self.scale, c, row, self.chunk) * rest
                )

    def finish(self):
        n = self.chunk
        lane = lane_of(n)
        for row in self.chunks():
            east = [self.load(self.east, c, row, n) for c in range(3)]
            west = west_of(east, self.shift, lane)
            for c in range(3):
                source = self.load(self.source, c, row, n)
                total = (
                    source + east[c] + west[c]
                    + self.load(self.north, c, row, n) + self.load(self.north, c, row - 1, n)
                )
                diag = jnp.where(source > 0.0, total, 1.0)
                self.west[c, pl.ds(PAD + row, n), :] = west[c]
                self.diag[c, pl.ds(PAD + row, n), :] = diag
                self.scale[c, pl.ds(PAD + row, n), :] = DAMPING / diag

    def pairs(self, ref, col, row, count):
        return (
            ref[col, pl.ds(PAD + 2 * row, count, stride=2), :],
            ref[col, pl.ds(PAD + 2 * row + 1, count, stride=2), :],
        )

    def coarse_faces(self, col, row, count):
        lane = lane_of(count)
        lower, upper = self.pairs(self.east, col, row, count)
        east = upper_of(lower + upper, self.shift, lane)
        _, upper = self.pairs(self.north, col, row, count)
        north = pair_sum(upper, self.shift, lane)
        lower, upper = self.pairs(self.source, col, row, count)
        return east, north, pair_sum(lower + upper, self.shift, lane)

    def coarse_rhs(self, col, row, count):
        lower, upper = self.pairs(self.tmp, col, row, count)
        return pair_sum(lower + upper, self.shift, lane_of(count))

    def descend(self):
        n = self.chunk
        for row in self.chunks():
            for c in range(3):
                self.vb[c, pl.ds(PAD + row, n), :] = self.load(self.scale, c, row, n) * self.load(self.rhs, c, row, n)
        self.smooth(self.vb, self.va)
        for row in self.chunks():
            _, image = self.apply(self.va, row, n)
            for c in range(3):
                self.tmp[c, pl.ds(PAD + row, n), :] = self.load(self.rhs, c, row, n) - image[c]

    def rise(self, coarse, offset, masked):
        half = self.rows // 2
        n = min(CHUNK, half)
        for row in range(0, half, n):
            for c in range(3):
                added = coarse[c, pl.ds(offset + row, n), :]
                for odd in range(2):
                    at = pl.ds(PAD + 2 * row + odd, n, stride=2)
                    own = jnp.where(self.source[c, at, :] > 0.0, added, 0.0) if masked else added
                    self.va[c, at, :] = self.va[c, at, :] + own
        self.smooth(self.va, self.vb)
        self.smooth(self.vb, self.va)


def body(
    shape, forcing, surface, sea, depth_levels, solution_out, residual_out,
    in_f, in_i, fields, *rest
):
    lat_count, lon_count, ring = shape
    level_refs = [rest[0:7], rest[7:17], rest[17:27]]
    (
        west_pack, east_pack, east_rim, west_rim, metric,
        face_slots, rhs_slots, faces, rhs, bottom, wide, piece,
        in_sem, out_sem, rim_send, rim_recv, slot_send, slot_recv,
        plane_send, plane_recv, pass_send, pass_recv,
    ) = rest[27:]
    planes_y = lon_count // ring
    planes_x = lat_count // CORES
    la, lo = lax.axis_index("lat"), lax.axis_index("lon")
    x, core = la // CORES, la % CORES
    y, z = lo // ring, lo % ring
    tiles = lon_count * (COLS >> 3) // LANES
    own_rows = ROWS >> 3
    group = LANES // (COLS >> 3)

    depth = fields.at[0]
    levels = [
        Level(0, (*level_refs[0][0:3], fields.at[2], *level_refs[0][3:5], fields.at[1], *level_refs[0][5:7], wide)),
        Level(1, level_refs[1]),
        Level(2, level_refs[2]),
    ]

    def device(lat, lon):
        return {"lat": lat, "lon": lon}

    loads = []
    for k, ref in enumerate((forcing, surface)):
        for c in range(2):
            loads.append(pltpu.make_async_copy(ref.at[:, pl.ds(c * LANES, LANES)], in_f.at[k, c], in_sem))
    for k, ref in enumerate((sea, depth_levels)):
        for c in range(2):
            loads.append(pltpu.make_async_copy(ref.at[:, pl.ds(c * LANES, LANES)], in_i.at[k, c], in_sem))
    for load in loads:
        load.start()

    rims = [(dy, dx) for dy in (-1, 0, 1) for dx in (-1, 0, 1) if (dy, dx) != (0, 0)]
    hops = sorted(
        ((dx, dy) for dx in range(planes_x) for dy in range(planes_y) if (dx, dy) != (0, 0)),
        key=lambda d: min(d[0], planes_x - d[0]) + min(d[1], planes_y - d[1]),
    )
    barrier = pltpu.get_barrier_semaphore()

    def greet(lat, lon):
        pl.semaphore_signal(barrier, inc=1, device_id=device(lat, lon), device_id_type=MESH)

    def beside(dy, dx):
        return la + dy, lax.rem(lo + dx + lon_count, lon_count)

    def ring_peer(step):
        return la, y * ring + lax.rem(z + step, ring)

    def plane_peer(dx, dy):
        return lax.rem(x + dx, planes_x) * CORES + core, lax.rem(y + dy, planes_y) * ring + z

    partner = (x * CORES + (1 - core), lo)
    inside = {-1: la > 0, 0: None, 1: la < lat_count - 1}

    def where_inside(dy, act):
        if dy == 0:
            act()
        else:
            pl.when(inside[dy])(act)

    for dy, dx in rims:
        where_inside(dy, lambda dy=dy, dx=dx: greet(*beside(dy, dx)))
    for step in range(1, ring):
        greet(*ring_peer(step))
    for dx, dy in hops:
        greet(*plane_peer(dx, dy))
    greet(*partner)

    def clear(ref, col, row, count):
        ref[col, pl.ds(row, count), :] = jnp.zeros((count, LANES), ref.dtype)

    for k in range(3):
        clear_to = fields.at[k]
        for c in range(3):
            clear(clear_to, c, 0, PAD)
            clear(clear_to, c, PAD + ROWS + 2 * RIM, PAD)
    for level in levels:
        for ref in (level.north, level.va, level.vb):
            for c in range(3):
                clear(ref, c, 0, PAD)
                clear(ref, c, PAD + level.rows, PAD)
    for ref in (faces.at[1], rhs, bottom.at[0]):
        for t in range(tiles):
            clear(ref, t, 0, PAD)
            clear(ref, t, PAD + lat_count * own_rows, PAD)
    for dy, row in ((-1, 0), (1, RIM + ROWS)):

        @pl.when(jnp.logical_not(inside[dy]))
        def _(row=row):
            for k in range(3):
                for c in range(2):
                    clear(fields.at[k], c, PAD + row, RIM)
            east_rim[pl.ds(row, RIM), :] = jnp.zeros((RIM, LANES), jnp.float32)
            west_rim[pl.ds(row, RIM), :] = jnp.zeros((RIM, LANES), jnp.float32)

    first = la * ROWS - RIM
    for row in range(0, ROWS + 2 * RIM, CHUNK):
        number = (first + row + lax.broadcasted_iota(jnp.int32, (CHUNK, LANES), 0)).astype(jnp.float32)
        metric[0, pl.ds(row, CHUNK), :] = cosines(number + 0.5)
        metric[1, pl.ds(row, CHUNK), :] = cosines(number + 1.0)

    for load in loads:
        load.wait()
    for row in range(0, ROWS, CHUNK):
        at = pl.ds(PAD + RIM + row, CHUNK)
        center = metric[0, pl.ds(RIM + row, CHUNK), :]
        own = pl.ds(row, CHUNK)
        lane = lane_of(CHUNK)
        values = []
        for c in range(2):
            sea_mask = in_i[0, c, own, :].astype(jnp.float32)
            layers = in_i[1, c, own, :].astype(jnp.float32)
            deep = sea_mask * ((layers + layers * (layers - 1.0) / 20.0) / 200.0)
            right = in_f[0, c, own, :] * sea_mask
            source = in_f[1, c, own, :] * center * sea_mask
            values.append((deep, right, source))
            for k in range(3):
                fields[k, c, at, :] = values[c][k]
        packed_west, packed_east = values[0][0], values[1][0]
        for k in range(1, 3):
            part = (lane >= RIM * k) & (lane < RIM * (k + 1))
            packed_west = jnp.where(part, pltpu.roll(values[0][k], RIM * k, 1), packed_west)
            part = (lane < LANES - RIM * k) & (lane >= LANES - RIM * (k + 1))
            packed_east = jnp.where(part, pltpu.roll(values[1][k], LANES - RIM * k, 1), packed_east)
        west_pack[own, :] = packed_west
        east_pack[own, :] = packed_east

    greeted = 2 + (ring - 1) + len(hops) + 1
    both = inside[-1].astype(jnp.int32) + inside[1].astype(jnp.int32)
    pl.semaphore_wait(barrier, greeted + 3 * both)

    def rim_copy(dy, dx):
        source_row, target_row = {1: (ROWS - RIM, 0), -1: (0, RIM + ROWS), 0: (0, RIM)}[dy]
        count = ROWS if dy == 0 else RIM
        if dx == 0:
            source = fields.at[:, pl.ds(0, 2), pl.ds(PAD + RIM + source_row, count), :]
            target = fields.at[:, pl.ds(0, 2), pl.ds(PAD + target_row, count), :]
        else:
            source = (east_pack if dx > 0 else west_pack).at[pl.ds(source_row, count), :]
            target = (west_rim if dx > 0 else east_rim).at[pl.ds(target_row, count), :]
        k = rims.index((dy, dx))
        return pltpu.make_async_remote_copy(
            source, target, rim_send.at[k], rim_recv.at[k],
            device_id=device(*beside(dy, dx)), device_id_type=MESH,
        )

    order = sorted(rims, key=lambda d: (d[1] == 0, d[0] == 0))
    for dy, dx in order:
        where_inside(dy, lambda dy=dy, dx=dx: rim_copy(dy, dx).start())
    for dy, dx in order:
        where_inside(-dy, lambda dy=dy, dx=dx: rim_copy(dy, dx).wait_recv())

    for row in range(0, ROWS + 2 * RIM, CHUNK):
        lane = lane_of(CHUNK)
        east, west = east_rim[pl.ds(row, CHUNK), :], west_rim[pl.ds(row, CHUNK), :]
        for k in range(3):
            moved_east = pltpu.roll(east, LANES - RIM * k, 1) if k else east
            moved_west = pltpu.roll(west, RIM * k, 1) if k else west
            fields[k, 2, pl.ds(PAD + row, CHUNK), :] = jnp.where(
                lane < RIM, moved_east, jnp.where(lane >= LANES - RIM, moved_west, 0.0)
            )

    top = levels[0]
    for row in top.chunks():
        n = top.chunk
        deep = [top.load(depth, c, row, n) for c in range(3)]
        east = east_of(deep, 1, lane_of(n))
        inverse = 1.0 / metric[0, pl.ds(row, n), :]
        northern = metric[1, pl.ds(row, n), :]
        for c in range(3):
            at = pl.ds(PAD + row, n)
            top.east[c, at, :] = jnp.minimum(deep[c], east[c]) * inverse
            top.north[c, at, :] = jnp.minimum(deep[c], top.load(depth, c, row + 1, n)) * northern
    for fine, coarse in zip(levels, levels[1:]):
        for row in coarse.chunks():
            for c in range(3):
                at = pl.ds(PAD + row, coarse.chunk)
                coarse.east[c, at, :], coarse.north[c, at, :], coarse.source[c, at, :] = fine.coarse_faces(c, row, coarse.chunk)

    lane = lane_of(own_rows)
    pick = (lane % 16) * 8
    low = (lane % 32) < 16

    def dense(west_tile, east_tile):
        return jnp.where(
            low, jnp.take_along_axis(west_tile, pick, axis=1), jnp.take_along_axis(east_tile, pick, axis=1)
        )

    own3 = RIM >> 3
    bottom_faces = [levels[2].coarse_faces(c, own3, own_rows) for c in range(2)]
    parts = [dense(bottom_faces[0][k], bottom_faces[1][k]) for k in range(3)]
    face_slots[z] = jnp.where(lane < 32, parts[0], jnp.where(lane < 64, parts[1], parts[2]))

    def slot_copy(slots, which, step):
        return pltpu.make_async_remote_copy(
            slots.at[z], slots.at[z], slot_send.at[which], slot_recv.at[which],
            device_id=device(*ring_peer(step)), device_id_type=MESH,
        )

    def all_slots(slots, which):
        return pltpu.make_async_remote_copy(
            slots.at[pl.ds(0, ring - 1)], slots.at[pl.ds(0, ring - 1)], slot_send.at[which], slot_recv.at[which],
            device_id=device(*ring_peer(1)), device_id_type=MESH,
        )

    def plane_block(which, lat, line):
        rows = pl.ds(pl.multiple_of(PAD + lat * own_rows, 8), own_rows)
        per_line = tiles // planes_y
        if which == 0:
            return faces.at[:, pl.ds(line * per_line, per_line), rows, :]
        return rhs.at[pl.ds(line * per_line, per_line), rows, :]

    def plane_copy(which, k, dx, dy):
        block = plane_block(which, la, y)
        return pltpu.make_async_remote_copy(
            block, block, plane_send.at[which, k], plane_recv.at[which, k],
            device_id=device(*plane_peer(dx, dy)), device_id_type=MESH,
        )

    def pass_copy(which, lat, line):
        block = plane_block(which, lat, line)
        return pltpu.make_async_remote_copy(
            block, block, pass_send.at[which], pass_recv.at[which],
            device_id=device(*partner), device_id_type=MESH,
        )

    def all_passed(which):
        half = pl.ds(PAD, lat_count * own_rows // CORES)
        block = faces.at[:, :, half, :] if which == 0 else rhs.at[:, half, :]
        return pltpu.make_async_remote_copy(
            block, block, pass_send.at[which], pass_recv.at[which],
            device_id=device(*partner), device_id_type=MESH,
        )

    def send_plane(which):
        for k, (dx, dy) in enumerate(hops):
            plane_copy(which, k, dx, dy).start()
        pass_copy(which, la, y).start()

    def take_plane(which):
        for k, (dx, dy) in enumerate(hops):
            plane_copy(which, k, dx, dy).wait_recv()
            pass_copy(which, *(lax.rem(x - dx + planes_x, planes_x) * CORES + core, lax.rem(y - dy + planes_y, planes_y))).start()

    for step in range(1, ring):
        slot_copy(face_slots, 0, step).start()

    levels[0].finish()
    levels[0].descend()

    all_slots(face_slots, 0).wait_recv()
    per_line = tiles // planes_y
    own_at = pl.ds(pl.multiple_of(PAD + la * own_rows, 8), own_rows)
    for h in range(per_line):
        for k in range(3):
            value = None
            for j in range(group):
                slot = face_slots[h * group + j]
                shift = (32 * (j - k)) % LANES
                moved = pltpu.roll(slot, shift, 1) if shift else slot
                value = moved if value is None else jnp.where(lane // 32 == j, moved, value)
            faces[k, y * per_line + h, own_at, :] = value
    send_plane(0)

    for fine, coarse in zip(levels, levels[1:]):
        for row in coarse.chunks():
            for c in range(3):
                coarse.rhs[c, pl.ds(PAD + row, coarse.chunk), :] = fine.coarse_rhs(c, row, coarse.chunk)
        coarse.finish()
        coarse.descend()

    bottom_rhs = [levels[2].coarse_rhs(c, own3, own_rows) for c in range(2)]
    rhs_slots[z] = dense(*bottom_rhs)
    for step in range(1, ring):
        slot_copy(rhs_slots, 1, step).start()
    all_slots(rhs_slots, 1).wait_recv()
    for h in range(per_line):
        value = None
        for j in range(group):
            slot = rhs_slots[h * group + j]
            value = slot if value is None else jnp.where(lane // 32 == j, slot, value)
        rhs[y * per_line + h, own_at, :] = value
    send_plane(1)
    take_plane(0)
    take_plane(1)

    height = lat_count * own_rows
    everything = pl.ds(PAD, height)
    lane3 = lane_of(height)
    west_face, diagonal = bottom.at[1], bottom.at[2]
    rest_ref, image_ref, along_ref = bottom.at[0], bottom.at[3], bottom.at[4]
    all_passed(0).wait_recv()
    for t in range(tiles):
        east = faces[0, t, everything, :]
        before = faces[0, (t - 1) % tiles, everything, :]
        west = pltpu.roll(jnp.where(lane3 >= LANES - 1, before, east), 1, 1)
        west_face[t, everything, :] = west
        diagonal[t, everything, :] = (
            faces[2, t, everything, :] + east + west
            + faces[1, t, everything, :] + faces[1, t, pl.ds(PAD - 1, height), :]
        )
    all_passed(1).wait_recv()

    def operate(ref):
        norm, product = None, None
        for t in range(tiles):
            value = ref[t, everything, :]
            east = pltpu.roll(jnp.where(lane3 < 1, ref[(t + 1) % tiles, everything, :], value), LANES - 1, 1)
            west = pltpu.roll(jnp.where(lane3 >= LANES - 1, ref[(t - 1) % tiles, everything, :], value), 1, 1)
            image = diagonal[t, everything, :] * value - (
                faces[0, t, everything, :] * east
                + west_face[t, everything, :] * west
                + faces[1, t, everything, :] * ref[t, pl.ds(PAD + 1, height), :]
                + faces[1, t, pl.ds(PAD - 1, height), :] * ref[t, pl.ds(PAD - 1, height), :]
            )
            image_ref[t, everything, :] = image
            square, mixed = value * value, value * image
            norm = square if norm is None else norm + square
            product = mixed if product is None else product + mixed
        return jnp.sum(norm, keepdims=True), jnp.sum(product, keepdims=True)

    own_tile = lo // group
    near_tiles = (lax.rem(own_tile - 1 + tiles, tiles), own_tile, lax.rem(own_tile + 1, tiles))
    near = pl.ds(pl.multiple_of(la * own_rows, 8), 2 * PAD + own_rows)
    solved = [None] * 3
    direction = [None] * 3
    norm, product = operate(rhs)
    alpha = norm / product
    beta = None
    for iteration in range(BOTTOM_ITERS):
        current = rhs if iteration == 0 else rest_ref
        for k in range(3):
            value = current[near_tiles[k], near, :]
            direction[k] = value if iteration == 0 else value + beta * direction[k]
            solved[k] = alpha * direction[k] if iteration == 0 else solved[k] + alpha * direction[k]
        if iteration == BOTTOM_ITERS - 1:
            break
        for t in range(tiles):
            along = image_ref[t, everything, :]
            if iteration:
                along = along + beta * along_ref[t, everything, :]
            along_ref[t, everything, :] = along
            rest_ref[t, everything, :] = current[t, everything, :] - alpha * along
        norm_next, product = operate(rest_ref)
        beta = norm_next / norm
        alpha = norm_next / (product - beta * norm_next / alpha)
        norm = norm_next

    quarter = (lo % group) * 32
    lane = lane_of(8)
    place = quarter + jnp.where(lane < LANES // 2, 32 + lane // 8, (lane - LANES) // 8)
    wrapped = place & (LANES - 1)
    for row in range(0, 2 * PAD + own_rows, 8):
        left, mine, right = (solved[k][row : row + 8] for k in range(3))
        piece[0, pl.ds(row, 8), :] = jnp.take_along_axis(mine, quarter + lane // 8, axis=1)
        piece[1, pl.ds(row, 8), :] = jnp.take_along_axis(mine, quarter + 16 + lane // 8, axis=1)
        piece[2, pl.ds(row, 8), :] = jnp.where(
            place < 0, jnp.take_along_axis(left, wrapped, axis=1),
            jnp.where(place >= LANES, jnp.take_along_axis(right, wrapped, axis=1), jnp.take_along_axis(mine, wrapped, axis=1)),
        )

    levels[2].rise(piece, PAD - own3, False)
    levels[1].rise(levels[2].va, PAD, False)
    levels[0].rise(levels[1].va, PAD, True)
    stores = []
    for c in range(2):
        stores.append(pltpu.make_async_copy(
            top.va.at[c, pl.ds(PAD + RIM, ROWS), :], solution_out.at[:, pl.ds(c * LANES, LANES)], out_sem))
        stores[-1].start()
    for row in range(RIM, RIM + ROWS, CHUNK):
        _, image = top.apply(top.va, row, CHUNK, cols=2)
        for c in range(2):
            top.tmp[c, pl.ds(PAD + row, CHUNK), :] = top.load(top.rhs, c, row, CHUNK) - image[c]
    for c in range(2):
        stores.append(pltpu.make_async_copy(
            top.tmp.at[c, pl.ds(PAD + RIM, ROWS), :], residual_out.at[:, pl.ds(c * LANES, LANES)], out_sem))
        stores[-1].start()

    for dy, dx in order:
        where_inside(dy, lambda dy=dy, dx=dx: rim_copy(dy, dx).wait_send())
    for which, slots in enumerate((face_slots, rhs_slots)):
        all_slots(slots, which).wait_send()
        for k, (dx, dy) in enumerate(hops):
            plane_copy(which, k, dx, dy).wait_send()
        all_passed(which).wait_send()
    for store in stores:
        store.wait()


def solution(mesh, ring=RING):
    lat_count, lon_count = mesh.shape["lat"], mesh.shape["lon"]
    planes = (lat_count // CORES) * (lon_count // ring)
    tiles = lon_count * (COLS >> 3) // LANES
    height = lat_count * (ROWS >> 3) + 2 * PAD
    f32 = jnp.float32

    def padded(level):
        return pltpu.VMEM((3, ((ROWS + 2 * RIM) >> level) + 2 * PAD, LANES), f32)

    rows = ROWS + 2 * RIM
    scratch = [
        pltpu.VMEM((2, 2, ROWS, LANES), f32),
        pltpu.VMEM((2, 2, ROWS, LANES), jnp.int32),
        pltpu.VMEM((3, 3, rows + 2 * PAD, LANES), f32),
        *[padded(0)] * 7,
        *[padded(1)] * 10,
        *[padded(2)] * 10,
        pltpu.VMEM((ROWS, LANES), f32),
        pltpu.VMEM((ROWS, LANES), f32),
        pltpu.VMEM((rows, LANES), f32),
        pltpu.VMEM((rows, LANES), f32),
        pltpu.VMEM((2, rows, LANES), f32),
        pltpu.VMEM((ring, 8, LANES), f32),
        pltpu.VMEM((ring, 8, LANES), f32),
        pltpu.VMEM((3, tiles, height, LANES), f32),
        pltpu.VMEM((tiles, height, LANES), f32),
        pltpu.VMEM((5, tiles, height, LANES), f32),
        padded(0),
        pltpu.VMEM((3, 2 * PAD + (ROWS >> 3), LANES), f32),
        pltpu.SemaphoreType.DMA,
        pltpu.SemaphoreType.DMA,
        pltpu.SemaphoreType.DMA((8,)),
        pltpu.SemaphoreType.DMA((8,)),
        pltpu.SemaphoreType.DMA((2,)),
        pltpu.SemaphoreType.DMA((2,)),
        pltpu.SemaphoreType.DMA((2, planes)),
        pltpu.SemaphoreType.DMA((2, planes)),
        pltpu.SemaphoreType.DMA((2,)),
        pltpu.SemaphoreType.DMA((2,)),
    ]

    def step(forcing, surface_term, sea_cells, levels):
        out = jax.ShapeDtypeStruct(forcing.shape, f32)
        return pl.pallas_call(
            functools.partial(body, (lat_count, lon_count, ring)),
            out_shape=(out, out),
            in_specs=[pl.BlockSpec(memory_space=pl.ANY)] * 4,
            out_specs=[pl.BlockSpec(memory_space=pl.ANY)] * 2,
            scratch_shapes=scratch,
            compiler_params=pltpu.CompilerParams(
                collective_id=0, has_side_effects=True, vmem_limit_bytes=48 << 20
            ),
        )(forcing, surface_term, sea_cells, levels)

    return jax.shard_map(
        step,
        mesh=mesh,
        in_specs=(P("lat", "lon"),) * 4,
        out_specs=(P("lat", "lon"),) * 2,
        check_vma=False,
    )
```

```python
import functools
import math

import jax
import jax.numpy as jnp
from jax import lax
from jax.experimental import pallas as pl
from jax.experimental.pallas import tpu as pltpu
from jax.sharding import PartitionSpec as P

MESH = pl.DeviceIdType.MESH
DAMPING = 0.8
ROW_STEP = 150.0 / 8640.0
BAND_SOUTH = -50.0
BAND_ROWS = 512
BOTTOM_ITERS = 6
CORES = 2
RING = 8

ROWS, COLS = 64, 256
RIM = 32
PAD = 8
LANES = 128
CHUNK = 32


def lane_of(rows):
    return lax.broadcasted_iota(jnp.int32, (rows, LANES), 1)


def east_of(cols, shift, lane):
    count = len(cols)
    return [
        pltpu.roll(jnp.where(lane < shift, cols[(c + 1) % count], cols[c]), LANES - shift, 1)
        for c in range(count)
    ]


def west_of(cols, shift, lane):
    count = len(cols)
    return [
        pltpu.roll(jnp.where(lane >= LANES - shift, cols[(c - 1) % count], cols[c]), shift, 1)
        for c in range(count)
    ]


def pair_sum(value, shift, lane):
    upper = (lane & shift) != 0
    return value + jnp.where(upper, pltpu.roll(value, shift, 1), pltpu.roll(value, LANES - shift, 1))


def upper_of(value, shift, lane):
    return jnp.where((lane & shift) != 0, value, pltpu.roll(value, LANES - shift, 1))


def cosines(row):
    middle = math.radians(BAND_SOUTH + ROW_STEP * (BAND_ROWS / 2))
    off = (row - BAND_ROWS / 2) * math.radians(ROW_STEP)
    sq = off * off
    cos_off = 1.0 - sq * (1.0 / 2 - sq * (1.0 / 24 - sq * (1.0 / 720)))
    sin_off = off * (1.0 - sq * (1.0 / 6 - sq * (1.0 / 120 - sq * (1.0 / 5040))))
    return math.cos(middle) * cos_off - math.sin(middle) * sin_off


class Level:
    def __init__(self, index, refs):
        self.index = index
        self.shift = 1 << index
        self.rows = (ROWS + 2 * RIM) >> index
        self.rim = RIM >> index
        self.east, self.west, self.north, self.source, self.diag, self.scale, self.rhs, self.va, self.vb, self.tmp = refs
        self.chunk = min(CHUNK, self.rows)

    def chunks(self):
        return range(0, self.rows, self.chunk)

    def load(self, ref, col, row, count):
        return ref[col, pl.ds(PAD + row, count), :]

    def apply(self, ref, row, count, cols=3):
        lane = lane_of(count)
        value = [self.load(ref, c, row, count) for c in range(3)]
        east = east_of(value, self.shift, lane)
        west = west_of(value, self.shift, lane)
        out = []
        for c in range(cols):
            around = (
                self.load(self.east, c, row, count) * east[c]
                + self.load(self.west, c, row, count) * west[c]
                + self.load(self.north, c, row, count) * self.load(ref, c, row + 1, count)
                + self.load(self.north, c, row - 1, count) * self.load(ref, c, row - 1, count)
            )
            out.append(self.load(self.diag, c, row, count) * value[c] - around)
        return value, out

    def smooth(self, source_ref, target_ref):
        for row in self.chunks():
            value, image = self.apply(source_ref, row, self.chunk)
            for c in range(3):
                rest = self.load(self.rhs, c, row, self.chunk) - image[c]
                target_ref[c, pl.ds(PAD + row, self.chunk), :] = (
                    value[c] + self.load(self.scale, c, row, self.chunk) * rest
                )

    def finish(self):
        n = self.chunk
        lane = lane_of(n)
        for row in self.chunks():
            east = [self.load(self.east, c, row, n) for c in range(3)]
            west = west_of(east, self.shift, lane)
            for c in range(3):
                source = self.load(self.source, c, row, n)
                total = (
                    source + east[c] + west[c]
                    + self.load(self.north, c, row, n) + self.load(self.north, c, row - 1, n)
                )
                diag = jnp.where(source > 0.0, total, 1.0)
                self.west[c, pl.ds(PAD + row, n), :] = west[c]
                self.diag[c, pl.ds(PAD + row, n), :] = diag
                self.scale[c, pl.ds(PAD + row, n), :] = DAMPING / diag

    def pairs(self, ref, col, row, count):
        return (
            ref[col, pl.ds(PAD + 2 * row, count, stride=2), :],
            ref[col, pl.ds(PAD + 2 * row + 1, count, stride=2), :],
        )

    def coarse_faces(self, col, row, count):
        lane = lane_of(count)
        lower, upper = self.pairs(self.east, col, row, count)
        east = upper_of(lower + upper, self.shift, lane)
        _, upper = self.pairs(self.north, col, row, count)
        north = pair_sum(upper, self.shift, lane)
        lower, upper = self.pairs(self.source, col, row, count)
        return east, north, pair_sum(lower + upper, self.shift, lane)

    def coarse_rhs(self, col, row, count):
        lower, upper = self.pairs(self.tmp, col, row, count)
        return pair_sum(lower + upper, self.shift, lane_of(count))

    def descend(self):
        n = self.chunk
        for row in self.chunks():
            for c in range(3):
                self.vb[c, pl.ds(PAD + row, n), :] = self.load(self.scale, c, row, n) * self.load(self.rhs, c, row, n)
        self.smooth(self.vb, self.va)
        for row in self.chunks():
            _, image = self.apply(self.va, row, n)
            for c in range(3):
                self.tmp[c, pl.ds(PAD + row, n), :] = self.load(self.rhs, c, row, n) - image[c]

    def rise(self, coarse, offset, masked):
        half = self.rows // 2
        n = min(CHUNK, half)
        for row in range(0, half, n):
            for c in range(3):
                added = coarse[c, pl.ds(offset + row, n), :]
                for odd in range(2):
                    at = pl.ds(PAD + 2 * row + odd, n, stride=2)
                    own = jnp.where(self.source[c, at, :] > 0.0, added, 0.0) if masked else added
                    self.va[c, at, :] = self.va[c, at, :] + own
        self.smooth(self.va, self.vb)
        self.smooth(self.vb, self.va)


def body(
    shape, forcing, surface, sea, depth_levels, solution_out, residual_out,
    in_f, in_i, fields, *rest
):
    lat_count, lon_count, ring = shape
    level_refs = [rest[0:7], rest[7:17], rest[17:27]]
    (
        west_pack, east_pack, east_rim, west_rim, metric,
        face_slots, rhs_slots, faces, rhs, bottom, wide, piece,
        in_sem, out_sem, rim_send, rim_recv, slot_send, slot_recv,
        plane_send, plane_recv, pass_send, pass_recv,
    ) = rest[27:]
    planes_y = lon_count // ring
    planes_x = lat_count // CORES
    tiles = lon_count * (COLS >> 3) // LANES
    per_line = tiles // planes_y
    la, lo = lax.axis_index("lat"), lax.axis_index("lon")
    x, core = la // CORES, la % CORES
    y, z = lo // ring, lo % ring
    own_rows = ROWS >> 3
    group = LANES // (COLS >> 3)

    depth = fields.at[0]
    levels = [
        Level(0, (*level_refs[0][0:3], fields.at[2], *level_refs[0][3:5], fields.at[1], *level_refs[0][5:7], wide)),
        Level(1, level_refs[1]),
        Level(2, level_refs[2]),
    ]

    def device(lat, lon):
        return {"lat": lat, "lon": lon}

    loads = []
    for k, ref in enumerate((forcing, surface)):
        for c in range(2):
            loads.append(pltpu.make_async_copy(ref.at[:, pl.ds(c * LANES, LANES)], in_f.at[k, c], in_sem))
    for k, ref in enumerate((sea, depth_levels)):
        for c in range(2):
            loads.append(pltpu.make_async_copy(ref.at[:, pl.ds(c * LANES, LANES)], in_i.at[k, c], in_sem))
    for load in loads:
        load.start()

    rims = [(dy, dx) for dy in (-1, 0, 1) for dx in (-1, 0, 1) if (dy, dx) != (0, 0)]
    hops = sorted(
        ((dx, dy) for dx in range(planes_x) for dy in range(planes_y) if (dx, dy) != (0, 0)),
        key=lambda d: -min(d[0], planes_x - d[0]) - min(d[1], planes_y - d[1]),
    )
    ring_steps = sorted(range(1, ring), key=lambda d: -min(d, ring - d))
    barrier = pltpu.get_barrier_semaphore()

    def greet(lat, lon):
        pl.semaphore_signal(barrier, inc=1, device_id=device(lat, lon), device_id_type=MESH)

    def beside(dy, dx):
        return la + dy, lax.rem(lo + dx + lon_count, lon_count)

    def ring_peer(step):
        return la, y * ring + lax.rem(z + step, ring)

    def plane_peer(dx, dy):
        return lax.rem(x + dx, planes_x) * CORES + core, lax.rem(y + dy, planes_y) * ring + z

    partner = (x * CORES + (1 - core), lo)
    inside = {-1: la > 0, 0: None, 1: la < lat_count - 1}

    def where_inside(dy, act):
        if dy == 0:
            act()
        else:
            pl.when(inside[dy])(act)

    for dy, dx in rims:
        where_inside(dy, lambda dy=dy, dx=dx: greet(*beside(dy, dx)))
    for step in ring_steps:
        greet(*ring_peer(step))
    for dx, dy in hops:
        greet(*plane_peer(dx, dy))
    greet(*partner)

    def clear(ref, col, row, count):
        ref[col, pl.ds(row, count), :] = jnp.zeros((count, LANES), ref.dtype)

    for k in range(3):
        clear_to = fields.at[k]
        for c in range(3):
            clear(clear_to, c, 0, PAD)
            clear(clear_to, c, PAD + ROWS + 2 * RIM, PAD)
    for level in levels:
        for ref in (level.north, level.va, level.vb):
            for c in range(3):
                clear(ref, c, 0, PAD)
                clear(ref, c, PAD + level.rows, PAD)
    for ref, count in ((faces.at[1], tiles), (rhs, tiles + planes_y), (bottom.at[0], tiles)):
        for t in range(count):
            clear(ref, t, 0, PAD)
            clear(ref, t, PAD + lat_count * own_rows, PAD)
    for dy, row in ((-1, 0), (1, RIM + ROWS)):

        @pl.when(jnp.logical_not(inside[dy]))
        def _(row=row):
            for k in range(3):
                for c in range(2):
                    clear(fields.at[k], c, PAD + row, RIM)
            east_rim[pl.ds(row, RIM), :] = jnp.zeros((RIM, LANES), jnp.float32)
            west_rim[pl.ds(row, RIM), :] = jnp.zeros((RIM, LANES), jnp.float32)

    first = la * ROWS - RIM
    for row in range(0, ROWS + 2 * RIM, CHUNK):
        number = (first + row + lax.broadcasted_iota(jnp.int32, (CHUNK, LANES), 0)).astype(jnp.float32)
        metric[0, pl.ds(row, CHUNK), :] = cosines(number + 0.5)
        metric[1, pl.ds(row, CHUNK), :] = cosines(number + 1.0)

    for load in loads:
        load.wait()
    for row in range(0, ROWS, CHUNK):
        at = pl.ds(PAD + RIM + row, CHUNK)
        center = metric[0, pl.ds(RIM + row, CHUNK), :]
        own = pl.ds(row, CHUNK)
        lane = lane_of(CHUNK)
        values = []
        for c in range(2):
            sea_mask = in_i[0, c, own, :].astype(jnp.float32)
            layers = in_i[1, c, own, :].astype(jnp.float32)
            deep = sea_mask * ((layers + layers * (layers - 1.0) / 20.0) / 200.0)
            right = in_f[0, c, own, :] * sea_mask
            source = in_f[1, c, own, :] * center * sea_mask
            values.append((deep, right, source))
            for k in range(3):
                fields[k, c, at, :] = values[c][k]
        packed_west, packed_east = values[0][0], values[1][0]
        for k in range(1, 3):
            part = (lane >= RIM * k) & (lane < RIM * (k + 1))
            packed_west = jnp.where(part, pltpu.roll(values[0][k], RIM * k, 1), packed_west)
            part = (lane < LANES - RIM * k) & (lane >= LANES - RIM * (k + 1))
            packed_east = jnp.where(part, pltpu.roll(values[1][k], LANES - RIM * k, 1), packed_east)
        west_pack[own, :] = packed_west
        east_pack[own, :] = packed_east

    own3 = RIM >> 3
    lane = lane_of(own_rows)
    line_row = lax.broadcasted_iota(jnp.int32, (own_rows, LANES), 0)
    pick = (lane % 16) * 8
    low = (lane % 32) < 16

    def dense(west_tile, east_tile, last=0):
        return jnp.where(
            low, jnp.take_along_axis(west_tile, pick + last, axis=1), jnp.take_along_axis(east_tile, pick + last, axis=1)
        )

    def lane_sum(value):
        for shift in (1, 2, 4):
            value = pair_sum(value, shift, lane)
        return value

    def every8(k, c, row):
        return fields[k, c, pl.ds(PAD + RIM + row, own_rows, stride=8), :]

    sums = [[None, None] for _ in range(3)]
    for row in range(8):
        deep = [every8(0, c, row) for c in range(2)]
        east = east_of(deep, 1, lane)
        inverse = 1.0 / metric[0, pl.ds(RIM + row, own_rows, stride=8), :]
        for c in range(2):
            face, term = jnp.minimum(deep[c], east[c]) * inverse, every8(2, c, row)
            sums[0][c] = face if row == 0 else sums[0][c] + face
            sums[2][c] = term if row == 0 else sums[2][c] + term
    for c in range(2):
        above = pltpu.roll(every8(0, c, 0), own_rows - 1, 0)
        face = jnp.minimum(every8(0, c, 7), above) * metric[1, pl.ds(RIM + 7, own_rows, stride=8), :]
        sums[1][c] = lane_sum(face)
        sums[2][c] = lane_sum(sums[2][c])
    parts = [dense(*sums[0], last=7), dense(*sums[1]), dense(*sums[2])]
    face_slots[z] = jnp.where(lane < 32, parts[0], jnp.where(lane < 64, parts[1], parts[2]))

    greeted = 2 + (ring - 1) + len(hops) + 1
    both = inside[-1].astype(jnp.int32) + inside[1].astype(jnp.int32)
    pl.semaphore_wait(barrier, greeted + 3 * both)

    def rim_copy(dy, dx):
        source_row, target_row = {1: (ROWS - RIM, 0), -1: (0, RIM + ROWS), 0: (0, RIM)}[dy]
        count = ROWS if dy == 0 else RIM
        if dx == 0:
            source = fields.at[:, pl.ds(0, 2), pl.ds(PAD + RIM + source_row, count), :]
            target = fields.at[:, pl.ds(0, 2), pl.ds(PAD + target_row, count), :]
        else:
            source = (east_pack if dx > 0 else west_pack).at[pl.ds(source_row, count), :]
            target = (west_rim if dx > 0 else east_rim).at[pl.ds(target_row, count), :]
        k = rims.index((dy, dx))
        return pltpu.make_async_remote_copy(
            source, target, rim_send.at[k], rim_recv.at[k],
            device_id=device(*beside(dy, dx)), device_id_type=MESH,
        )

    def slot_copy(slots, which, step):
        return pltpu.make_async_remote_copy(
            slots.at[z], slots.at[z], slot_send.at[which], slot_recv.at[which],
            device_id=device(*ring_peer(step)), device_id_type=MESH,
        )

    def all_slots(slots, which):
        return pltpu.make_async_remote_copy(
            slots.at[pl.ds(0, ring - 1)], slots.at[pl.ds(0, ring - 1)], slot_send.at[which], slot_recv.at[which],
            device_id=device(*ring_peer(1)), device_id_type=MESH,
        )

    def plane_block(which, lat, line):
        rows = pl.ds(pl.multiple_of(PAD + lat * own_rows, 8), own_rows)
        if which == 0:
            return faces.at[:, pl.ds(line * per_line, per_line), rows, :]
        return rhs.at[pl.ds(line * (per_line + 1), per_line + 1), rows, :]

    def plane_copy(which, k, dx, dy):
        block = plane_block(which, la, y)
        return pltpu.make_async_remote_copy(
            block, block, plane_send.at[which, k], plane_recv.at[which, k],
            device_id=device(*plane_peer(dx, dy)), device_id_type=MESH,
        )

    def pass_copy(which, lat, line):
        block = plane_block(which, lat, line)
        return pltpu.make_async_remote_copy(
            block, block, pass_send.at[which], pass_recv.at[which],
            device_id=device(*partner), device_id_type=MESH,
        )

    def all_passed(which):
        half = pl.ds(PAD, lat_count * own_rows // CORES)
        block = faces.at[:, :, half, :] if which == 0 else rhs.at[:, half, :]
        return pltpu.make_async_remote_copy(
            block, block, pass_send.at[which], pass_recv.at[which],
            device_id=device(*partner), device_id_type=MESH,
        )

    def send_plane(which):
        for k, (dx, dy) in enumerate(hops):
            plane_copy(which, k, dx, dy).start()
        pass_copy(which, la, y).start()

    def sent(which):
        for k, (dx, dy) in enumerate(hops):
            plane_copy(which, k, dx, dy).wait_send()
        all_passed(which).wait_send()

    def take_plane(which):
        for k, (dx, dy) in reversed([*enumerate(hops)]):
            plane_copy(which, k, dx, dy).wait_recv()
            pass_copy(which, *(lax.rem(x - dx + planes_x, planes_x) * CORES + core, lax.rem(y - dy + planes_y, planes_y))).start()

    order = sorted(rims, key=lambda d: (d[1] == 0, d[0] == 0))
    for dy, dx in order:
        where_inside(dy, lambda dy=dy, dx=dx: rim_copy(dy, dx).start())
    for step in ring_steps:
        slot_copy(face_slots, 0, step).start()
    for dy, dx in order:
        where_inside(-dy, lambda dy=dy, dx=dx: rim_copy(dy, dx).wait_recv())

    for row in range(0, ROWS + 2 * RIM, CHUNK):
        wide_lane = lane_of(CHUNK)
        east, west = east_rim[pl.ds(row, CHUNK), :], west_rim[pl.ds(row, CHUNK), :]
        for k in range(3):
            moved_east = pltpu.roll(east, LANES - RIM * k, 1) if k else east
            moved_west = pltpu.roll(west, RIM * k, 1) if k else west
            fields[k, 2, pl.ds(PAD + row, CHUNK), :] = jnp.where(
                wide_lane < RIM, moved_east, jnp.where(wide_lane >= LANES - RIM, moved_west, 0.0)
            )

    top = levels[0]
    for row in top.chunks():
        n = top.chunk
        deep = [top.load(depth, c, row, n) for c in range(3)]
        east = east_of(deep, 1, lane_of(n))
        inverse = 1.0 / metric[0, pl.ds(row, n), :]
        northern = metric[1, pl.ds(row, n), :]
        for c in range(3):
            at = pl.ds(PAD + row, n)
            top.east[c, at, :] = jnp.minimum(deep[c], east[c]) * inverse
            top.north[c, at, :] = jnp.minimum(deep[c], top.load(depth, c, row + 1, n)) * northern
    for fine, coarse in zip(levels, levels[1:]):
        for row in coarse.chunks():
            for c in range(3):
                at = pl.ds(PAD + row, coarse.chunk)
                coarse.east[c, at, :], coarse.north[c, at, :], coarse.source[c, at, :] = fine.coarse_faces(c, row, coarse.chunk)

    levels[0].finish()
    levels[0].descend()
    for fine, coarse in zip(levels, levels[1:]):
        for row in coarse.chunks():
            for c in range(3):
                coarse.rhs[c, pl.ds(PAD + row, coarse.chunk), :] = fine.coarse_rhs(c, row, coarse.chunk)
        coarse.finish()
        coarse.descend()

    bottom_faces = [levels[2].coarse_faces(c, own3, own_rows) for c in range(2)]
    bottom_rhs = [levels[2].coarse_rhs(c, own3, own_rows) for c in range(2)]
    last = jnp.take_along_axis(bottom_faces[1][0], jnp.full_like(lane, LANES - 1), axis=1)
    last = jnp.where(lane % 8 == line_row, last, 0.0)
    for shift in (4, 2, 1):
        last = last + pltpu.roll(last, shift, 0)
    rhs_slots[z] = jnp.where(
        lane < 32, dense(*bottom_rhs), jnp.where(lane < 64, dense(bottom_faces[0][1], bottom_faces[1][1]), last)
    )
    for step in ring_steps:
        slot_copy(rhs_slots, 1, step).start()

    def gathered(slots, h, k):
        value = None
        for j in range(group):
            slot = slots[h * group + j]
            shift = (32 * (j - k)) % LANES
            moved = pltpu.roll(slot, shift, 1) if shift else slot
            value = moved if value is None else jnp.where(lane // 32 == j, moved, value)
        return value

    own_at = pl.ds(pl.multiple_of(PAD + la * own_rows, 8), own_rows)
    all_slots(face_slots, 0).wait_recv()
    for h in range(per_line):
        for k in range(3):
            faces[k, y * per_line + h, own_at, :] = gathered(face_slots, h, k)
    send_plane(0)
    all_slots(rhs_slots, 1).wait_recv()
    edge = None
    for j in range(ring):
        moved = pltpu.roll(rhs_slots[j], LANES // 2, 1) if 8 * j < LANES // 2 else rhs_slots[j]
        edge = moved if edge is None else jnp.where(lane // 8 == j, moved, edge)
    for h in range(per_line):
        rhs[y * (per_line + 1) + h, own_at, :] = gathered(rhs_slots, h, 0)
        north = gathered(rhs_slots, h, 1)
        edge = jnp.where(line_row == 7 - h, pltpu.roll(north, 8 - h, 0) if h else north, edge)
    rhs[y * (per_line + 1) + per_line, own_at, :] = edge
    send_plane(1)
    take_plane(0)
    take_plane(1)

    height = lat_count * own_rows
    everything = pl.ds(PAD, height)
    lane3 = lane_of(height)
    west_face, diagonal = bottom.at[1], bottom.at[2]
    rest_ref, image_ref, along_ref = bottom.at[0], bottom.at[3], bottom.at[4]
    all_passed(0).wait_recv()
    all_passed(1).wait_recv()

    def rhs_tile(t):
        return t // per_line * (per_line + 1) + t % per_line

    sent(0)
    lane_lat = lane_of(lat_count)
    for t in range(tiles):
        h, edge_tile = t % per_line, t // per_line * (per_line + 1) + per_line
        side = pl.ds(PAD + 7, lat_count, stride=8)
        faces[1, t, side, :] = rhs[edge_tile, pl.ds(PAD + 7 - h, lat_count, stride=8), :]
        east = rhs[edge_tile, pl.ds(PAD, lat_count, stride=8), :]
        for row in range(own_rows):
            at = pl.ds(PAD + row, lat_count, stride=8)
            moved = jnp.take_along_axis(east, 8 * (h * group + lane_lat // 32) + row, axis=1)
            faces[0, t, at, :] = jnp.where(lane_lat % 32 == 31, moved, faces[0, t, at, :])
    for t in range(tiles):
        east = faces[0, t, everything, :]
        before = faces[0, (t - 1) % tiles, everything, :]
        west = pltpu.roll(jnp.where(lane3 >= LANES - 1, before, east), 1, 1)
        west_face[t, everything, :] = west
        diagonal[t, everything, :] = (
            faces[2, t, everything, :] + east + west
            + faces[1, t, everything, :] + faces[1, t, pl.ds(PAD - 1, height), :]
        )

    def operate(ref, place):
        norm, product = None, None
        for t in range(tiles):
            value = ref[place(t), everything, :]
            east = pltpu.roll(jnp.where(lane3 < 1, ref[place((t + 1) % tiles), everything, :], value), LANES - 1, 1)
            west = pltpu.roll(jnp.where(lane3 >= LANES - 1, ref[place((t - 1) % tiles), everything, :], value), 1, 1)
            image = diagonal[t, everything, :] * value - (
                faces[0, t, everything, :] * east
                + west_face[t, everything, :] * west
                + faces[1, t, everything, :] * ref[place(t), pl.ds(PAD + 1, height), :]
                + faces[1, t, pl.ds(PAD - 1, height), :] * ref[place(t), pl.ds(PAD - 1, height), :]
            )
            image_ref[t, everything, :] = image
            square, mixed = value * value, value * image
            norm = square if norm is None else norm + square
            product = mixed if product is None else product + mixed
        return jnp.sum(norm, keepdims=True), jnp.sum(product, keepdims=True)

    own_tile = lo // group
    near_tiles = (lax.rem(own_tile - 1 + tiles, tiles), own_tile, lax.rem(own_tile + 1, tiles))
    near = pl.ds(pl.multiple_of(la * own_rows, 8), 2 * PAD + own_rows)
    solved = [None] * 3
    direction = [None] * 3
    norm, product = operate(rhs, rhs_tile)
    alpha = norm / product
    beta = None
    for iteration in range(BOTTOM_ITERS):
        current, tile_at = (rhs, rhs_tile) if iteration == 0 else (rest_ref, lambda t: t)
        for k in range(3):
            value = current[tile_at(near_tiles[k]), near, :]
            direction[k] = value if iteration == 0 else value + beta * direction[k]
            solved[k] = alpha * direction[k] if iteration == 0 else solved[k] + alpha * direction[k]
        if iteration == BOTTOM_ITERS - 1:
            break
        for t in range(tiles):
            along = image_ref[t, everything, :]
            if iteration:
                along = along + beta * along_ref[t, everything, :]
            along_ref[t, everything, :] = along
            rest_ref[t, everything, :] = current[tile_at(t), everything, :] - alpha * along
        norm_next, product = operate(rest_ref, lambda t: t)
        beta = norm_next / norm
        alpha = norm_next / (product - beta * norm_next / alpha)
        norm = norm_next

    quarter = (lo % group) * 32
    lane = lane_of(8)
    place = quarter + jnp.where(lane < LANES // 2, 32 + lane // 8, (lane - LANES) // 8)
    wrapped = place & (LANES - 1)
    for row in range(0, 2 * PAD + own_rows, 8):
        left, mine, right = (solved[k][row : row + 8] for k in range(3))
        piece[0, pl.ds(row, 8), :] = jnp.take_along_axis(mine, quarter + lane // 8, axis=1)
        piece[1, pl.ds(row, 8), :] = jnp.take_along_axis(mine, quarter + 16 + lane // 8, axis=1)
        piece[2, pl.ds(row, 8), :] = jnp.where(
            place < 0, jnp.take_along_axis(left, wrapped, axis=1),
            jnp.where(place >= LANES, jnp.take_along_axis(right, wrapped, axis=1), jnp.take_along_axis(mine, wrapped, axis=1)),
        )

    levels[2].rise(piece, PAD - own3, False)
    levels[1].rise(levels[2].va, PAD, False)
    levels[0].rise(levels[1].va, PAD, True)
    stores = []
    for c in range(2):
        stores.append(pltpu.make_async_copy(
            top.va.at[c, pl.ds(PAD + RIM, ROWS), :], solution_out.at[:, pl.ds(c * LANES, LANES)], out_sem))
        stores[-1].start()
    for row in range(RIM, RIM + ROWS, CHUNK):
        _, image = top.apply(top.va, row, CHUNK, cols=2)
        for c in range(2):
            top.tmp[c, pl.ds(PAD + row, CHUNK), :] = top.load(top.rhs, c, row, CHUNK) - image[c]
    for c in range(2):
        stores.append(pltpu.make_async_copy(
            top.tmp.at[c, pl.ds(PAD + RIM, ROWS), :], residual_out.at[:, pl.ds(c * LANES, LANES)], out_sem))
        stores[-1].start()

    for dy, dx in order:
        where_inside(dy, lambda dy=dy, dx=dx: rim_copy(dy, dx).wait_send())
    for which, slots in enumerate((face_slots, rhs_slots)):
        all_slots(slots, which).wait_send()
    sent(1)
    for store in stores:
        store.wait()


def put_out(solution_in, residual_in, solution_out, residual_out, sems):
    copies = [
        pltpu.make_async_copy(solution_in, solution_out, sems.at[0]),
        pltpu.make_async_copy(residual_in, residual_out, sems.at[1]),
    ]
    for copy in copies:
        copy.start()
    for copy in copies:
        copy.wait()


def solution(mesh, ring=RING):
    lat_count, lon_count = mesh.shape["lat"], mesh.shape["lon"]
    planes = (lat_count // CORES) * (lon_count // ring)
    tiles = lon_count * (COLS >> 3) // LANES
    height = lat_count * (ROWS >> 3) + 2 * PAD
    f32 = jnp.float32

    def padded(level):
        return pltpu.VMEM((3, ((ROWS + 2 * RIM) >> level) + 2 * PAD, LANES), f32)

    rows = ROWS + 2 * RIM
    scratch = [
        pltpu.VMEM((2, 2, ROWS, LANES), f32),
        pltpu.VMEM((2, 2, ROWS, LANES), jnp.int32),
        pltpu.VMEM((3, 3, rows + 2 * PAD, LANES), f32),
        *[padded(0)] * 7,
        *[padded(1)] * 10,
        *[padded(2)] * 10,
        pltpu.VMEM((ROWS, LANES), f32),
        pltpu.VMEM((ROWS, LANES), f32),
        pltpu.VMEM((rows, LANES), f32),
        pltpu.VMEM((rows, LANES), f32),
        pltpu.VMEM((2, rows, LANES), f32),
        pltpu.VMEM((ring, 8, LANES), f32),
        pltpu.VMEM((ring, 8, LANES), f32),
        pltpu.VMEM((3, tiles, height, LANES), f32),
        pltpu.VMEM((tiles + lon_count // ring, height, LANES), f32),
        pltpu.VMEM((5, tiles, height, LANES), f32),
        padded(0),
        pltpu.VMEM((3, 2 * PAD + (ROWS >> 3), LANES), f32),
        pltpu.SemaphoreType.DMA,
        pltpu.SemaphoreType.DMA,
        pltpu.SemaphoreType.DMA((8,)),
        pltpu.SemaphoreType.DMA((8,)),
        pltpu.SemaphoreType.DMA((2,)),
        pltpu.SemaphoreType.DMA((2,)),
        pltpu.SemaphoreType.DMA((2, planes)),
        pltpu.SemaphoreType.DMA((2, planes)),
        pltpu.SemaphoreType.DMA((2,)),
        pltpu.SemaphoreType.DMA((2,)),
    ]

    def step(forcing, surface_term, sea_cells, levels):
        out = jax.ShapeDtypeStruct(forcing.shape, f32)
        results = pl.pallas_call(
            functools.partial(body, (lat_count, lon_count, ring)),
            out_shape=(out, out),
            in_specs=[pl.BlockSpec(memory_space=pltpu.HBM)] * 4,
            out_specs=[pl.BlockSpec(memory_space=pl.ANY)] * 2,
            scratch_shapes=scratch,
            compiler_params=pltpu.CompilerParams(
                collective_id=0, has_side_effects=True, vmem_limit_bytes=48 << 20
            ),
        )(*(pltpu.with_memory_space_constraint(v, pltpu.HBM) for v in (forcing, surface_term, sea_cells, levels)))
        return pl.pallas_call(
            put_out,
            out_shape=(out, out),
            in_specs=[pl.BlockSpec(memory_space=pltpu.VMEM)] * 2,
            out_specs=[pl.BlockSpec(memory_space=pltpu.HBM)] * 2,
            scratch_shapes=[pltpu.SemaphoreType.DMA((2,))],
        )(*(pltpu.with_memory_space_constraint(v, pltpu.VMEM) for v in results))

    return jax.shard_map(
        step,
        mesh=mesh,
        in_specs=(P("lat", "lon"),) * 4,
        out_specs=(P("lat", "lon"),) * 2,
        check_vma=False,
    )
```

```python
import functools
import math

import jax
import jax.numpy as jnp
from jax import lax
from jax.experimental import pallas as pl
from jax.experimental.pallas import tpu as pltpu
from jax.sharding import PartitionSpec as P

MESH = pl.DeviceIdType.MESH
DAMPING = 0.8
ROW_STEP = 150.0 / 8640.0
BAND_SOUTH = -50.0
BAND_ROWS = 512
BOTTOM_ITERS = 6
CORES = 2
RING = 8

ROWS, COLS = 64, 256
RIM = 32
NEAR = 16
PAD = 8
LANES = 128
CHUNK = 32


def lane_of(rows):
    return lax.broadcasted_iota(jnp.int32, (rows, LANES), 1)


def east_of(cols, shift, lane):
    count = len(cols)
    return [
        pltpu.roll(jnp.where(lane < shift, cols[(c + 1) % count], cols[c]), LANES - shift, 1)
        for c in range(count)
    ]


def west_of(cols, shift, lane):
    count = len(cols)
    return [
        pltpu.roll(jnp.where(lane >= LANES - shift, cols[(c - 1) % count], cols[c]), shift, 1)
        for c in range(count)
    ]


def pair_sum(value, shift, lane):
    upper = (lane & shift) != 0
    return value + jnp.where(upper, pltpu.roll(value, shift, 1), pltpu.roll(value, LANES - shift, 1))


def upper_of(value, shift, lane):
    return jnp.where((lane & shift) != 0, value, pltpu.roll(value, LANES - shift, 1))


def cosines(row):
    middle = math.radians(BAND_SOUTH + ROW_STEP * (BAND_ROWS / 2))
    off = (row - BAND_ROWS / 2) * math.radians(ROW_STEP)
    sq = off * off
    cos_off = 1.0 - sq * (1.0 / 2 - sq * (1.0 / 24 - sq * (1.0 / 720)))
    sin_off = off * (1.0 - sq * (1.0 / 6 - sq * (1.0 / 120 - sq * (1.0 / 5040))))
    return math.cos(middle) * cos_off - math.sin(middle) * sin_off


class Level:
    def __init__(self, index, rim, refs):
        self.index = index
        self.shift = 1 << index
        self.rows = (ROWS + 2 * rim) >> index
        self.rim = rim >> index
        self.east, self.west, self.north, self.source, self.diag, self.scale, self.rhs, self.va, self.vb, self.tmp = refs
        self.chunk = next(n for n in (32, 24, 16, 8) if self.rows % n == 0)

    def chunks(self):
        return range(0, self.rows, self.chunk)

    def load(self, ref, col, row, count):
        return ref[col, pl.ds(PAD + row, count), :]

    def apply(self, ref, row, count, cols=3):
        lane = lane_of(count)
        value = [self.load(ref, c, row, count) for c in range(3)]
        east = east_of(value, self.shift, lane)
        west = west_of(value, self.shift, lane)
        out = []
        for c in range(cols):
            around = (
                self.load(self.east, c, row, count) * east[c]
                + self.load(self.west, c, row, count) * west[c]
                + self.load(self.north, c, row, count) * self.load(ref, c, row + 1, count)
                + self.load(self.north, c, row - 1, count) * self.load(ref, c, row - 1, count)
            )
            out.append(self.load(self.diag, c, row, count) * value[c] - around)
        return value, out

    def smooth(self, source_ref, target_ref):
        for row in self.chunks():
            value, image = self.apply(source_ref, row, self.chunk)
            for c in range(3):
                rest = self.load(self.rhs, c, row, self.chunk) - image[c]
                target_ref[c, pl.ds(PAD + row, self.chunk), :] = (
                    value[c] + self.load(self.scale, c, row, self.chunk) * rest
                )

    def finish(self):
        n = self.chunk
        lane = lane_of(n)
        for row in self.chunks():
            east = [self.load(self.east, c, row, n) for c in range(3)]
            west = west_of(east, self.shift, lane)
            for c in range(3):
                source = self.load(self.source, c, row, n)
                total = (
                    source + east[c] + west[c]
                    + self.load(self.north, c, row, n) + self.load(self.north, c, row - 1, n)
                )
                diag = jnp.where(source > 0.0, total, 1.0)
                self.west[c, pl.ds(PAD + row, n), :] = west[c]
                self.diag[c, pl.ds(PAD + row, n), :] = diag
                self.scale[c, pl.ds(PAD + row, n), :] = DAMPING / diag

    def pairs(self, ref, col, row, count):
        return (
            ref[col, pl.ds(PAD + 2 * row, count, stride=2), :],
            ref[col, pl.ds(PAD + 2 * row + 1, count, stride=2), :],
        )

    def coarse_faces(self, col, row, count):
        lane = lane_of(count)
        lower, upper = self.pairs(self.east, col, row, count)
        east = upper_of(lower + upper, self.shift, lane)
        _, upper = self.pairs(self.north, col, row, count)
        north = pair_sum(upper, self.shift, lane)
        lower, upper = self.pairs(self.source, col, row, count)
        return east, north, pair_sum(lower + upper, self.shift, lane)

    def coarse_rhs(self, col, row, count):
        lower, upper = self.pairs(self.tmp, col, row, count)
        return pair_sum(lower + upper, self.shift, lane_of(count))

    def descend(self):
        n = self.chunk
        for row in self.chunks():
            for c in range(3):
                self.vb[c, pl.ds(PAD + row, n), :] = self.load(self.scale, c, row, n) * self.load(self.rhs, c, row, n)
        self.smooth(self.vb, self.va)
        for row in self.chunks():
            _, image = self.apply(self.va, row, n)
            for c in range(3):
                self.tmp[c, pl.ds(PAD + row, n), :] = self.load(self.rhs, c, row, n) - image[c]

    def rise(self, coarse, offset, masked):
        half = self.rows // 2
        n = min(CHUNK, half)
        for row in range(0, half, n):
            for c in range(3):
                added = coarse[c, pl.ds(offset + row, n), :]
                for odd in range(2):
                    at = pl.ds(PAD + 2 * row + odd, n, stride=2)
                    own = jnp.where(self.source[c, at, :] > 0.0, added, 0.0) if masked else added
                    self.va[c, at, :] = self.va[c, at, :] + own
        self.smooth(self.va, self.vb)
        self.smooth(self.vb, self.va)


def body(
    shape, forcing, surface, sea, depth_levels, solution_out, residual_out,
    in_f, in_i, fields, *rest
):
    lat_count, lon_count, ring = shape
    level_refs = [rest[0:8], rest[8:18], rest[18:28]]
    near_fields, near_refs = rest[28], [rest[29:37], rest[37:47], rest[47:57]]
    (
        west_pack, east_pack, east_rim, west_rim, near_packs, near_rims, near_corners, metric,
        face_slots, rhs_slots, side_slots, faces, rhs, sides, bottom, piece,
        in_sem, out_sem, rim_send, rim_recv, slot_send, slot_recv,
        plane_send, bulk_recv, plane_recv, pass_send, pass_recv,
    ) = rest[57:]
    planes_y = lon_count // ring
    planes_x = lat_count // CORES
    tiles = lon_count * (COLS >> 3) // LANES
    per_line = tiles // planes_y
    la, lo = lax.axis_index("lat"), lax.axis_index("lon")
    x, core = la // CORES, la % CORES
    y, z = lo // ring, lo % ring
    own_rows = ROWS >> 3
    group = LANES // (COLS >> 3)

    def levels_of(rim, base, refs):
        first = (*refs[0][0:3], base.at[2], *refs[0][3:5], base.at[1], *refs[0][5:8])
        return [Level(0, rim, first), Level(1, rim, refs[1]), Level(2, rim, refs[2])]

    levels = levels_of(RIM, fields, level_refs)
    near_levels = levels_of(NEAR, near_fields, near_refs)
    top = levels[0]

    def device(lat, lon):
        return {"lat": lat, "lon": lon}

    loads = []
    for k, ref in enumerate((forcing, surface)):
        for c in range(2):
            loads.append(pltpu.make_async_copy(ref.at[:, pl.ds(c * LANES, LANES)], in_f.at[k, c], in_sem))
    for k, ref in enumerate((sea, depth_levels)):
        for c in range(2):
            loads.append(pltpu.make_async_copy(ref.at[:, pl.ds(c * LANES, LANES)], in_i.at[k, c], in_sem))
    for load in loads:
        load.start()

    rims = [(dy, dx) for dy in (-1, 0, 1) for dx in (-1, 0, 1) if (dy, dx) != (0, 0)]
    hops = sorted(
        ((dx, dy) for dx in range(planes_x) for dy in range(planes_y) if (dx, dy) != (0, 0)),
        key=lambda d: -min(d[0], planes_x - d[0]) - min(d[1], planes_y - d[1]),
    )
    ring_steps = sorted(range(1, ring), key=lambda d: -min(d, ring - d))
    barrier = pltpu.get_barrier_semaphore()

    def greet(lat, lon):
        pl.semaphore_signal(barrier, inc=1, device_id=device(lat, lon), device_id_type=MESH)

    def beside(dy, dx):
        return la + dy, lax.rem(lo + dx + lon_count, lon_count)

    def ring_peer(step):
        return la, y * ring + lax.rem(z + step, ring)

    def plane_peer(dx, dy):
        return lax.rem(x + dx, planes_x) * CORES + core, lax.rem(y + dy, planes_y) * ring + z

    partner = (x * CORES + (1 - core), lo)
    inside = {-1: la > 0, 0: None, 1: la < lat_count - 1}

    def where_inside(dy, act):
        if dy == 0:
            act()
        else:
            pl.when(inside[dy])(act)

    for dy, dx in rims:
        where_inside(dy, lambda dy=dy, dx=dx: greet(*beside(dy, dx)))
    for step in ring_steps:
        greet(*ring_peer(step))
    for dx, dy in hops:
        greet(*plane_peer(dx, dy))
    greet(*partner)

    def clear(ref, col, row, count):
        ref[col, pl.ds(row, count), :] = jnp.zeros((count, LANES), ref.dtype)

    for base, group_of in ((fields, levels), (near_fields, near_levels)):
        for c in range(3):
            for k in range(3):
                clear(base.at[k], c, 0, PAD)
                clear(base.at[k], c, PAD + group_of[0].rows, PAD)
            for level in group_of:
                for ref in (level.north, level.va, level.vb):
                    clear(ref, c, 0, PAD)
                    clear(ref, c, PAD + level.rows, PAD)
    for ref in (faces.at[1], rhs, bottom.at[0], bottom.at[6]):
        for t in range(tiles):
            clear(ref, t, 0, PAD)
            clear(ref, t, PAD + lat_count * own_rows, PAD)
    for dy, row, near_row in ((-1, 0, 0), (1, RIM + ROWS, NEAR + ROWS)):

        @pl.when(jnp.logical_not(inside[dy]))
        def _(dy=dy, row=row, near_row=near_row):
            for k in range(3):
                for c in range(2):
                    clear(fields.at[k], c, PAD + row, RIM)
                    clear(near_fields.at[k], c, PAD + near_row, NEAR)
            for side in range(2):
                clear(near_corners.at[side], (dy + 1) // 2, 0, NEAR)
            east_rim[pl.ds(row, RIM), :] = jnp.zeros((RIM, LANES), jnp.float32)
            west_rim[pl.ds(row, RIM), :] = jnp.zeros((RIM, LANES), jnp.float32)

    first = la * ROWS - RIM
    for row in range(0, ROWS + 2 * RIM, CHUNK):
        number = (first + row + lax.broadcasted_iota(jnp.int32, (CHUNK, LANES), 0)).astype(jnp.float32)
        metric[0, pl.ds(row, CHUNK), :] = cosines(number + 0.5)
        metric[1, pl.ds(row, CHUNK), :] = cosines(number + 1.0)

    for load in loads:
        load.wait()
    near_strips = [None, None]
    for row in range(0, ROWS, CHUNK):
        at = pl.ds(PAD + RIM + row, CHUNK)
        center = metric[0, pl.ds(RIM + row, CHUNK), :]
        own = pl.ds(row, CHUNK)
        lane = lane_of(CHUNK)
        values = []
        for c in range(2):
            sea_mask = in_i[0, c, own, :].astype(jnp.float32)
            layers = in_i[1, c, own, :].astype(jnp.float32)
            deep = sea_mask * ((layers + layers * (layers - 1.0) / 20.0) / 200.0)
            right = in_f[0, c, own, :] * sea_mask
            source = in_f[1, c, own, :] * center * sea_mask
            values.append((deep, right, source))
            for k in range(3):
                fields[k, c, at, :] = values[c][k]
                near_fields[k, c, pl.ds(PAD + NEAR + row, CHUNK), :] = values[c][k]
        packed_west, packed_east = values[0][0], values[1][0]
        for k in range(1, 3):
            part = (lane >= RIM * k) & (lane < RIM * (k + 1))
            packed_west = jnp.where(part, pltpu.roll(values[0][k], RIM * k, 1), packed_west)
            part = (lane < LANES - RIM * k) & (lane >= LANES - RIM * (k + 1))
            packed_east = jnp.where(part, pltpu.roll(values[1][k], LANES - RIM * k, 1), packed_east)
        west_pack[own, :] = packed_west
        east_pack[own, :] = packed_east
        for side in range(2):
            for k in range(3):
                place = row * 2 + NEAR * k
                moved = pltpu.roll(values[side][k], (place + NEAR * side) % LANES, 1)
                part = (lane >= place) & (lane < place + NEAR)
                near_strips[side] = moved if near_strips[side] is None else jnp.where(part, moved, near_strips[side])
    for side in range(2):
        near_packs[side] = near_strips[side]

    own3 = RIM >> 3
    lane = lane_of(own_rows)
    line_row = lax.broadcasted_iota(jnp.int32, (own_rows, LANES), 0)
    pick = (lane % 16) * 8
    low = (lane % 32) < 16

    def dense(west_tile, east_tile, last=0):
        return jnp.where(
            low, jnp.take_along_axis(west_tile, pick + last, axis=1), jnp.take_along_axis(east_tile, pick + last, axis=1)
        )

    def lane_sum(value):
        for shift in (1, 2, 4):
            value = pair_sum(value, shift, lane)
        return value

    def every8(k, c, row):
        return fields[k, c, pl.ds(PAD + RIM + row, own_rows, stride=8), :]

    sums = [[None, None] for _ in range(3)]
    for row in range(8):
        deep = [every8(0, c, row) for c in range(2)]
        east = east_of(deep, 1, lane)
        inverse = 1.0 / metric[0, pl.ds(RIM + row, own_rows, stride=8), :]
        for c in range(2):
            face, term = jnp.minimum(deep[c], east[c]) * inverse, every8(2, c, row)
            sums[0][c] = face if row == 0 else sums[0][c] + face
            sums[2][c] = term if row == 0 else sums[2][c] + term
    for c in range(2):
        above = pltpu.roll(every8(0, c, 0), own_rows - 1, 0)
        face = jnp.minimum(every8(0, c, 7), above) * metric[1, pl.ds(RIM + 7, own_rows, stride=8), :]
        sums[1][c] = lane_sum(face)
        sums[2][c] = lane_sum(sums[2][c])
    parts = [dense(*sums[0], last=7), dense(*sums[1]), dense(*sums[2])]
    face_slots[z] = jnp.where(lane < 32, parts[0], jnp.where(lane < 64, parts[1], parts[2]))

    greeted = 2 + (ring - 1) + len(hops) + 1
    both = inside[-1].astype(jnp.int32) + inside[1].astype(jnp.int32)
    pl.semaphore_wait(barrier, greeted + 3 * both)

    def to_beside(source, target, k, dy, dx):
        return pltpu.make_async_remote_copy(
            source, target, rim_send.at[k], rim_recv.at[k],
            device_id=device(*beside(dy, dx)), device_id_type=MESH,
        )

    def rim_copy(dy, dx):
        k = 1 if dx == 0 else 2
        if dx == 0:
            source_row, target_row = (ROWS - RIM, 0) if dy > 0 else (0, RIM + ROWS)
            return to_beside(
                fields.at[:, pl.ds(0, 2), pl.ds(PAD + RIM + source_row, RIM), :],
                fields.at[:, pl.ds(0, 2), pl.ds(PAD + target_row, RIM), :], k, dy, dx,
            )
        source_row, target_row = {1: (ROWS - RIM, 0), -1: (0, RIM + ROWS), 0: (0, RIM)}[dy]
        count = ROWS if dy == 0 else RIM
        return to_beside(
            (east_pack if dx > 0 else west_pack).at[pl.ds(source_row, count), :],
            (west_rim if dx > 0 else east_rim).at[pl.ds(target_row, count), :], k, dy, dx,
        )

    def near_copy(dy, dx):
        k = 0
        if dx == 0:
            source_row, target_row = (ROWS - NEAR, 0) if dy > 0 else (0, NEAR + ROWS)
            return to_beside(
                near_fields.at[:, pl.ds(0, 2), pl.ds(PAD + NEAR + source_row, NEAR), :],
                near_fields.at[:, pl.ds(0, 2), pl.ds(PAD + target_row, NEAR), :], k, dy, dx,
            )
        side = (dx + 1) // 2
        if dy == 0:
            return to_beside(near_packs.at[side], near_rims.at[side], k, dy, dx)
        source_row = NEAR if dy > 0 else 0
        return to_beside(
            near_packs.at[side, pl.ds(source_row, NEAR), :], near_corners.at[side, (1 - dy) // 2], k, dy, dx
        )

    def all_rims(k, wait):
        per_side = ((6 + 2) * NEAR, 6 * RIM, 2 * RIM)[k]
        level_with = (ROWS, 0, 2 * ROWS)[k]
        between = jnp.logical_and(inside[-1], inside[1])
        for when, count in ((between, 2 * per_side + level_with), (jnp.logical_not(between), per_side + level_with)):

            @pl.when(when)
            def _(count=count):
                as_much = fields.at[pl.ds(0, 2), pl.ds(0, 2), pl.ds(0, count // 4), :]
                wait(to_beside(as_much, as_much, k, 0, 1))

    def slot_copy(slots, which, step):
        return pltpu.make_async_remote_copy(
            slots.at[z], slots.at[z], slot_send.at[which], slot_recv.at[which],
            device_id=device(*ring_peer(step)), device_id_type=MESH,
        )

    def all_slots(slots, which):
        return pltpu.make_async_remote_copy(
            slots.at[pl.ds(0, ring - 1)], slots.at[pl.ds(0, ring - 1)], slot_send.at[which], slot_recv.at[which],
            device_id=device(*ring_peer(1)), device_id_type=MESH,
        )

    def plane_block(which, lat, line):
        rows = pl.ds(pl.multiple_of(PAD + lat * own_rows, 8), own_rows)
        if which == 0:
            return faces.at[:, pl.ds(line * per_line, per_line), rows, :]
        if which == 1:
            return rhs.at[pl.ds(line * per_line, per_line), rows, :]
        return sides.at[line, rows, :]

    def plane_copy(which, k, dx, dy):
        block = plane_block(which, la, y)
        return pltpu.make_async_remote_copy(
            block, block, plane_send.at[which], plane_recv.at[k] if which == 1 else bulk_recv.at[which // 2],
            device_id=device(*plane_peer(dx, dy)), device_id_type=MESH,
        )

    def all_planes(which):
        count = len(hops)
        lines, rows = (3, count // 3 * 8) if count % 3 == 0 else (1, count * 8)
        rows, of_tiles = pl.ds(0, rows), pl.ds(0, lines * per_line)
        block = (faces.at[:, of_tiles, rows, :], rhs.at[of_tiles, rows, :], sides.at[pl.ds(0, lines), rows, :])[which]
        return pltpu.make_async_remote_copy(
            block, block, plane_send.at[which], bulk_recv.at[which // 2],
            device_id=device(*partner), device_id_type=MESH,
        )

    def pass_copy(which, lat, line):
        block = plane_block(which, lat, line)
        return pltpu.make_async_remote_copy(
            block, block, pass_send.at[which], pass_recv.at[which],
            device_id=device(*partner), device_id_type=MESH,
        )

    def all_passed(which):
        half = pl.ds(PAD, lat_count * own_rows // CORES)
        block = (faces.at[:, :, half, :], rhs.at[:, half, :], sides.at[:, half, :])[which]
        return pltpu.make_async_remote_copy(
            block, block, pass_send.at[which], pass_recv.at[which],
            device_id=device(*partner), device_id_type=MESH,
        )

    def send_plane(which):
        for k, (dx, dy) in enumerate(hops):
            plane_copy(which, k, dx, dy).start()
        if which == 1:
            pass_copy(which, la, y).start()

    def sent(which):
        all_planes(which).wait_send()
        all_passed(which).wait_send()

    def take_bulk(which):
        all_planes(which).wait_recv()
        for line in range(planes_x):
            rows = pl.ds(pl.multiple_of(PAD + (line * CORES + core) * own_rows, 8), own_rows)
            block = faces.at[:, :, rows, :] if which == 0 else sides.at[:, rows, :]
            pltpu.make_async_remote_copy(
                block, block, pass_send.at[which], pass_recv.at[which],
                device_id=device(*partner), device_id_type=MESH,
            ).start()

    def take_plane(which):
        for k, (dx, dy) in reversed([*enumerate(hops)]):
            plane_copy(which, k, dx, dy).wait_recv()
            pass_copy(which, *(lax.rem(x - dx + planes_x, planes_x) * CORES + core, lax.rem(y - dy + planes_y, planes_y))).start()

    order = sorted(rims, key=lambda d: (d[1] == 0, d[0] == 0))
    for dy, dx in order:
        where_inside(dy, lambda dy=dy, dx=dx: near_copy(dy, dx).start())
    for step in ring_steps:
        slot_copy(face_slots, 0, step).start()
    for dy, dx in order:
        where_inside(dy, lambda dy=dy, dx=dx: rim_copy(dy, dx).start())

    def find_faces(some, base):
        first = some[0]
        n = first.chunk
        for row in first.chunks():
            deep = [first.load(base.at[0], c, row, n) for c in range(3)]
            east = east_of(deep, 1, lane_of(n))
            inverse = 1.0 / metric[0, pl.ds(RIM - first.rim + row, n), :]
            northern = metric[1, pl.ds(RIM - first.rim + row, n), :]
            for c in range(3):
                at = pl.ds(PAD + row, n)
                first.east[c, at, :] = jnp.minimum(deep[c], east[c]) * inverse
                first.north[c, at, :] = jnp.minimum(deep[c], first.load(base.at[0], c, row + 1, n)) * northern
        for fine, coarse in zip(some, some[1:]):
            for row in coarse.chunks():
                for c in range(3):
                    at = pl.ds(PAD + row, coarse.chunk)
                    coarse.east[c, at, :], coarse.north[c, at, :], coarse.source[c, at, :] = fine.coarse_faces(c, row, coarse.chunk)

    def descend(some):
        some[0].finish()
        some[0].descend()
        for fine, coarse in zip(some, some[1:]):
            for row in coarse.chunks():
                for c in range(3):
                    coarse.rhs[c, pl.ds(PAD + row, coarse.chunk), :] = fine.coarse_rhs(c, row, coarse.chunk)
            coarse.finish()
            coarse.descend()

    all_rims(0, lambda copy: copy.wait_recv())

    half_rows = ROWS // 2
    for row, count, quarter in (
        (0, NEAR, 1), (NEAR, half_rows, 0), (NEAR + half_rows, half_rows, 1), (NEAR + ROWS, NEAR, 0)
    ):
        wide_lane = lane_of(count)
        if count == NEAR:
            east, west = (near_corners[side, 0 if row == 0 else 1] for side in range(2))
        else:
            east, west = near_rims[0], near_rims[1]
        for k in range(3):
            place = quarter * (LANES // 2) + NEAR * k
            moved_east = pltpu.roll(east, LANES - place, 1) if place else east
            moved_west = pltpu.roll(west, LANES - NEAR - place, 1)
            near_fields[k, 2, pl.ds(PAD + row, count), :] = jnp.where(
                wide_lane < NEAR, moved_east, jnp.where(wide_lane >= LANES - NEAR, moved_west, 0.0)
            )

    find_faces(near_levels, near_fields)
    near3 = NEAR >> 3
    bottom_faces = [near_levels[2].coarse_faces(c, near3, own_rows) for c in range(2)]
    last = jnp.take_along_axis(bottom_faces[1][0], jnp.full_like(lane, LANES - 1), axis=1)
    last = jnp.where(lane % 8 == line_row, last, 0.0)
    for shift in (4, 2, 1):
        last = last + pltpu.roll(last, shift, 0)
    north = pltpu.roll(dense(bottom_faces[0][1], bottom_faces[1][1]), 1, 0)
    side_slots[z] = jnp.where(line_row == 0, north, last)[0:2]
    for step in ring_steps:
        slot_copy(side_slots, 2, step).start()
    descend(near_levels)

    bottom_rhs = [near_levels[2].coarse_rhs(c, near3, own_rows) for c in range(2)]
    packed = jnp.where(lane // 32 == line_row // 2, dense(*bottom_rhs), 0.0)
    for shift in (4, 2):
        packed = packed + pltpu.roll(packed, shift, 0)
    rhs_slots[z] = packed[0:2]
    for step in ring_steps:
        slot_copy(rhs_slots, 1, step).start()

    own_at = pl.ds(pl.multiple_of(PAD + la * own_rows, 8), own_rows)
    all_slots(face_slots, 0).wait_recv()
    for h in range(per_line):
        for k in range(3):
            value = None
            for j in range(group):
                slot = face_slots[h * group + j]
                shift = (32 * (j - k)) % LANES
                moved = pltpu.roll(slot, shift, 1) if shift else slot
                value = moved if value is None else jnp.where(lane // 32 == j, moved, value)
            faces[k, y * per_line + h, own_at, :] = value
    send_plane(0)

    def spread(ref, j, row):
        return jnp.broadcast_to(ref[j, pl.ds(row, 1), :], (own_rows, LANES))

    for k in (1, 2):
        all_rims(k, lambda copy: copy.wait_recv())
    for row in range(0, ROWS + 2 * RIM, CHUNK):
        wide_lane = lane_of(CHUNK)
        east, west = east_rim[pl.ds(row, CHUNK), :], west_rim[pl.ds(row, CHUNK), :]
        for k in range(3):
            moved_east = pltpu.roll(east, LANES - RIM * k, 1) if k else east
            moved_west = pltpu.roll(west, RIM * k, 1) if k else west
            fields[k, 2, pl.ds(PAD + row, CHUNK), :] = jnp.where(
                wide_lane < RIM, moved_east, jnp.where(wide_lane >= LANES - RIM, moved_west, 0.0)
            )
    find_faces(levels, fields)
    descend(levels)

    all_slots(side_slots, 2).wait_recv()
    side = None
    for j in range(ring):
        value = spread(side_slots, j, 1)
        side = value if side is None else jnp.where(lane // 8 == j, value, side)
    for h in range(per_line):
        for j in range(group):
            side = jnp.where((line_row == 7 - h) & (lane // 32 == j), spread(side_slots, h * group + j, 0), side)
    sides[y, own_at, :] = side
    send_plane(2)

    all_slots(rhs_slots, 1).wait_recv()
    unpick = 32 * (line_row // 2) + lane % 32
    for h in range(per_line):
        value = None
        for j in range(group):
            both_rows = jnp.where(line_row % 2 == 0, spread(rhs_slots, h * group + j, 0), spread(rhs_slots, h * group + j, 1))
            moved = jnp.take_along_axis(both_rows, unpick, axis=1)
            value = moved if value is None else jnp.where(lane // 32 == j, moved, value)
        rhs[y * per_line + h, own_at, :] = value
    send_plane(1)
    take_bulk(0)
    take_bulk(2)
    take_plane(1)

    height = lat_count * own_rows
    everything = pl.ds(PAD, height)
    lane3 = lane_of(height)
    west_face, diagonal = bottom.at[1], bottom.at[2]
    rest_ref, image_ref, along_ref = bottom.at[0], bottom.at[3], bottom.at[4]
    all_passed(0).wait_recv()
    all_passed(2).wait_recv()
    east_face, north_face = bottom.at[5], bottom.at[6]
    lane_lat = lane_of(lat_count)
    for t in range(tiles):
        h, line = t % per_line, t // per_line
        north_face[t, everything, :] = faces[1, t, everything, :]
        north_face[t, pl.ds(PAD + 7, lat_count, stride=8), :] = sides[line, pl.ds(PAD + 7 - h, lat_count, stride=8), :]
        east = sides[line, pl.ds(PAD, lat_count, stride=8), :]
        for row in range(own_rows):
            at = pl.ds(PAD + row, lat_count, stride=8)
            moved = jnp.take_along_axis(east, 8 * (h * group + lane_lat // 32) + row, axis=1)
            east_face[t, at, :] = jnp.where(lane_lat % 32 == 31, moved, faces[0, t, at, :])
    for t in range(tiles):
        east = east_face[t, everything, :]
        before = east_face[(t - 1) % tiles, everything, :]
        west = pltpu.roll(jnp.where(lane3 >= LANES - 1, before, east), 1, 1)
        west_face[t, everything, :] = west
        diagonal[t, everything, :] = (
            faces[2, t, everything, :] + east + west
            + north_face[t, everything, :] + north_face[t, pl.ds(PAD - 1, height), :]
        )
    all_passed(1).wait_recv()

    def operate(ref):
        norm, product = None, None
        for t in range(tiles):
            value = ref[t, everything, :]
            east = pltpu.roll(jnp.where(lane3 < 1, ref[(t + 1) % tiles, everything, :], value), LANES - 1, 1)
            west = pltpu.roll(jnp.where(lane3 >= LANES - 1, ref[(t - 1) % tiles, everything, :], value), 1, 1)
            image = diagonal[t, everything, :] * value - (
                east_face[t, everything, :] * east
                + west_face[t, everything, :] * west
                + north_face[t, everything, :] * ref[t, pl.ds(PAD + 1, height), :]
                + north_face[t, pl.ds(PAD - 1, height), :] * ref[t, pl.ds(PAD - 1, height), :]
            )
            image_ref[t, everything, :] = image
            square, mixed = value * value, value * image
            norm = square if norm is None else norm + square
            product = mixed if product is None else product + mixed
        return jnp.sum(norm, keepdims=True), jnp.sum(product, keepdims=True)

    own_tile = lo // group
    near_tiles = (lax.rem(own_tile - 1 + tiles, tiles), own_tile, lax.rem(own_tile + 1, tiles))
    near = pl.ds(pl.multiple_of(la * own_rows, 8), 2 * PAD + own_rows)
    solved = [None] * 3
    direction = [None] * 3
    norm, product = operate(rhs)
    alpha = norm / product
    beta = None
    for iteration in range(BOTTOM_ITERS):
        current = rhs if iteration == 0 else rest_ref
        for k in range(3):
            value = current[near_tiles[k], near, :]
            direction[k] = value if iteration == 0 else value + beta * direction[k]
            solved[k] = alpha * direction[k] if iteration == 0 else solved[k] + alpha * direction[k]
        if iteration == BOTTOM_ITERS - 1:
            break
        for t in range(tiles):
            along = image_ref[t, everything, :]
            if iteration:
                along = along + beta * along_ref[t, everything, :]
            along_ref[t, everything, :] = along
            rest_ref[t, everything, :] = current[t, everything, :] - alpha * along
        norm_next, product = operate(rest_ref)
        beta = norm_next / norm
        alpha = norm_next / (product - beta * norm_next / alpha)
        norm = norm_next

    quarter = (lo % group) * 32
    lane = lane_of(8)
    place = quarter + jnp.where(lane < LANES // 2, 32 + lane // 8, (lane - LANES) // 8)
    wrapped = place & (LANES - 1)
    for row in range(0, 2 * PAD + own_rows, 8):
        left, mine, right = (solved[k][row : row + 8] for k in range(3))
        piece[0, pl.ds(row, 8), :] = jnp.take_along_axis(mine, quarter + lane // 8, axis=1)
        piece[1, pl.ds(row, 8), :] = jnp.take_along_axis(mine, quarter + 16 + lane // 8, axis=1)
        piece[2, pl.ds(row, 8), :] = jnp.where(
            place < 0, jnp.take_along_axis(left, wrapped, axis=1),
            jnp.where(place >= LANES, jnp.take_along_axis(right, wrapped, axis=1), jnp.take_along_axis(mine, wrapped, axis=1)),
        )

    levels[2].rise(piece, PAD - own3, False)
    levels[1].rise(levels[2].va, PAD, False)
    levels[0].rise(levels[1].va, PAD, True)
    stores = []
    for c in range(2):
        stores.append(pltpu.make_async_copy(
            top.va.at[c, pl.ds(PAD + RIM, ROWS), :], solution_out.at[:, pl.ds(c * LANES, LANES)], out_sem))
        stores[-1].start()
    for row in range(RIM, RIM + ROWS, CHUNK):
        _, image = top.apply(top.va, row, CHUNK, cols=2)
        for c in range(2):
            top.tmp[c, pl.ds(PAD + row, CHUNK), :] = top.load(top.rhs, c, row, CHUNK) - image[c]
    for c in range(2):
        stores.append(pltpu.make_async_copy(
            top.tmp.at[c, pl.ds(PAD + RIM, ROWS), :], residual_out.at[:, pl.ds(c * LANES, LANES)], out_sem))
        stores[-1].start()

    for k in range(3):
        all_rims(k, lambda copy: copy.wait_send())
    for which, slots in enumerate((face_slots, rhs_slots, side_slots)):
        all_slots(slots, which).wait_send()
        sent(which)
    for store in stores:
        store.wait()


def put_out(solution_in, residual_in, solution_out, residual_out, sems):
    copies = [
        pltpu.make_async_copy(solution_in, solution_out, sems.at[0]),
        pltpu.make_async_copy(residual_in, residual_out, sems.at[1]),
    ]
    for copy in copies:
        copy.start()
    for copy in copies:
        copy.wait()


def solution(mesh, ring=RING):
    lat_count, lon_count = mesh.shape["lat"], mesh.shape["lon"]
    planes = (lat_count // CORES) * (lon_count // ring)
    tiles = lon_count * (COLS >> 3) // LANES
    height = lat_count * (ROWS >> 3) + 2 * PAD
    f32 = jnp.float32

    def padded(level, rim=RIM):
        return pltpu.VMEM((3, ((ROWS + 2 * rim) >> level) + 2 * PAD, LANES), f32)

    rows = ROWS + 2 * RIM
    scratch = [
        pltpu.VMEM((2, 2, ROWS, LANES), f32),
        pltpu.VMEM((2, 2, ROWS, LANES), jnp.int32),
        pltpu.VMEM((3, 3, rows + 2 * PAD, LANES), f32),
        *[padded(0)] * 8,
        *[padded(1)] * 10,
        *[padded(2)] * 10,
        pltpu.VMEM((3, 3, ROWS + 2 * NEAR + 2 * PAD, LANES), f32),
        *[padded(0, NEAR)] * 8,
        *[padded(1, NEAR)] * 10,
        *[padded(2, NEAR)] * 10,
        pltpu.VMEM((ROWS, LANES), f32),
        pltpu.VMEM((ROWS, LANES), f32),
        pltpu.VMEM((rows, LANES), f32),
        pltpu.VMEM((rows, LANES), f32),
        pltpu.VMEM((2, ROWS // 2, LANES), f32),
        pltpu.VMEM((2, ROWS // 2, LANES), f32),
        pltpu.VMEM((2, 2, NEAR, LANES), f32),
        pltpu.VMEM((2, rows, LANES), f32),
        pltpu.VMEM((ring, 8, LANES), f32),
        pltpu.VMEM((ring, 2, LANES), f32),
        pltpu.VMEM((ring, 2, LANES), f32),
        pltpu.VMEM((3, tiles, height, LANES), f32),
        pltpu.VMEM((tiles, height, LANES), f32),
        pltpu.VMEM((lon_count // ring, height, LANES), f32),
        pltpu.VMEM((7, tiles, height, LANES), f32),
        pltpu.VMEM((3, 2 * PAD + (ROWS >> 3), LANES), f32),
        pltpu.SemaphoreType.DMA,
        pltpu.SemaphoreType.DMA,
        pltpu.SemaphoreType.DMA((3,)),
        pltpu.SemaphoreType.DMA((3,)),
        pltpu.SemaphoreType.DMA((3,)),
        pltpu.SemaphoreType.DMA((3,)),
        pltpu.SemaphoreType.DMA((3,)),
        pltpu.SemaphoreType.DMA((2,)),
        pltpu.SemaphoreType.DMA((planes - 1,)),
        pltpu.SemaphoreType.DMA((3,)),
        pltpu.SemaphoreType.DMA((3,)),
    ]

    def step(forcing, surface_term, sea_cells, levels):
        out = jax.ShapeDtypeStruct(forcing.shape, f32)
        results = pl.pallas_call(
            functools.partial(body, (lat_count, lon_count, ring)),
            out_shape=(out, out),
            in_specs=[pl.BlockSpec(memory_space=pltpu.HBM)] * 4,
            out_specs=[pl.BlockSpec(memory_space=pl.ANY)] * 2,
            scratch_shapes=scratch,
            compiler_params=pltpu.CompilerParams(
                collective_id=0, has_side_effects=True, vmem_limit_bytes=48 << 20
            ),
        )(*(pltpu.with_memory_space_constraint(v, pltpu.HBM) for v in (forcing, surface_term, sea_cells, levels)))
        return pl.pallas_call(
            put_out,
            out_shape=(out, out),
            in_specs=[pl.BlockSpec(memory_space=pltpu.VMEM)] * 2,
            out_specs=[pl.BlockSpec(memory_space=pltpu.HBM)] * 2,
            scratch_shapes=[pltpu.SemaphoreType.DMA((2,))],
        )(*(pltpu.with_memory_space_constraint(v, pltpu.VMEM) for v in results))

    return jax.shard_map(
        step,
        mesh=mesh,
        in_specs=(P("lat", "lon"),) * 4,
        out_specs=(P("lat", "lon"),) * 2,
        check_vma=False,
    )
```

```python
import functools
import math

import jax
import jax.numpy as jnp
from jax import lax
from jax.experimental import pallas as pl
from jax.experimental.pallas import tpu as pltpu
from jax.sharding import PartitionSpec as P

MESH = pl.DeviceIdType.MESH
DAMPING = 0.8
ROW_STEP = 150.0 / 8640.0
BAND_SOUTH = -50.0
BAND_ROWS = 512
BOTTOM_ITERS = 6
CORES = 2
RING = 8

ROWS, COLS = 64, 256
RIM = 32
NEAR = 16
PAD = 8
LANES = 128
CHUNK = 32


def lane_of(rows):
    return lax.broadcasted_iota(jnp.int32, (rows, LANES), 1)


def east_of(cols, shift, lane):
    count = len(cols)
    return [
        pltpu.roll(jnp.where(lane < shift, cols[(c + 1) % count], cols[c]), LANES - shift, 1)
        for c in range(count)
    ]


def west_of(cols, shift, lane):
    count = len(cols)
    return [
        pltpu.roll(jnp.where(lane >= LANES - shift, cols[(c - 1) % count], cols[c]), shift, 1)
        for c in range(count)
    ]


def pair_sum(value, shift, lane):
    upper = (lane & shift) != 0
    return value + jnp.where(upper, pltpu.roll(value, shift, 1), pltpu.roll(value, LANES - shift, 1))


def upper_of(value, shift, lane):
    return jnp.where((lane & shift) != 0, value, pltpu.roll(value, LANES - shift, 1))


def cosines(row):
    middle = math.radians(BAND_SOUTH + ROW_STEP * (BAND_ROWS / 2))
    off = (row - BAND_ROWS / 2) * math.radians(ROW_STEP)
    sq = off * off
    cos_off = 1.0 - sq * (1.0 / 2 - sq * (1.0 / 24 - sq * (1.0 / 720)))
    sin_off = off * (1.0 - sq * (1.0 / 6 - sq * (1.0 / 120 - sq * (1.0 / 5040))))
    return math.cos(middle) * cos_off - math.sin(middle) * sin_off


class Level:
    def __init__(self, index, rim, refs):
        self.index = index
        self.shift = 1 << index
        self.rows = (ROWS + 2 * rim) >> index
        self.rim = rim >> index
        self.east, self.west, self.north, self.source, self.diag, self.scale, self.rhs, self.va, self.vb, self.tmp = refs
        self.chunk = next(n for n in (32, 24, 16, 8) if self.rows % n == 0)

    def chunks(self):
        return range(0, self.rows, self.chunk)

    def load(self, ref, col, row, count):
        return ref[col, pl.ds(PAD + row, count), :]

    def apply(self, ref, row, count, cols=3):
        lane = lane_of(count)
        value = [self.load(ref, c, row, count) for c in range(3)]
        east = east_of(value, self.shift, lane)
        west = west_of(value, self.shift, lane)
        out = []
        for c in range(cols):
            around = (
                self.load(self.east, c, row, count) * east[c]
                + self.load(self.west, c, row, count) * west[c]
                + self.load(self.north, c, row, count) * self.load(ref, c, row + 1, count)
                + self.load(self.north, c, row - 1, count) * self.load(ref, c, row - 1, count)
            )
            out.append(self.load(self.diag, c, row, count) * value[c] - around)
        return value, out

    def smooth(self, source_ref, target_ref, chunks=None):
        for row, n in chunks or [(row, self.chunk) for row in self.chunks()]:
            value, image = self.apply(source_ref, row, n)
            for c in range(3):
                rest = self.load(self.rhs, c, row, n) - image[c]
                target_ref[c, pl.ds(PAD + row, n), :] = value[c] + self.load(self.scale, c, row, n) * rest

    def finish(self):
        n = self.chunk
        lane = lane_of(n)
        for row in self.chunks():
            east = [self.load(self.east, c, row, n) for c in range(3)]
            west = west_of(east, self.shift, lane)
            for c in range(3):
                source = self.load(self.source, c, row, n)
                total = (
                    source + east[c] + west[c]
                    + self.load(self.north, c, row, n) + self.load(self.north, c, row - 1, n)
                )
                diag = jnp.where(source > 0.0, total, 1.0)
                self.west[c, pl.ds(PAD + row, n), :] = west[c]
                self.diag[c, pl.ds(PAD + row, n), :] = diag
                self.scale[c, pl.ds(PAD + row, n), :] = DAMPING / diag

    def pairs(self, ref, col, row, count):
        return (
            ref[col, pl.ds(PAD + 2 * row, count, stride=2), :],
            ref[col, pl.ds(PAD + 2 * row + 1, count, stride=2), :],
        )

    def coarse_faces(self, col, row, count):
        lane = lane_of(count)
        lower, upper = self.pairs(self.east, col, row, count)
        east = upper_of(lower + upper, self.shift, lane)
        _, upper = self.pairs(self.north, col, row, count)
        north = pair_sum(upper, self.shift, lane)
        lower, upper = self.pairs(self.source, col, row, count)
        return east, north, pair_sum(lower + upper, self.shift, lane)

    def coarse_rhs(self, col, row, count):
        lower, upper = self.pairs(self.tmp, col, row, count)
        return pair_sum(lower + upper, self.shift, lane_of(count))

    def descend(self):
        n = self.chunk
        for row in self.chunks():
            for c in range(3):
                self.vb[c, pl.ds(PAD + row, n), :] = self.load(self.scale, c, row, n) * self.load(self.rhs, c, row, n)
        self.smooth(self.vb, self.va)
        for row in self.chunks():
            _, image = self.apply(self.va, row, n)
            for c in range(3):
                self.tmp[c, pl.ds(PAD + row, n), :] = self.load(self.rhs, c, row, n) - image[c]

    def rise(self, coarse, offset, masked):
        begin = (self.rim - 4) // 8 * 8
        count = self.rows - 2 * begin
        n = next(n for n in (32, 24, 16) if count % n == 0)
        for row in range(begin // 2, (begin + count) // 2, n // 2):
            for c in range(3):
                added = coarse[c, pl.ds(offset + row, n // 2), :]
                for odd in range(2):
                    at = pl.ds(PAD + 2 * row + odd, n // 2, stride=2)
                    own = jnp.where(self.source[c, at, :] > 0.0, added, 0.0) if masked else added
                    self.va[c, at, :] = self.va[c, at, :] + own
        chunks = [(row, n) for row in range(begin, begin + count, n)]
        self.smooth(self.va, self.vb, chunks)
        self.smooth(self.vb, self.va, chunks)


def body(
    shape, forcing, surface, sea, depth_levels, solution_out, residual_out,
    in_f, in_i, fields, *rest
):
    lat_count, lon_count, ring = shape
    level_refs = [rest[0:8], rest[8:18], rest[18:28]]
    near_fields, near_refs = rest[28], [rest[29:37], rest[37:47], rest[47:57]]
    (
        west_pack, east_pack, east_rim, west_rim, near_packs, near_rims, near_corners, metric,
        face_slots, rhs_slots, side_slots, faces, rhs, sides, bottom, piece,
        in_sem, out_sem, rim_send, rim_recv, slot_send, slot_recv,
        plane_send, plane_recv, pass_send, pass_recv,
    ) = rest[57:]
    planes_y = lon_count // ring
    planes_x = lat_count // CORES
    tiles = lon_count * (COLS >> 3) // LANES
    per_line = tiles // planes_y
    la, lo = lax.axis_index("lat"), lax.axis_index("lon")
    x, core = la // CORES, la % CORES
    y, z = lo // ring, lo % ring
    own_rows = ROWS >> 3
    group = LANES // (COLS >> 3)

    def levels_of(rim, base, refs):
        first = (*refs[0][0:3], base.at[2], *refs[0][3:5], base.at[1], *refs[0][5:8])
        return [Level(0, rim, first), Level(1, rim, refs[1]), Level(2, rim, refs[2])]

    levels = levels_of(RIM, fields, level_refs)
    near_levels = levels_of(NEAR, near_fields, near_refs)
    top = levels[0]

    def device(lat, lon):
        return {"lat": lat, "lon": lon}

    loads = []
    for k, ref in enumerate((forcing, surface)):
        for c in range(2):
            loads.append(pltpu.make_async_copy(ref.at[:, pl.ds(c * LANES, LANES)], in_f.at[k, c], in_sem))
    for k, ref in enumerate((sea, depth_levels)):
        for c in range(2):
            loads.append(pltpu.make_async_copy(ref.at[:, pl.ds(c * LANES, LANES)], in_i.at[k, c], in_sem))
    for load in loads:
        load.start()

    rims = [(dy, dx) for dy in (-1, 0, 1) for dx in (-1, 0, 1) if (dy, dx) != (0, 0)]
    hops = sorted(
        ((dx, dy) for dx in range(planes_x) for dy in range(planes_y) if (dx, dy) != (0, 0)),
        key=lambda d: -min(d[0], planes_x - d[0]) - min(d[1], planes_y - d[1]),
    )
    ring_steps = sorted(range(1, ring), key=lambda d: -min(d, ring - d))
    barrier = pltpu.get_barrier_semaphore()

    def greet(lat, lon):
        pl.semaphore_signal(barrier, inc=1, device_id=device(lat, lon), device_id_type=MESH)

    def beside(dy, dx):
        return la + dy, lax.rem(lo + dx + lon_count, lon_count)

    def ring_peer(step):
        return la, y * ring + lax.rem(z + step, ring)

    def plane_peer(dx, dy, other=0):
        return lax.rem(x + dx, planes_x) * CORES + (1 - core if other else core), lax.rem(y + dy, planes_y) * ring + z

    partner = (x * CORES + (1 - core), lo)
    inside = {-1: la > 0, 0: None, 1: la < lat_count - 1}

    def where_inside(dy, act):
        if dy == 0:
            act()
        else:
            pl.when(inside[dy])(act)

    for dy, dx in rims:
        where_inside(dy, lambda dy=dy, dx=dx: greet(*beside(dy, dx)))
    for step in ring_steps:
        greet(*ring_peer(step))
    for dx, dy in hops:
        for other in range(CORES):
            greet(*plane_peer(dx, dy, other))
    greet(*partner)

    def clear(ref, col, row, count):
        ref[col, pl.ds(row, count), :] = jnp.zeros((count, LANES), ref.dtype)

    for base, group_of in ((fields, levels), (near_fields, near_levels)):
        for c in range(3):
            for k in range(3):
                clear(base.at[k], c, 0, PAD)
                clear(base.at[k], c, PAD + group_of[0].rows, PAD)
            for level in group_of:
                for ref in (level.north, level.va, level.vb):
                    clear(ref, c, 0, PAD)
                    clear(ref, c, PAD + level.rows, PAD)
    for ref in (faces.at[1], rhs, bottom.at[0], bottom.at[6]):
        for t in range(tiles):
            clear(ref, t, 0, PAD)
            clear(ref, t, PAD + lat_count * own_rows, PAD)
    for dy, row, near_row in ((-1, 0, 0), (1, RIM + ROWS, NEAR + ROWS)):

        @pl.when(jnp.logical_not(inside[dy]))
        def _(dy=dy, row=row, near_row=near_row):
            for k in range(3):
                for c in range(2):
                    clear(fields.at[k], c, PAD + row, RIM)
                    clear(near_fields.at[k], c, PAD + near_row, NEAR)
            for side in range(2):
                clear(near_corners.at[side], (dy + 1) // 2, 0, NEAR)
            east_rim[pl.ds(row, RIM), :] = jnp.zeros((RIM, LANES), jnp.float32)
            west_rim[pl.ds(row, RIM), :] = jnp.zeros((RIM, LANES), jnp.float32)

    first = la * ROWS - RIM
    for row in range(0, ROWS + 2 * RIM, CHUNK):
        number = (first + row + lax.broadcasted_iota(jnp.int32, (CHUNK, LANES), 0)).astype(jnp.float32)
        metric[0, pl.ds(row, CHUNK), :] = cosines(number + 0.5)
        metric[2, pl.ds(row, CHUNK), :] = 1.0 / metric[0, pl.ds(row, CHUNK), :]
        metric[1, pl.ds(row, CHUNK), :] = cosines(number + 1.0)

    for load in loads:
        load.wait()
    near_strips = [None, None]
    for row in range(0, ROWS, CHUNK):
        at = pl.ds(PAD + RIM + row, CHUNK)
        center = metric[0, pl.ds(RIM + row, CHUNK), :]
        own = pl.ds(row, CHUNK)
        lane = lane_of(CHUNK)
        values = []
        for c in range(2):
            sea_mask = in_i[0, c, own, :].astype(jnp.float32)
            layers = in_i[1, c, own, :].astype(jnp.float32)
            deep = sea_mask * ((layers + layers * (layers - 1.0) / 20.0) / 200.0)
            right = in_f[0, c, own, :] * sea_mask
            source = in_f[1, c, own, :] * center * sea_mask
            values.append((deep, right, source))
            for k in range(3):
                fields[k, c, at, :] = values[c][k]
                near_fields[k, c, pl.ds(PAD + NEAR + row, CHUNK), :] = values[c][k]
        packed_west, packed_east = values[0][0], values[1][0]
        for k in range(1, 3):
            part = (lane >= RIM * k) & (lane < RIM * (k + 1))
            packed_west = jnp.where(part, pltpu.roll(values[0][k], RIM * k, 1), packed_west)
            part = (lane < LANES - RIM * k) & (lane >= LANES - RIM * (k + 1))
            packed_east = jnp.where(part, pltpu.roll(values[1][k], LANES - RIM * k, 1), packed_east)
        west_pack[own, :] = packed_west
        east_pack[own, :] = packed_east
        for side in range(2):
            for k in range(3):
                place = row * 2 + NEAR * k
                moved = pltpu.roll(values[side][k], (place + NEAR * side) % LANES, 1)
                part = (lane >= place) & (lane < place + NEAR)
                near_strips[side] = moved if near_strips[side] is None else jnp.where(part, moved, near_strips[side])
    for side in range(2):
        near_packs[side] = near_strips[side]

    own3 = RIM >> 3
    lane = lane_of(own_rows)
    line_row = lax.broadcasted_iota(jnp.int32, (own_rows, LANES), 0)
    pick = (lane % 16) * 8
    low = (lane % 32) < 16

    def dense(west_tile, east_tile, last=0):
        return jnp.where(
            low, jnp.take_along_axis(west_tile, pick + last, axis=1), jnp.take_along_axis(east_tile, pick + last, axis=1)
        )

    def lane_sum(value):
        for shift in (1, 2, 4):
            value = pair_sum(value, shift, lane)
        return value

    def every8(k, c, row):
        return fields[k, c, pl.ds(PAD + RIM + row, own_rows, stride=8), :]

    sums = [[None, None] for _ in range(3)]
    for row in range(8):
        deep = [every8(0, c, row) for c in range(2)]
        east = east_of(deep, 1, lane)
        inverse = metric[2, pl.ds(RIM + row, own_rows, stride=8), :]
        for c in range(2):
            face, term = jnp.minimum(deep[c], east[c]) * inverse, every8(2, c, row)
            sums[0][c] = face if row == 0 else sums[0][c] + face
            sums[2][c] = term if row == 0 else sums[2][c] + term
    for c in range(2):
        above = pltpu.roll(every8(0, c, 0), own_rows - 1, 0)
        face = jnp.minimum(every8(0, c, 7), above) * metric[1, pl.ds(RIM + 7, own_rows, stride=8), :]
        sums[1][c] = lane_sum(face)
        sums[2][c] = lane_sum(sums[2][c])
    parts = [dense(*sums[0], last=7), dense(*sums[1]), dense(*sums[2])]
    face_slots[z] = jnp.where(lane < 32, parts[0], jnp.where(lane < 64, parts[1], parts[2]))

    greeted = 2 + (ring - 1) + CORES * len(hops) + 1
    both = inside[-1].astype(jnp.int32) + inside[1].astype(jnp.int32)
    pl.semaphore_wait(barrier, greeted + 3 * both)

    def to_beside(source, target, k, dy, dx):
        return pltpu.make_async_remote_copy(
            source, target, rim_send.at[k], rim_recv.at[k],
            device_id=device(*beside(dy, dx)), device_id_type=MESH,
        )

    def rim_copy(dy, dx):
        k = 1 if dx == 0 else 2
        if dx == 0:
            source_row, target_row = (ROWS - RIM, 0) if dy > 0 else (0, RIM + ROWS)
            return to_beside(
                fields.at[:, pl.ds(0, 2), pl.ds(PAD + RIM + source_row, RIM), :],
                fields.at[:, pl.ds(0, 2), pl.ds(PAD + target_row, RIM), :], k, dy, dx,
            )
        source_row, target_row = {1: (ROWS - RIM, 0), -1: (0, RIM + ROWS), 0: (0, RIM)}[dy]
        count = ROWS if dy == 0 else RIM
        return to_beside(
            (east_pack if dx > 0 else west_pack).at[pl.ds(source_row, count), :],
            (west_rim if dx > 0 else east_rim).at[pl.ds(target_row, count), :], k, dy, dx,
        )

    def near_copy(dy, dx):
        k = 0
        if dx == 0:
            source_row, target_row = (ROWS - NEAR, 0) if dy > 0 else (0, NEAR + ROWS)
            return to_beside(
                near_fields.at[:, pl.ds(0, 2), pl.ds(PAD + NEAR + source_row, NEAR), :],
                near_fields.at[:, pl.ds(0, 2), pl.ds(PAD + target_row, NEAR), :], k, dy, dx,
            )
        side = (dx + 1) // 2
        if dy == 0:
            return to_beside(near_packs.at[side], near_rims.at[side], k, dy, dx)
        source_row = NEAR if dy > 0 else 0
        return to_beside(
            near_packs.at[side, pl.ds(source_row, NEAR), :], near_corners.at[side, (1 - dy) // 2], k, dy, dx
        )

    def all_rims(k, wait):
        per_side = ((6 + 2) * NEAR, 6 * RIM, 2 * RIM)[k]
        level_with = (ROWS, 0, 2 * ROWS)[k]
        between = jnp.logical_and(inside[-1], inside[1])
        for when, count in ((between, 2 * per_side + level_with), (jnp.logical_not(between), per_side + level_with)):

            @pl.when(when)
            def _(count=count):
                as_much = fields.at[pl.ds(0, 2), pl.ds(0, 2), pl.ds(0, count // 4), :]
                wait(to_beside(as_much, as_much, k, 0, 1))

    def slot_copy(slots, which, step):
        return pltpu.make_async_remote_copy(
            slots.at[z], slots.at[z], slot_send.at[which], slot_recv.at[which],
            device_id=device(*ring_peer(step)), device_id_type=MESH,
        )

    def all_slots(slots, which):
        return pltpu.make_async_remote_copy(
            slots.at[pl.ds(0, ring - 1)], slots.at[pl.ds(0, ring - 1)], slot_send.at[which], slot_recv.at[which],
            device_id=device(*ring_peer(1)), device_id_type=MESH,
        )

    def plane_block(which, lat, line):
        rows = pl.ds(pl.multiple_of(PAD + lat * own_rows, 8), own_rows)
        if which == 0:
            return faces.at[:, pl.ds(line * per_line, per_line), rows, :]
        if which == 1:
            return rhs.at[pl.ds(line * per_line, per_line), rows, :]
        return sides.at[line, rows, :]

    def plane_copy(which, dx, dy, other):
        block = plane_block(which, la, y)
        return pltpu.make_async_remote_copy(
            block, block, plane_send.at[which], plane_recv.at[which],
            device_id=device(*plane_peer(dx, dy, other)), device_id_type=MESH,
        )

    def all_planes(which):
        count = len(hops) * (CORES if which == 1 else 1)
        lines, rows = (3, count // 3 * 8) if count % 3 == 0 else (1, count * 8)
        rows, of_tiles = pl.ds(0, rows), pl.ds(0, lines * per_line)
        block = (faces.at[:, of_tiles, rows, :], rhs.at[of_tiles, rows, :], sides.at[pl.ds(0, lines), rows, :])[which]
        return pltpu.make_async_remote_copy(
            block, block, plane_send.at[which], plane_recv.at[which],
            device_id=device(*partner), device_id_type=MESH,
        )

    def pass_copy(which, lat, line):
        block = plane_block(which, lat, line)
        return pltpu.make_async_remote_copy(
            block, block, pass_send.at[which], pass_recv.at[which],
            device_id=device(*partner), device_id_type=MESH,
        )

    def all_passed(which):
        half = pl.ds(PAD, lat_count * own_rows // CORES)
        block = (faces.at[:, :, half, :], rhs.at[:, half, :], sides.at[:, half, :])[which]
        return pltpu.make_async_remote_copy(
            block, block, pass_send.at[which], pass_recv.at[which],
            device_id=device(*partner), device_id_type=MESH,
        )

    def send_plane(which):
        for dx, dy in hops:
            for other in range(CORES if which == 1 else 1):
                plane_copy(which, dx, dy, other).start()
        if which == 1:
            pass_copy(which, la, y).start()

    def sent(which):
        all_planes(which).wait_send()
        if which == 1:
            pass_copy(1, la, y).wait_send()
        else:
            all_passed(which).wait_send()

    def take_bulk(which):
        all_planes(which).wait_recv()
        for line in range(planes_x):
            rows = pl.ds(pl.multiple_of(PAD + (line * CORES + core) * own_rows, 8), own_rows)
            block = faces.at[:, :, rows, :] if which == 0 else sides.at[:, rows, :]
            pltpu.make_async_remote_copy(
                block, block, pass_send.at[which], pass_recv.at[which],
                device_id=device(*partner), device_id_type=MESH,
            ).start()

    order = sorted(rims, key=lambda d: (d[1] == 0, d[0] == 0))
    for dy, dx in order:
        where_inside(dy, lambda dy=dy, dx=dx: near_copy(dy, dx).start())
    for step in ring_steps:
        slot_copy(face_slots, 0, step).start()
    for dy, dx in order:
        where_inside(dy, lambda dy=dy, dx=dx: rim_copy(dy, dx).start())

    def find_faces(some, base):
        first = some[0]
        n = first.chunk
        for row in first.chunks():
            deep = [first.load(base.at[0], c, row, n) for c in range(3)]
            east = east_of(deep, 1, lane_of(n))
            inverse = metric[2, pl.ds(RIM - first.rim + row, n), :]
            northern = metric[1, pl.ds(RIM - first.rim + row, n), :]
            for c in range(3):
                at = pl.ds(PAD + row, n)
                first.east[c, at, :] = jnp.minimum(deep[c], east[c]) * inverse
                first.north[c, at, :] = jnp.minimum(deep[c], first.load(base.at[0], c, row + 1, n)) * northern
        for fine, coarse in zip(some, some[1:]):
            for row in coarse.chunks():
                for c in range(3):
                    at = pl.ds(PAD + row, coarse.chunk)
                    coarse.east[c, at, :], coarse.north[c, at, :], coarse.source[c, at, :] = fine.coarse_faces(c, row, coarse.chunk)

    def descend(some):
        some[0].finish()
        some[0].descend()
        for fine, coarse in zip(some, some[1:]):
            for row in coarse.chunks():
                for c in range(3):
                    coarse.rhs[c, pl.ds(PAD + row, coarse.chunk), :] = fine.coarse_rhs(c, row, coarse.chunk)
            coarse.finish()
            coarse.descend()

    all_rims(0, lambda copy: copy.wait_recv())

    half_rows = ROWS // 2
    for row, count, quarter in (
        (0, NEAR, 1), (NEAR, half_rows, 0), (NEAR + half_rows, half_rows, 1), (NEAR + ROWS, NEAR, 0)
    ):
        wide_lane = lane_of(count)
        if count == NEAR:
            east, west = (near_corners[side, 0 if row == 0 else 1] for side in range(2))
        else:
            east, west = near_rims[0], near_rims[1]
        for k in range(3):
            place = quarter * (LANES // 2) + NEAR * k
            moved_east = pltpu.roll(east, LANES - place, 1) if place else east
            moved_west = pltpu.roll(west, LANES - NEAR - place, 1)
            near_fields[k, 2, pl.ds(PAD + row, count), :] = jnp.where(
                wide_lane < NEAR, moved_east, jnp.where(wide_lane >= LANES - NEAR, moved_west, 0.0)
            )

    find_faces(near_levels, near_fields)
    near3 = NEAR >> 3
    bottom_faces = [near_levels[2].coarse_faces(c, near3, own_rows) for c in range(2)]
    last = jnp.take_along_axis(bottom_faces[1][0], jnp.full_like(lane, LANES - 1), axis=1)
    last = jnp.where(lane % 8 == line_row, last, 0.0)
    for shift in (4, 2, 1):
        last = last + pltpu.roll(last, shift, 0)
    north = pltpu.roll(dense(bottom_faces[0][1], bottom_faces[1][1]), 1, 0)
    side_slots[z] = jnp.where(line_row == 0, north, last)[0:2]
    for step in ring_steps:
        slot_copy(side_slots, 2, step).start()
    descend(near_levels)

    bottom_rhs = [near_levels[2].coarse_rhs(c, near3, own_rows) for c in range(2)]
    packed = jnp.where(lane // 32 == line_row // 2, dense(*bottom_rhs), 0.0)
    for shift in (4, 2):
        packed = packed + pltpu.roll(packed, shift, 0)
    rhs_slots[z] = packed[0:2]
    for step in ring_steps:
        slot_copy(rhs_slots, 1, step).start()

    own_at = pl.ds(pl.multiple_of(PAD + la * own_rows, 8), own_rows)
    all_slots(face_slots, 0).wait_recv()
    for h in range(per_line):
        for k in range(3):
            value = None
            for j in range(group):
                slot = face_slots[h * group + j]
                shift = (32 * (j - k)) % LANES
                moved = pltpu.roll(slot, shift, 1) if shift else slot
                value = moved if value is None else jnp.where(lane // 32 == j, moved, value)
            faces[k, y * per_line + h, own_at, :] = value
    send_plane(0)

    def spread(ref, j, row):
        return jnp.broadcast_to(ref[j, pl.ds(row, 1), :], (own_rows, LANES))

    for k in (1, 2):
        all_rims(k, lambda copy: copy.wait_recv())
    for row in range(0, ROWS + 2 * RIM, CHUNK):
        wide_lane = lane_of(CHUNK)
        east, west = east_rim[pl.ds(row, CHUNK), :], west_rim[pl.ds(row, CHUNK), :]
        for k in range(3):
            moved_east = pltpu.roll(east, LANES - RIM * k, 1) if k else east
            moved_west = pltpu.roll(west, RIM * k, 1) if k else west
            fields[k, 2, pl.ds(PAD + row, CHUNK), :] = jnp.where(
                wide_lane < RIM, moved_east, jnp.where(wide_lane >= LANES - RIM, moved_west, 0.0)
            )
    find_faces(levels, fields)
    descend(levels)

    all_slots(side_slots, 2).wait_recv()
    side = None
    for j in range(ring):
        value = spread(side_slots, j, 1)
        side = value if side is None else jnp.where(lane // 8 == j, value, side)
    for h in range(per_line):
        for j in range(group):
            side = jnp.where((line_row == 7 - h) & (lane // 32 == j), spread(side_slots, h * group + j, 0), side)
    sides[y, own_at, :] = side
    send_plane(2)

    all_slots(rhs_slots, 1).wait_recv()
    unpick = 32 * (line_row // 2) + lane % 32
    for h in range(per_line):
        value = None
        for j in range(group):
            both_rows = jnp.where(line_row % 2 == 0, spread(rhs_slots, h * group + j, 0), spread(rhs_slots, h * group + j, 1))
            moved = jnp.take_along_axis(both_rows, unpick, axis=1)
            value = moved if value is None else jnp.where(lane // 32 == j, moved, value)
        rhs[y * per_line + h, own_at, :] = value
    send_plane(1)
    take_bulk(0)
    take_bulk(2)

    height = lat_count * own_rows
    everything = pl.ds(PAD, height)
    lane3 = lane_of(height)
    west_face, diagonal = bottom.at[1], bottom.at[2]
    rest_ref, image_ref, along_ref = bottom.at[0], bottom.at[3], bottom.at[4]
    all_passed(0).wait_recv()
    all_passed(2).wait_recv()
    east_face, north_face = bottom.at[5], bottom.at[6]
    lane_lat = lane_of(lat_count)
    for t in range(tiles):
        h, line = t % per_line, t // per_line
        north_face[t, everything, :] = faces[1, t, everything, :]
        north_face[t, pl.ds(PAD + 7, lat_count, stride=8), :] = sides[line, pl.ds(PAD + 7 - h, lat_count, stride=8), :]
        east = sides[line, pl.ds(PAD, lat_count, stride=8), :]
        for row in range(own_rows):
            at = pl.ds(PAD + row, lat_count, stride=8)
            moved = jnp.take_along_axis(east, 8 * (h * group + lane_lat // 32) + row, axis=1)
            east_face[t, at, :] = jnp.where(lane_lat % 32 == 31, moved, faces[0, t, at, :])
    for t in range(tiles):
        east = east_face[t, everything, :]
        before = east_face[(t - 1) % tiles, everything, :]
        west = pltpu.roll(jnp.where(lane3 >= LANES - 1, before, east), 1, 1)
        west_face[t, everything, :] = west
        diagonal[t, everything, :] = (
            faces[2, t, everything, :] + east + west
            + north_face[t, everything, :] + north_face[t, pl.ds(PAD - 1, height), :]
        )
    all_planes(1).wait_recv()
    pass_copy(1, la, y).wait_recv()

    def operate(ref):
        norm, product = None, None
        for t in range(tiles):
            value = ref[t, everything, :]
            east = pltpu.roll(jnp.where(lane3 < 1, ref[(t + 1) % tiles, everything, :], value), LANES - 1, 1)
            west = pltpu.roll(jnp.where(lane3 >= LANES - 1, ref[(t - 1) % tiles, everything, :], value), 1, 1)
            image = diagonal[t, everything, :] * value - (
                east_face[t, everything, :] * east
                + west_face[t, everything, :] * west
                + north_face[t, everything, :] * ref[t, pl.ds(PAD + 1, height), :]
                + north_face[t, pl.ds(PAD - 1, height), :] * ref[t, pl.ds(PAD - 1, height), :]
            )
            image_ref[t, everything, :] = image
            square, mixed = value * value, value * image
            norm = square if norm is None else norm + square
            product = mixed if product is None else product + mixed
        return jnp.sum(norm, keepdims=True), jnp.sum(product, keepdims=True)

    own_tile = lo // group
    near_tiles = (lax.rem(own_tile - 1 + tiles, tiles), own_tile, lax.rem(own_tile + 1, tiles))
    near = pl.ds(pl.multiple_of(la * own_rows, 8), 2 * PAD + own_rows)
    solved = [None] * 3
    direction = [None] * 3
    norm, product = operate(rhs)
    alpha = norm / product
    beta = None
    for iteration in range(BOTTOM_ITERS):
        current = rhs if iteration == 0 else rest_ref
        for k in range(3):
            value = current[near_tiles[k], near, :]
            direction[k] = value if iteration == 0 else value + beta * direction[k]
            solved[k] = alpha * direction[k] if iteration == 0 else solved[k] + alpha * direction[k]
        if iteration == BOTTOM_ITERS - 1:
            break
        for t in range(tiles):
            along = image_ref[t, everything, :]
            if iteration:
                along = along + beta * along_ref[t, everything, :]
            along_ref[t, everything, :] = along
            rest_ref[t, everything, :] = current[t, everything, :] - alpha * along
        norm_next, product = operate(rest_ref)
        beta = norm_next / norm
        alpha = norm_next / (product - beta * norm_next / alpha)
        norm = norm_next

    quarter = (lo % group) * 32
    lane = lane_of(8)
    place = quarter + jnp.where(lane < LANES // 2, 32 + lane // 8, (lane - LANES) // 8)
    wrapped = place & (LANES - 1)
    for row in range(0, 2 * PAD + own_rows, 8):
        left, mine, right = (solved[k][row : row + 8] for k in range(3))
        piece[0, pl.ds(row, 8), :] = jnp.take_along_axis(mine, quarter + lane // 8, axis=1)
        piece[1, pl.ds(row, 8), :] = jnp.take_along_axis(mine, quarter + 16 + lane // 8, axis=1)
        piece[2, pl.ds(row, 8), :] = jnp.where(
            place < 0, jnp.take_along_axis(left, wrapped, axis=1),
            jnp.where(place >= LANES, jnp.take_along_axis(right, wrapped, axis=1), jnp.take_along_axis(mine, wrapped, axis=1)),
        )

    levels[2].rise(piece, PAD - own3, False)
    levels[1].rise(levels[2].va, PAD, False)
    levels[0].rise(levels[1].va, PAD, True)
    stores = []
    for c in range(2):
        stores.append(pltpu.make_async_copy(
            top.va.at[c, pl.ds(PAD + RIM, ROWS), :], solution_out.at[:, pl.ds(c * LANES, LANES)], out_sem))
        stores[-1].start()
    for row in range(RIM, RIM + ROWS, CHUNK):
        _, image = top.apply(top.va, row, CHUNK, cols=2)
        for c in range(2):
            top.tmp[c, pl.ds(PAD + row, CHUNK), :] = top.load(top.rhs, c, row, CHUNK) - image[c]
    for c in range(2):
        stores.append(pltpu.make_async_copy(
            top.tmp.at[c, pl.ds(PAD + RIM, ROWS), :], residual_out.at[:, pl.ds(c * LANES, LANES)], out_sem))
        stores[-1].start()

    for k in range(3):
        all_rims(k, lambda copy: copy.wait_send())
    for which, slots in enumerate((face_slots, rhs_slots, side_slots)):
        all_slots(slots, which).wait_send()
        sent(which)
    for store in stores:
        store.wait()


def put_out(solution_in, residual_in, solution_out, residual_out, sems):
    copies = [
        pltpu.make_async_copy(solution_in, solution_out, sems.at[0]),
        pltpu.make_async_copy(residual_in, residual_out, sems.at[1]),
    ]
    for copy in copies:
        copy.start()
    for copy in copies:
        copy.wait()


def solution(mesh, ring=RING):
    lat_count, lon_count = mesh.shape["lat"], mesh.shape["lon"]
    tiles = lon_count * (COLS >> 3) // LANES
    height = lat_count * (ROWS >> 3) + 2 * PAD
    f32 = jnp.float32

    def padded(level, rim=RIM):
        return pltpu.VMEM((3, ((ROWS + 2 * rim) >> level) + 2 * PAD, LANES), f32)

    rows = ROWS + 2 * RIM
    scratch = [
        pltpu.VMEM((2, 2, ROWS, LANES), f32),
        pltpu.VMEM((2, 2, ROWS, LANES), jnp.int32),
        pltpu.VMEM((3, 3, rows + 2 * PAD, LANES), f32),
        *[padded(0)] * 8,
        *[padded(1)] * 10,
        *[padded(2)] * 10,
        pltpu.VMEM((3, 3, ROWS + 2 * NEAR + 2 * PAD, LANES), f32),
        *[padded(0, NEAR)] * 8,
        *[padded(1, NEAR)] * 10,
        *[padded(2, NEAR)] * 10,
        pltpu.VMEM((ROWS, LANES), f32),
        pltpu.VMEM((ROWS, LANES), f32),
        pltpu.VMEM((rows, LANES), f32),
        pltpu.VMEM((rows, LANES), f32),
        pltpu.VMEM((2, ROWS // 2, LANES), f32),
        pltpu.VMEM((2, ROWS // 2, LANES), f32),
        pltpu.VMEM((2, 2, NEAR, LANES), f32),
        pltpu.VMEM((3, rows, LANES), f32),
        pltpu.VMEM((ring, 8, LANES), f32),
        pltpu.VMEM((ring, 2, LANES), f32),
        pltpu.VMEM((ring, 2, LANES), f32),
        pltpu.VMEM((3, tiles, height, LANES), f32),
        pltpu.VMEM((tiles, height, LANES), f32),
        pltpu.VMEM((lon_count // ring, height, LANES), f32),
        pltpu.VMEM((7, tiles, height, LANES), f32),
        pltpu.VMEM((3, 2 * PAD + (ROWS >> 3), LANES), f32),
        pltpu.SemaphoreType.DMA,
        pltpu.SemaphoreType.DMA,
        pltpu.SemaphoreType.DMA((3,)),
        pltpu.SemaphoreType.DMA((3,)),
        pltpu.SemaphoreType.DMA((3,)),
        pltpu.SemaphoreType.DMA((3,)),
        pltpu.SemaphoreType.DMA((3,)),
        pltpu.SemaphoreType.DMA((3,)),
        pltpu.SemaphoreType.DMA((3,)),
        pltpu.SemaphoreType.DMA((3,)),
    ]

    def step(forcing, surface_term, sea_cells, levels):
        out = jax.ShapeDtypeStruct(forcing.shape, f32)
        results = pl.pallas_call(
            functools.partial(body, (lat_count, lon_count, ring)),
            out_shape=(out, out),
            in_specs=[pl.BlockSpec(memory_space=pltpu.HBM)] * 4,
            out_specs=[pl.BlockSpec(memory_space=pl.ANY)] * 2,
            scratch_shapes=scratch,
            compiler_params=pltpu.CompilerParams(
                collective_id=0, has_side_effects=True, vmem_limit_bytes=48 << 20
            ),
        )(*(pltpu.with_memory_space_constraint(v, pltpu.HBM) for v in (forcing, surface_term, sea_cells, levels)))
        return pl.pallas_call(
            put_out,
            out_shape=(out, out),
            in_specs=[pl.BlockSpec(memory_space=pltpu.VMEM)] * 2,
            out_specs=[pl.BlockSpec(memory_space=pltpu.HBM)] * 2,
            scratch_shapes=[pltpu.SemaphoreType.DMA((2,))],
        )(*(pltpu.with_memory_space_constraint(v, pltpu.VMEM) for v in results))

    return jax.shard_map(
        step,
        mesh=mesh,
        in_specs=(P("lat", "lon"),) * 4,
        out_specs=(P("lat", "lon"),) * 2,
        check_vma=False,
    )
```

```python
import functools
import math

import jax
import jax.numpy as jnp
from jax import lax
from jax.experimental import pallas as pl
from jax.experimental.pallas import tpu as pltpu
from jax.sharding import PartitionSpec as P

MESH = pl.DeviceIdType.MESH
DAMPING = 0.8
ROW_STEP = 150.0 / 8640.0
BAND_SOUTH = -50.0
BAND_ROWS = 512
BOTTOM_ITERS = 6
CORES = 2
RING = 8

ROWS, COLS = 64, 256
RIM = 32
NEAR = 16
PAD = 8
LANES = 128
CHUNK = 32


def lane_of(rows):
    return lax.broadcasted_iota(jnp.int32, (rows, LANES), 1)


def east_of(cols, shift, lane):
    count = len(cols)
    return [
        pltpu.roll(jnp.where(lane < shift, cols[(c + 1) % count], cols[c]), LANES - shift, 1)
        for c in range(count)
    ]


def west_of(cols, shift, lane):
    count = len(cols)
    return [
        pltpu.roll(jnp.where(lane >= LANES - shift, cols[(c - 1) % count], cols[c]), shift, 1)
        for c in range(count)
    ]


def pair_sum(value, shift, lane):
    upper = (lane & shift) != 0
    return value + jnp.where(upper, pltpu.roll(value, shift, 1), pltpu.roll(value, LANES - shift, 1))


def upper_of(value, shift, lane):
    return jnp.where((lane & shift) != 0, value, pltpu.roll(value, LANES - shift, 1))


def cosines(row):
    middle = math.radians(BAND_SOUTH + ROW_STEP * (BAND_ROWS / 2))
    off = (row - BAND_ROWS / 2) * math.radians(ROW_STEP)
    sq = off * off
    cos_off = 1.0 - sq * (1.0 / 2 - sq * (1.0 / 24 - sq * (1.0 / 720)))
    sin_off = off * (1.0 - sq * (1.0 / 6 - sq * (1.0 / 120 - sq * (1.0 / 5040))))
    return math.cos(middle) * cos_off - math.sin(middle) * sin_off


class Level:
    def __init__(self, index, rim, refs):
        self.index = index
        self.shift = 1 << index
        self.rows = (ROWS + 2 * rim) >> index
        self.rim = rim >> index
        self.east, self.west, self.north, self.source, self.diag, self.scale, self.rhs, self.va, self.vb, self.tmp = refs
        self.chunk = next(n for n in (16, 8) if self.rows % n == 0)

    def chunks(self):
        return range(0, self.rows, self.chunk)

    def load(self, ref, col, row, count):
        return ref[col, pl.ds(PAD + row, count), :]

    def apply(self, ref, row, count, cols=3):
        lane = lane_of(count)
        value = [self.load(ref, c, row, count) for c in range(3)]
        east = east_of(value, self.shift, lane)
        west = west_of(value, self.shift, lane)
        out = []
        for c in range(cols):
            around = (
                self.load(self.east, c, row, count) * east[c]
                + self.load(self.west, c, row, count) * west[c]
                + self.load(self.north, c, row, count) * self.load(ref, c, row + 1, count)
                + self.load(self.north, c, row - 1, count) * self.load(ref, c, row - 1, count)
            )
            out.append(self.load(self.diag, c, row, count) * value[c] - around)
        return value, out

    def smooth(self, source_ref, target_ref, chunks=None):
        for row, n in chunks or [(row, self.chunk) for row in self.chunks()]:
            value, image = self.apply(source_ref, row, n)
            for c in range(3):
                rest = self.load(self.rhs, c, row, n) - image[c]
                target_ref[c, pl.ds(PAD + row, n), :] = value[c] + self.load(self.scale, c, row, n) * rest

    def finish(self):
        n = self.chunk
        lane = lane_of(n)
        for row in self.chunks():
            east = [self.load(self.east, c, row, n) for c in range(3)]
            west = west_of(east, self.shift, lane)
            for c in range(3):
                source = self.load(self.source, c, row, n)
                total = (
                    source + east[c] + west[c]
                    + self.load(self.north, c, row, n) + self.load(self.north, c, row - 1, n)
                )
                diag = jnp.where(source > 0.0, total, 1.0)
                self.west[c, pl.ds(PAD + row, n), :] = west[c]
                self.diag[c, pl.ds(PAD + row, n), :] = diag
                self.scale[c, pl.ds(PAD + row, n), :] = DAMPING / diag

    def pairs(self, ref, col, row, count):
        return (
            ref[col, pl.ds(PAD + 2 * row, count, stride=2), :],
            ref[col, pl.ds(PAD + 2 * row + 1, count, stride=2), :],
        )

    def coarse_faces(self, col, row, count):
        lane = lane_of(count)
        lower, upper = self.pairs(self.east, col, row, count)
        east = upper_of(lower + upper, self.shift, lane)
        _, upper = self.pairs(self.north, col, row, count)
        north = pair_sum(upper, self.shift, lane)
        lower, upper = self.pairs(self.source, col, row, count)
        return east, north, pair_sum(lower + upper, self.shift, lane)

    def coarse_rhs(self, col, row, count):
        lower, upper = self.pairs(self.tmp, col, row, count)
        return pair_sum(lower + upper, self.shift, lane_of(count))

    def descend(self):
        n = self.chunk
        for row in self.chunks():
            for c in range(3):
                self.vb[c, pl.ds(PAD + row, n), :] = self.load(self.scale, c, row, n) * self.load(self.rhs, c, row, n)
        self.smooth(self.vb, self.va)
        for row in self.chunks():
            _, image = self.apply(self.va, row, n)
            for c in range(3):
                self.tmp[c, pl.ds(PAD + row, n), :] = self.load(self.rhs, c, row, n) - image[c]

    def rise(self, coarse, offset, masked):
        begin = (self.rim - 4) // 8 * 8
        count = self.rows - 2 * begin
        n = 16
        for row in range(begin // 2, (begin + count) // 2, n // 2):
            for c in range(3):
                added = coarse[c, pl.ds(offset + row, n // 2), :]
                for odd in range(2):
                    at = pl.ds(PAD + 2 * row + odd, n // 2, stride=2)
                    own = jnp.where(self.source[c, at, :] > 0.0, added, 0.0) if masked else added
                    self.va[c, at, :] = self.va[c, at, :] + own
        chunks = [(row, n) for row in range(begin, begin + count, n)]
        self.smooth(self.va, self.vb, chunks)
        self.smooth(self.vb, self.va, chunks)


def body(
    shape, forcing, surface, sea, depth_levels, solution_out, residual_out,
    in_f, in_i, fields, *rest
):
    lat_count, lon_count, ring = shape
    level_refs = [rest[0:8], rest[8:18], rest[18:28]]
    near_fields, near_refs = rest[28], [rest[29:37], rest[37:47], rest[47:57]]
    (
        west_pack, east_pack, east_rim, west_rim, near_packs, near_rims, near_corners, metric,
        face_slots, rhs_slots, side_slots, faces, rhs, sides, bottom, piece,
        in_sem, out_sem, rim_send, rim_recv, slot_send, slot_recv,
        plane_send, plane_recv, pass_send, pass_recv,
    ) = rest[57:]
    planes_y = lon_count // ring
    planes_x = lat_count // CORES
    tiles = lon_count * (COLS >> 3) // LANES
    per_line = tiles // planes_y
    la, lo = lax.axis_index("lat"), lax.axis_index("lon")
    x, core = la // CORES, la % CORES
    y, z = lo // ring, lo % ring
    own_rows = ROWS >> 3
    group = LANES // (COLS >> 3)

    def levels_of(rim, base, refs):
        first = (*refs[0][0:3], base.at[2], *refs[0][3:5], base.at[1], *refs[0][5:8])
        return [Level(0, rim, first), Level(1, rim, refs[1]), Level(2, rim, refs[2])]

    levels = levels_of(RIM, fields, level_refs)
    near_levels = levels_of(NEAR, near_fields, near_refs)
    top = levels[0]

    def device(lat, lon):
        return {"lat": lat, "lon": lon}

    loads = []
    for k, ref in enumerate((forcing, surface)):
        for c in range(2):
            loads.append(pltpu.make_async_copy(ref.at[:, pl.ds(c * LANES, LANES)], in_f.at[k, c], in_sem))
    for k, ref in enumerate((sea, depth_levels)):
        for c in range(2):
            loads.append(pltpu.make_async_copy(ref.at[:, pl.ds(c * LANES, LANES)], in_i.at[k, c], in_sem))
    rims = [(dy, dx) for dy in (-1, 0, 1) for dx in (-1, 0, 1) if (dy, dx) != (0, 0)]
    hops = sorted(
        ((dx, dy) for dx in range(planes_x) for dy in range(planes_y) if (dx, dy) != (0, 0)),
        key=lambda d: -min(d[0], planes_x - d[0]) - min(d[1], planes_y - d[1]),
    )
    ring_steps = sorted(range(1, ring), key=lambda d: -min(d, ring - d))
    barrier = pltpu.get_barrier_semaphore()

    def greet(lat, lon):
        pl.semaphore_signal(barrier, inc=1, device_id=device(lat, lon), device_id_type=MESH)

    def beside(dy, dx):
        return la + dy, lax.rem(lo + dx + lon_count, lon_count)

    def ring_peer(step):
        return la, y * ring + lax.rem(z + step, ring)

    def plane_peer(dx, dy, other=0):
        return lax.rem(x + dx, planes_x) * CORES + (1 - core if other else core), lax.rem(y + dy, planes_y) * ring + z

    partner = (x * CORES + (1 - core), lo)
    inside = {-1: la > 0, 0: None, 1: la < lat_count - 1}

    def where_inside(dy, act):
        if dy == 0:
            act()
        else:
            pl.when(inside[dy])(act)

    for dx, dy in hops:
        for other in range(CORES):
            greet(*plane_peer(dx, dy, other))
    for step in ring_steps:
        greet(*ring_peer(step))
    for dy, dx in sorted(rims, key=lambda d: (d[1] == 0, d[0] == 0)):
        where_inside(dy, lambda dy=dy, dx=dx: greet(*beside(dy, dx)))
    for load in loads:
        load.start()

    def clear(ref, col, row, count):
        ref[col, pl.ds(row, count), :] = jnp.zeros((count, LANES), ref.dtype)

    for base, group_of in ((fields, levels), (near_fields, near_levels)):
        for c in range(3):
            for k in range(3):
                clear(base.at[k], c, 0, PAD)
                clear(base.at[k], c, PAD + group_of[0].rows, PAD)
            for level in group_of:
                for ref in (level.north, level.va, level.vb):
                    clear(ref, c, 0, PAD)
                    clear(ref, c, PAD + level.rows, PAD)
    for ref in (faces.at[1], rhs, bottom.at[0], bottom.at[3], bottom.at[6]):
        for t in range(tiles):
            clear(ref, t, 0, PAD)
            clear(ref, t, PAD + lat_count * own_rows, PAD)
    for dy, row, near_row in ((-1, 0, 0), (1, RIM + ROWS, NEAR + ROWS)):

        @pl.when(jnp.logical_not(inside[dy]))
        def _(dy=dy, row=row, near_row=near_row):
            for k in range(3):
                for c in range(2):
                    clear(fields.at[k], c, PAD + row, RIM)
                    clear(near_fields.at[k], c, PAD + near_row, NEAR)
            for side in range(2):
                clear(near_corners.at[side], (dy + 1) // 2, 0, NEAR)
            east_rim[pl.ds(row, RIM), :] = jnp.zeros((RIM, LANES), jnp.float32)
            west_rim[pl.ds(row, RIM), :] = jnp.zeros((RIM, LANES), jnp.float32)

    first = la * ROWS - RIM
    for row in range(0, ROWS + 2 * RIM, CHUNK):
        number = (first + row + lax.broadcasted_iota(jnp.int32, (CHUNK, LANES), 0)).astype(jnp.float32)
        metric[0, pl.ds(row, CHUNK), :] = cosines(number + 0.5)
        metric[2, pl.ds(row, CHUNK), :] = 1.0 / metric[0, pl.ds(row, CHUNK), :]
        metric[1, pl.ds(row, CHUNK), :] = cosines(number + 1.0)

    for load in loads:
        load.wait()
    near_strips = [None, None]
    for row in range(0, ROWS, CHUNK):
        at = pl.ds(PAD + RIM + row, CHUNK)
        center = metric[0, pl.ds(RIM + row, CHUNK), :]
        own = pl.ds(row, CHUNK)
        lane = lane_of(CHUNK)
        values = []
        for c in range(2):
            sea_mask = in_i[0, c, own, :].astype(jnp.float32)
            layers = in_i[1, c, own, :].astype(jnp.float32)
            deep = sea_mask * ((layers + layers * (layers - 1.0) / 20.0) / 200.0)
            right = in_f[0, c, own, :] * sea_mask
            source = in_f[1, c, own, :] * center * sea_mask
            values.append((deep, right, source))
            for k in range(3):
                fields[k, c, at, :] = values[c][k]
                near_fields[k, c, pl.ds(PAD + NEAR + row, CHUNK), :] = values[c][k]
        packed_west, packed_east = values[0][0], values[1][0]
        for k in range(1, 3):
            part = (lane >= RIM * k) & (lane < RIM * (k + 1))
            packed_west = jnp.where(part, pltpu.roll(values[0][k], RIM * k, 1), packed_west)
            part = (lane < LANES - RIM * k) & (lane >= LANES - RIM * (k + 1))
            packed_east = jnp.where(part, pltpu.roll(values[1][k], LANES - RIM * k, 1), packed_east)
        west_pack[own, :] = packed_west
        east_pack[own, :] = packed_east
        for side in range(2):
            for k in range(3):
                place = row * 2 + NEAR * k
                moved = pltpu.roll(values[side][k], (place + NEAR * side) % LANES, 1)
                part = (lane >= place) & (lane < place + NEAR)
                near_strips[side] = moved if near_strips[side] is None else jnp.where(part, moved, near_strips[side])
    for side in range(2):
        near_packs[side] = near_strips[side]

    own3 = RIM >> 3
    lane = lane_of(own_rows)
    line_row = lax.broadcasted_iota(jnp.int32, (own_rows, LANES), 0)
    pick = (lane % 16) * 8
    low = (lane % 32) < 16

    def dense(west_tile, east_tile, last=0):
        return jnp.where(
            low, jnp.take_along_axis(west_tile, pick + last, axis=1), jnp.take_along_axis(east_tile, pick + last, axis=1)
        )

    def lane_sum(value):
        for shift in (1, 2, 4):
            value = pair_sum(value, shift, lane)
        return value

    def every8(k, c, row):
        return fields[k, c, pl.ds(PAD + RIM + row, own_rows, stride=8), :]

    sums = [[None, None] for _ in range(3)]
    for row in range(8):
        deep = [every8(0, c, row) for c in range(2)]
        east = east_of(deep, 1, lane)
        inverse = metric[2, pl.ds(RIM + row, own_rows, stride=8), :]
        for c in range(2):
            face, term = jnp.minimum(deep[c], east[c]) * inverse, every8(2, c, row)
            sums[0][c] = face if row == 0 else sums[0][c] + face
            sums[2][c] = term if row == 0 else sums[2][c] + term
    for c in range(2):
        above = pltpu.roll(every8(0, c, 0), own_rows - 1, 0)
        face = jnp.minimum(every8(0, c, 7), above) * metric[1, pl.ds(RIM + 7, own_rows, stride=8), :]
        sums[1][c] = lane_sum(face)
        sums[2][c] = lane_sum(sums[2][c])
    parts = [dense(*sums[0], last=7), dense(*sums[1]), dense(*sums[2])]
    face_slots[z] = jnp.where(lane < 32, parts[0], jnp.where(lane < 64, parts[1], parts[2]))

    greeted = 2 + (ring - 1) + CORES * len(hops)
    both = inside[-1].astype(jnp.int32) + inside[1].astype(jnp.int32)
    pl.semaphore_wait(barrier, greeted + 3 * both)

    def to_beside(source, target, k, dy, dx):
        return pltpu.make_async_remote_copy(
            source, target, rim_send.at[k], rim_recv.at[k],
            device_id=device(*beside(dy, dx)), device_id_type=MESH,
        )

    def rim_copy(dy, dx):
        k = 1 if dx == 0 else 2
        if dx == 0:
            source_row, target_row = (ROWS - RIM, 0) if dy > 0 else (0, RIM + ROWS)
            return to_beside(
                fields.at[:, pl.ds(0, 2), pl.ds(PAD + RIM + source_row, RIM), :],
                fields.at[:, pl.ds(0, 2), pl.ds(PAD + target_row, RIM), :], k, dy, dx,
            )
        source_row, target_row = {1: (ROWS - RIM, 0), -1: (0, RIM + ROWS), 0: (0, RIM)}[dy]
        count = ROWS if dy == 0 else RIM
        return to_beside(
            (east_pack if dx > 0 else west_pack).at[pl.ds(source_row, count), :],
            (west_rim if dx > 0 else east_rim).at[pl.ds(target_row, count), :], k, dy, dx,
        )

    def near_copy(dy, dx):
        k = 0
        if dx == 0:
            source_row, target_row = (ROWS - NEAR, 0) if dy > 0 else (0, NEAR + ROWS)
            return to_beside(
                near_fields.at[:, pl.ds(0, 2), pl.ds(PAD + NEAR + source_row, NEAR), :],
                near_fields.at[:, pl.ds(0, 2), pl.ds(PAD + target_row, NEAR), :], k, dy, dx,
            )
        side = (dx + 1) // 2
        if dy == 0:
            return to_beside(near_packs.at[side], near_rims.at[side], k, dy, dx)
        source_row = NEAR if dy > 0 else 0
        return to_beside(
            near_packs.at[side, pl.ds(source_row, NEAR), :], near_corners.at[side, (1 - dy) // 2], k, dy, dx
        )

    def all_rims(k, wait):
        per_side = ((6 + 2) * NEAR, 6 * RIM, 2 * RIM)[k]
        level_with = (ROWS, 0, 2 * ROWS)[k]
        between = jnp.logical_and(inside[-1], inside[1])
        for when, count in ((between, 2 * per_side + level_with), (jnp.logical_not(between), per_side + level_with)):

            @pl.when(when)
            def _(count=count):
                as_much = fields.at[pl.ds(0, 2), pl.ds(0, 2), pl.ds(0, count // 4), :]
                wait(to_beside(as_much, as_much, k, 0, 1))

    def slot_copy(slots, which, step):
        return pltpu.make_async_remote_copy(
            slots.at[z], slots.at[z], slot_send.at[which], slot_recv.at[which],
            device_id=device(*ring_peer(step)), device_id_type=MESH,
        )

    def all_slots(slots, which):
        return pltpu.make_async_remote_copy(
            slots.at[pl.ds(0, ring - 1)], slots.at[pl.ds(0, ring - 1)], slot_send.at[which], slot_recv.at[which],
            device_id=device(*ring_peer(1)), device_id_type=MESH,
        )

    def plane_block(which, lat, line):
        rows = pl.ds(pl.multiple_of(PAD + lat * own_rows, 8), own_rows)
        if which == 0:
            return faces.at[:, pl.ds(line * per_line, per_line), rows, :]
        if which == 1:
            return rhs.at[pl.ds(line * per_line, per_line), rows, :]
        return sides.at[line, rows, :]

    def plane_copy(which, dx, dy, other):
        block = plane_block(which, la, y)
        return pltpu.make_async_remote_copy(
            block, block, plane_send.at[which], plane_recv.at[which],
            device_id=device(*plane_peer(dx, dy, other)), device_id_type=MESH,
        )

    def all_planes(which):
        count = len(hops) * (CORES if which == 1 else 1)
        lines, rows = (3, count // 3 * 8) if count % 3 == 0 else (1, count * 8)
        rows, of_tiles = pl.ds(0, rows), pl.ds(0, lines * per_line)
        block = (faces.at[:, of_tiles, rows, :], rhs.at[of_tiles, rows, :], sides.at[pl.ds(0, lines), rows, :])[which]
        return pltpu.make_async_remote_copy(
            block, block, plane_send.at[which], plane_recv.at[which],
            device_id=device(*partner), device_id_type=MESH,
        )

    def pass_copy(which, lat, line):
        block = plane_block(which, lat, line)
        return pltpu.make_async_remote_copy(
            block, block, pass_send.at[which], pass_recv.at[which],
            device_id=device(*partner), device_id_type=MESH,
        )

    def all_passed(which):
        half = pl.ds(PAD, lat_count * own_rows // CORES)
        block = (faces.at[:, :, half, :], rhs.at[:, half, :], sides.at[:, half, :])[which]
        return pltpu.make_async_remote_copy(
            block, block, pass_send.at[which], pass_recv.at[which],
            device_id=device(*partner), device_id_type=MESH,
        )

    def send_plane(which):
        for dx, dy in hops:
            for other in range(CORES if which == 1 else 1):
                plane_copy(which, dx, dy, other).start()
        if which == 1:
            pass_copy(which, la, y).start()

    def sent(which):
        all_planes(which).wait_send()
        if which == 1:
            pass_copy(1, la, y).wait_send()
        else:
            all_passed(which).wait_send()

    def take_bulk(which):
        all_planes(which).wait_recv()
        for line in range(planes_x):
            rows = pl.ds(pl.multiple_of(PAD + (line * CORES + core) * own_rows, 8), own_rows)
            block = faces.at[:, :, rows, :] if which == 0 else sides.at[:, rows, :]
            pltpu.make_async_remote_copy(
                block, block, pass_send.at[which], pass_recv.at[which],
                device_id=device(*partner), device_id_type=MESH,
            ).start()

    order = sorted(rims, key=lambda d: (d[1] == 0, d[0] == 0))
    for dy, dx in order:
        where_inside(dy, lambda dy=dy, dx=dx: near_copy(dy, dx).start())
    for step in ring_steps:
        slot_copy(face_slots, 0, step).start()
    for dy, dx in order:
        where_inside(dy, lambda dy=dy, dx=dx: rim_copy(dy, dx).start())

    def find_faces(some, base):
        first = some[0]
        n = first.chunk
        for row in first.chunks():
            deep = [first.load(base.at[0], c, row, n) for c in range(3)]
            east = east_of(deep, 1, lane_of(n))
            inverse = metric[2, pl.ds(RIM - first.rim + row, n), :]
            northern = metric[1, pl.ds(RIM - first.rim + row, n), :]
            for c in range(3):
                at = pl.ds(PAD + row, n)
                first.east[c, at, :] = jnp.minimum(deep[c], east[c]) * inverse
                first.north[c, at, :] = jnp.minimum(deep[c], first.load(base.at[0], c, row + 1, n)) * northern
        for fine, coarse in zip(some, some[1:]):
            for row in coarse.chunks():
                for c in range(3):
                    at = pl.ds(PAD + row, coarse.chunk)
                    coarse.east[c, at, :], coarse.north[c, at, :], coarse.source[c, at, :] = fine.coarse_faces(c, row, coarse.chunk)

    def descend(some):
        some[0].finish()
        some[0].descend()
        for fine, coarse in zip(some, some[1:]):
            for row in coarse.chunks():
                for c in range(3):
                    coarse.rhs[c, pl.ds(PAD + row, coarse.chunk), :] = fine.coarse_rhs(c, row, coarse.chunk)
            coarse.finish()
            coarse.descend()

    all_rims(0, lambda copy: copy.wait_recv())

    half_rows = ROWS // 2
    for row, count, quarter in (
        (0, NEAR, 1), (NEAR, half_rows, 0), (NEAR + half_rows, half_rows, 1), (NEAR + ROWS, NEAR, 0)
    ):
        wide_lane = lane_of(count)
        if count == NEAR:
            east, west = (near_corners[side, 0 if row == 0 else 1] for side in range(2))
        else:
            east, west = near_rims[0], near_rims[1]
        for k in range(3):
            place = quarter * (LANES // 2) + NEAR * k
            moved_east = pltpu.roll(east, LANES - place, 1) if place else east
            moved_west = pltpu.roll(west, LANES - NEAR - place, 1)
            near_fields[k, 2, pl.ds(PAD + row, count), :] = jnp.where(
                wide_lane < NEAR, moved_east, jnp.where(wide_lane >= LANES - NEAR, moved_west, 0.0)
            )

    find_faces(near_levels, near_fields)
    near3 = NEAR >> 3
    bottom_faces = [near_levels[2].coarse_faces(c, near3, own_rows) for c in range(2)]
    last = jnp.take_along_axis(bottom_faces[1][0], jnp.full_like(lane, LANES - 1), axis=1)
    last = jnp.where(lane % 8 == line_row, last, 0.0)
    for shift in (4, 2, 1):
        last = last + pltpu.roll(last, shift, 0)
    north = pltpu.roll(dense(bottom_faces[0][1], bottom_faces[1][1]), 1, 0)
    side_slots[z] = jnp.where(line_row == 0, north, last)[0:2]
    for step in ring_steps:
        slot_copy(side_slots, 2, step).start()
    descend(near_levels)

    bottom_rhs = [near_levels[2].coarse_rhs(c, near3, own_rows) for c in range(2)]
    packed = jnp.where(lane // 32 == line_row // 2, dense(*bottom_rhs), 0.0)
    for shift in (4, 2):
        packed = packed + pltpu.roll(packed, shift, 0)
    rhs_slots[z] = packed[0:2]
    for step in ring_steps:
        slot_copy(rhs_slots, 1, step).start()

    own_at = pl.ds(pl.multiple_of(PAD + la * own_rows, 8), own_rows)
    all_slots(face_slots, 0).wait_recv()
    for h in range(per_line):
        for k in range(3):
            value = None
            for j in range(group):
                slot = face_slots[h * group + j]
                shift = (32 * (j - k)) % LANES
                moved = pltpu.roll(slot, shift, 1) if shift else slot
                value = moved if value is None else jnp.where(lane // 32 == j, moved, value)
            faces[k, y * per_line + h, own_at, :] = value
    send_plane(0)

    def spread(ref, j, row):
        return jnp.broadcast_to(ref[j, pl.ds(row, 1), :], (own_rows, LANES))

    for k in (1, 2):
        all_rims(k, lambda copy: copy.wait_recv())
    for row in range(0, ROWS + 2 * RIM, CHUNK):
        wide_lane = lane_of(CHUNK)
        east, west = east_rim[pl.ds(row, CHUNK), :], west_rim[pl.ds(row, CHUNK), :]
        for k in range(3):
            moved_east = pltpu.roll(east, LANES - RIM * k, 1) if k else east
            moved_west = pltpu.roll(west, RIM * k, 1) if k else west
            fields[k, 2, pl.ds(PAD + row, CHUNK), :] = jnp.where(
                wide_lane < RIM, moved_east, jnp.where(wide_lane >= LANES - RIM, moved_west, 0.0)
            )
    find_faces(levels, fields)
    descend(levels)

    all_slots(side_slots, 2).wait_recv()
    side = None
    for j in range(ring):
        value = spread(side_slots, j, 1)
        side = value if side is None else jnp.where(lane // 8 == j, value, side)
    for h in range(per_line):
        for j in range(group):
            side = jnp.where((line_row == 7 - h) & (lane // 32 == j), spread(side_slots, h * group + j, 0), side)
    sides[y, own_at, :] = side
    send_plane(2)

    all_slots(rhs_slots, 1).wait_recv()
    unpick = 32 * (line_row // 2) + lane % 32
    for h in range(per_line):
        value = None
        for j in range(group):
            both_rows = jnp.where(line_row % 2 == 0, spread(rhs_slots, h * group + j, 0), spread(rhs_slots, h * group + j, 1))
            moved = jnp.take_along_axis(both_rows, unpick, axis=1)
            value = moved if value is None else jnp.where(lane // 32 == j, moved, value)
        rhs[y * per_line + h, own_at, :] = value
    send_plane(1)
    take_bulk(0)
    take_bulk(2)

    height = lat_count * own_rows
    everything = pl.ds(PAD, height)
    lane3 = lane_of(height)
    west_face, diagonal = bottom.at[1], bottom.at[2]
    rest_ref, image_ref, along_ref = bottom.at[0], bottom.at[3], bottom.at[4]
    image_image, far_ref = bottom.at[7], bottom.at[8]
    all_passed(0).wait_recv()
    all_passed(2).wait_recv()
    east_face, north_face = bottom.at[5], bottom.at[6]
    lane_lat = lane_of(lat_count)
    for t in range(tiles):
        h, line = t % per_line, t // per_line
        north_face[t, everything, :] = faces[1, t, everything, :]
        north_face[t, pl.ds(PAD + 7, lat_count, stride=8), :] = sides[line, pl.ds(PAD + 7 - h, lat_count, stride=8), :]
        east = sides[line, pl.ds(PAD, lat_count, stride=8), :]
        for row in range(own_rows):
            at = pl.ds(PAD + row, lat_count, stride=8)
            moved = jnp.take_along_axis(east, 8 * (h * group + lane_lat // 32) + row, axis=1)
            east_face[t, at, :] = jnp.where(lane_lat % 32 == 31, moved, faces[0, t, at, :])
    for t in range(tiles):
        east = east_face[t, everything, :]
        before = east_face[(t - 1) % tiles, everything, :]
        west = pltpu.roll(jnp.where(lane3 >= LANES - 1, before, east), 1, 1)
        west_face[t, everything, :] = west
        diagonal[t, everything, :] = (
            faces[2, t, everything, :] + east + west
            + north_face[t, everything, :] + north_face[t, pl.ds(PAD - 1, height), :]
        )
    all_planes(1).wait_recv()
    pass_copy(1, la, y).wait_recv()

    part = 16
    lane3 = lane_of(part)
    pieces = [(t, row) for t in range(tiles) for row in range(PAD, PAD + height, part)]

    def add(total, value):
        return value if total is None else total + value

    def operate(ref, target, sums):
        norm, product = None, None
        for t, row in pieces:
            at = pl.ds(row, part)
            value = ref[t, at, :]
            east = pltpu.roll(jnp.where(lane3 < 1, ref[(t + 1) % tiles, at, :], value), LANES - 1, 1)
            west = pltpu.roll(jnp.where(lane3 >= LANES - 1, ref[(t - 1) % tiles, at, :], value), 1, 1)
            image = diagonal[t, at, :] * value - (
                east_face[t, at, :] * east
                + west_face[t, at, :] * west
                + north_face[t, at, :] * ref[t, pl.ds(row + 1, part), :]
                + north_face[t, pl.ds(row - 1, part), :] * ref[t, pl.ds(row - 1, part), :]
            )
            target[t, at, :] = image
            if sums:
                norm, product = add(norm, value * value), add(product, value * image)
        if sums:
            return jnp.sum(norm, keepdims=True), jnp.sum(product, keepdims=True)

    own_tile = lo // group
    near_tiles = (lax.rem(own_tile - 1 + tiles, tiles), own_tile, lax.rem(own_tile + 1, tiles))
    near = pl.ds(pl.multiple_of(la * own_rows, 8), 2 * PAD + own_rows)
    solved = [None] * 3
    direction = [None] * 3
    norm, product = operate(rhs, image_ref, True)
    beta = None
    for iteration in range(BOTTOM_ITERS):
        final = iteration == BOTTOM_ITERS - 1
        current = rhs if iteration == 0 else rest_ref
        if not final:
            operate(image_ref, image_image, False)
        if iteration:
            beta = norm * inverse_norm
            product = product - beta * norm * inverse_alpha
        alpha = norm / product
        inverse_norm = 1.0 / norm
        inverse_alpha = product * inverse_norm
        for k in range(3):
            value = current[near_tiles[k], near, :]
            direction[k] = value if iteration == 0 else value + beta * direction[k]
            solved[k] = alpha * direction[k] if iteration == 0 else solved[k] + alpha * direction[k]
        if final:
            break
        norm, product = None, None
        for t, row in pieces:
            at = pl.ds(row, part)
            image = image_ref[t, at, :]
            along, far = image, image_image[t, at, :]
            if iteration:
                along = along + beta * along_ref[t, at, :]
                far = far + beta * far_ref[t, at, :]
            rest = current[t, at, :] - alpha * along
            image = image - alpha * far
            rest_ref[t, at, :] = rest
            if iteration < BOTTOM_ITERS - 2:
                along_ref[t, at, :] = along
                far_ref[t, at, :] = far
                image_ref[t, at, :] = image
            norm, product = add(norm, rest * rest), add(product, rest * image)
        norm, product = jnp.sum(norm, keepdims=True), jnp.sum(product, keepdims=True)

    quarter = (lo % group) * 32
    lane = lane_of(8)
    place = quarter + jnp.where(lane < LANES // 2, 32 + lane // 8, (lane - LANES) // 8)
    wrapped = place & (LANES - 1)
    for row in range(0, 2 * PAD + own_rows, 8):
        left, mine, right = (solved[k][row : row + 8] for k in range(3))
        piece[0, pl.ds(row, 8), :] = jnp.take_along_axis(mine, quarter + lane // 8, axis=1)
        piece[1, pl.ds(row, 8), :] = jnp.take_along_axis(mine, quarter + 16 + lane // 8, axis=1)
        piece[2, pl.ds(row, 8), :] = jnp.where(
            place < 0, jnp.take_along_axis(left, wrapped, axis=1),
            jnp.where(place >= LANES, jnp.take_along_axis(right, wrapped, axis=1), jnp.take_along_axis(mine, wrapped, axis=1)),
        )

    levels[2].rise(piece, PAD - own3, False)
    levels[1].rise(levels[2].va, PAD, False)
    levels[0].rise(levels[1].va, PAD, True)
    stores = []
    for c in range(2):
        stores.append(pltpu.make_async_copy(
            top.va.at[c, pl.ds(PAD + RIM, ROWS), :], solution_out.at[:, pl.ds(c * LANES, LANES)], out_sem))
        stores[-1].start()
    for row in range(RIM, RIM + ROWS, CHUNK):
        _, image = top.apply(top.va, row, CHUNK, cols=2)
        for c in range(2):
            top.tmp[c, pl.ds(PAD + row, CHUNK), :] = top.load(top.rhs, c, row, CHUNK) - image[c]
    for c in range(2):
        stores.append(pltpu.make_async_copy(
            top.tmp.at[c, pl.ds(PAD + RIM, ROWS), :], residual_out.at[:, pl.ds(c * LANES, LANES)], out_sem))
        stores[-1].start()

    for k in range(3):
        all_rims(k, lambda copy: copy.wait_send())
    for which, slots in enumerate((face_slots, rhs_slots, side_slots)):
        all_slots(slots, which).wait_send()
        sent(which)
    for store in stores:
        store.wait()


def put_out(solution_in, residual_in, solution_out, residual_out, sems):
    copies = [
        pltpu.make_async_copy(solution_in, solution_out, sems.at[0]),
        pltpu.make_async_copy(residual_in, residual_out, sems.at[1]),
    ]
    for copy in copies:
        copy.start()
    for copy in copies:
        copy.wait()


def solution(mesh, ring=RING):
    lat_count, lon_count = mesh.shape["lat"], mesh.shape["lon"]
    tiles = lon_count * (COLS >> 3) // LANES
    height = lat_count * (ROWS >> 3) + 2 * PAD
    f32 = jnp.float32

    def padded(level, rim=RIM):
        return pltpu.VMEM((3, ((ROWS + 2 * rim) >> level) + 2 * PAD, LANES), f32)

    rows = ROWS + 2 * RIM
    scratch = [
        pltpu.VMEM((2, 2, ROWS, LANES), f32),
        pltpu.VMEM((2, 2, ROWS, LANES), jnp.int32),
        pltpu.VMEM((3, 3, rows + 2 * PAD, LANES), f32),
        *[padded(0)] * 8,
        *[padded(1)] * 10,
        *[padded(2)] * 10,
        pltpu.VMEM((3, 3, ROWS + 2 * NEAR + 2 * PAD, LANES), f32),
        *[padded(0, NEAR)] * 8,
        *[padded(1, NEAR)] * 10,
        *[padded(2, NEAR)] * 10,
        pltpu.VMEM((ROWS, LANES), f32),
        pltpu.VMEM((ROWS, LANES), f32),
        pltpu.VMEM((rows, LANES), f32),
        pltpu.VMEM((rows, LANES), f32),
        pltpu.VMEM((2, ROWS // 2, LANES), f32),
        pltpu.VMEM((2, ROWS // 2, LANES), f32),
        pltpu.VMEM((2, 2, NEAR, LANES), f32),
        pltpu.VMEM((3, rows, LANES), f32),
        pltpu.VMEM((ring, 8, LANES), f32),
        pltpu.VMEM((ring, 2, LANES), f32),
        pltpu.VMEM((ring, 2, LANES), f32),
        pltpu.VMEM((3, tiles, height, LANES), f32),
        pltpu.VMEM((tiles, height, LANES), f32),
        pltpu.VMEM((lon_count // ring, height, LANES), f32),
        pltpu.VMEM((9, tiles, height, LANES), f32),
        pltpu.VMEM((3, 2 * PAD + (ROWS >> 3), LANES), f32),
        pltpu.SemaphoreType.DMA,
        pltpu.SemaphoreType.DMA,
        pltpu.SemaphoreType.DMA((3,)),
        pltpu.SemaphoreType.DMA((3,)),
        pltpu.SemaphoreType.DMA((3,)),
        pltpu.SemaphoreType.DMA((3,)),
        pltpu.SemaphoreType.DMA((3,)),
        pltpu.SemaphoreType.DMA((3,)),
        pltpu.SemaphoreType.DMA((3,)),
        pltpu.SemaphoreType.DMA((3,)),
    ]

    def step(forcing, surface_term, sea_cells, levels):
        out = jax.ShapeDtypeStruct(forcing.shape, f32)
        results = pl.pallas_call(
            functools.partial(body, (lat_count, lon_count, ring)),
            out_shape=(out, out),
            in_specs=[pl.BlockSpec(memory_space=pltpu.HBM)] * 4,
            out_specs=[pl.BlockSpec(memory_space=pl.ANY)] * 2,
            scratch_shapes=scratch,
            compiler_params=pltpu.CompilerParams(
                collective_id=0, has_side_effects=True, vmem_limit_bytes=48 << 20
            ),
        )(*(pltpu.with_memory_space_constraint(v, pltpu.HBM) for v in (forcing, surface_term, sea_cells, levels)))
        return pl.pallas_call(
            put_out,
            out_shape=(out, out),
            in_specs=[pl.BlockSpec(memory_space=pltpu.VMEM)] * 2,
            out_specs=[pl.BlockSpec(memory_space=pltpu.HBM)] * 2,
            scratch_shapes=[pltpu.SemaphoreType.DMA((2,))],
        )(*(pltpu.with_memory_space_constraint(v, pltpu.VMEM) for v in results))

    return jax.shard_map(
        step,
        mesh=mesh,
        in_specs=(P("lat", "lon"),) * 4,
        out_specs=(P("lat", "lon"),) * 2,
        check_vma=False,
    )
```

```python
import functools
import math

import jax
import jax.numpy as jnp
from jax import lax
from jax.experimental import pallas as pl
from jax.experimental.pallas import tpu as pltpu
from jax.sharding import PartitionSpec as P

MESH = pl.DeviceIdType.MESH
DAMPING = 0.8
ROW_STEP = 150.0 / 8640.0
BAND_SOUTH = -50.0
BAND_ROWS = 512
BOTTOM_ITERS = 6
CORES = 2
RING = 8

ROWS, COLS = 64, 256
RIM = 32
NEAR = 16
PAD = 8
LANES = 128
CHUNK = 32


def lane_of(rows):
    return lax.broadcasted_iota(jnp.int32, (rows, LANES), 1)


def east_of(cols, shift, lane):
    count = len(cols)
    return [
        pltpu.roll(jnp.where(lane < shift, cols[(c + 1) % count], cols[c]), LANES - shift, 1)
        for c in range(count)
    ]


def west_of(cols, shift, lane):
    count = len(cols)
    return [
        pltpu.roll(jnp.where(lane >= LANES - shift, cols[(c - 1) % count], cols[c]), shift, 1)
        for c in range(count)
    ]


def pair_sum(value, shift, lane):
    upper = (lane & shift) != 0
    return value + jnp.where(upper, pltpu.roll(value, shift, 1), pltpu.roll(value, LANES - shift, 1))


def upper_of(value, shift, lane):
    return jnp.where((lane & shift) != 0, value, pltpu.roll(value, LANES - shift, 1))


def cosines(row):
    middle = math.radians(BAND_SOUTH + ROW_STEP * (BAND_ROWS / 2))
    off = (row - BAND_ROWS / 2) * math.radians(ROW_STEP)
    sq = off * off
    cos_off = 1.0 - sq * (1.0 / 2 - sq * (1.0 / 24 - sq * (1.0 / 720)))
    sin_off = off * (1.0 - sq * (1.0 / 6 - sq * (1.0 / 120 - sq * (1.0 / 5040))))
    return math.cos(middle) * cos_off - math.sin(middle) * sin_off


class Level:
    def __init__(self, index, rim, refs):
        self.index = index
        self.shift = 1 << index
        self.rows = (ROWS + 2 * rim) >> index
        self.rim = rim >> index
        self.east, self.west, self.north, self.source, self.diag, self.scale, self.rhs, self.va, self.vb, self.tmp = refs
        self.chunk = next(n for n in (16, 8) if self.rows % n == 0)

    def chunks(self):
        return range(0, self.rows, self.chunk)

    def load(self, ref, col, row, count):
        return ref[col, pl.ds(PAD + row, count), :]

    def apply(self, ref, row, count, cols=3):
        lane = lane_of(count)
        value = [self.load(ref, c, row, count) for c in range(3)]
        east = east_of(value, self.shift, lane)
        west = west_of(value, self.shift, lane)
        out = []
        for c in range(cols):
            around = (
                self.load(self.east, c, row, count) * east[c]
                + self.load(self.west, c, row, count) * west[c]
                + self.load(self.north, c, row, count) * self.load(ref, c, row + 1, count)
                + self.load(self.north, c, row - 1, count) * self.load(ref, c, row - 1, count)
            )
            out.append(self.load(self.diag, c, row, count) * value[c] - around)
        return value, out

    def smooth(self, source_ref, target_ref, chunks=None):
        for row, n in chunks or [(row, self.chunk) for row in self.chunks()]:
            value, image = self.apply(source_ref, row, n)
            for c in range(3):
                rest = self.load(self.rhs, c, row, n) - image[c]
                target_ref[c, pl.ds(PAD + row, n), :] = value[c] + self.load(self.scale, c, row, n) * rest

    def finish(self):
        n = self.chunk
        lane = lane_of(n)
        for row in self.chunks():
            east = [self.load(self.east, c, row, n) for c in range(3)]
            west = west_of(east, self.shift, lane)
            for c in range(3):
                source = self.load(self.source, c, row, n)
                total = (
                    source + east[c] + west[c]
                    + self.load(self.north, c, row, n) + self.load(self.north, c, row - 1, n)
                )
                diag = jnp.where(source > 0.0, total, 1.0)
                self.west[c, pl.ds(PAD + row, n), :] = west[c]
                self.diag[c, pl.ds(PAD + row, n), :] = diag
                self.scale[c, pl.ds(PAD + row, n), :] = DAMPING / diag

    def pairs(self, ref, col, row, count):
        return (
            ref[col, pl.ds(PAD + 2 * row, count, stride=2), :],
            ref[col, pl.ds(PAD + 2 * row + 1, count, stride=2), :],
        )

    def coarse_faces(self, col, row, count):
        lane = lane_of(count)
        lower, upper = self.pairs(self.east, col, row, count)
        east = upper_of(lower + upper, self.shift, lane)
        _, upper = self.pairs(self.north, col, row, count)
        north = pair_sum(upper, self.shift, lane)
        lower, upper = self.pairs(self.source, col, row, count)
        return east, north, pair_sum(lower + upper, self.shift, lane)

    def coarse_rhs(self, col, row, count):
        lower, upper = self.pairs(self.tmp, col, row, count)
        return pair_sum(lower + upper, self.shift, lane_of(count))

    def descend(self):
        n = self.chunk
        for row in self.chunks():
            for c in range(3):
                self.vb[c, pl.ds(PAD + row, n), :] = self.load(self.scale, c, row, n) * self.load(self.rhs, c, row, n)
        self.smooth(self.vb, self.va)
        for row in self.chunks():
            _, image = self.apply(self.va, row, n)
            for c in range(3):
                self.tmp[c, pl.ds(PAD + row, n), :] = self.load(self.rhs, c, row, n) - image[c]

    def rise(self, coarse, offset, masked):
        begin = (self.rim - 4) // 8 * 8
        count = self.rows - 2 * begin
        n = 16
        for row in range(begin // 2, (begin + count) // 2, n // 2):
            for c in range(3):
                added = coarse[c, pl.ds(offset + row, n // 2), :]
                for odd in range(2):
                    at = pl.ds(PAD + 2 * row + odd, n // 2, stride=2)
                    own = jnp.where(self.source[c, at, :] > 0.0, added, 0.0) if masked else added
                    self.va[c, at, :] = self.va[c, at, :] + own
        chunks = [(row, n) for row in range(begin, begin + count, n)]
        self.smooth(self.va, self.vb, chunks)
        self.smooth(self.vb, self.va, chunks)


def body(
    shape, forcing, surface, sea, depth_levels, solution_out, residual_out,
    in_f, in_i, fields, *rest
):
    lat_count, lon_count, ring = shape
    level_refs = [rest[0:8], rest[8:18], rest[18:28]]
    near_fields, near_refs = rest[28], [rest[29:37], rest[37:47], rest[47:57]]
    (
        west_pack, east_pack, east_rim, west_rim, near_packs, near_rims, near_corners, metric,
        face_slots, rhs_slots, side_slots, faces, rhs, sides, bottom, piece,
        in_sem, out_sem, rim_send, rim_recv, slot_send, slot_recv,
        plane_send, plane_recv, pass_send, pass_recv,
    ) = rest[57:]
    planes_y = lon_count // ring
    planes_x = lat_count // CORES
    tiles = lon_count * (COLS >> 3) // LANES
    per_line = tiles // planes_y
    la, lo = lax.axis_index("lat"), lax.axis_index("lon")
    x, core = la // CORES, la % CORES
    y, z = lo // ring, lo % ring
    own_rows = ROWS >> 3
    group = LANES // (COLS >> 3)

    def levels_of(rim, base, refs):
        first = (*refs[0][0:3], base.at[2], *refs[0][3:5], base.at[1], *refs[0][5:8])
        return [Level(0, rim, first), Level(1, rim, refs[1]), Level(2, rim, refs[2])]

    levels = levels_of(RIM, fields, level_refs)
    near_levels = levels_of(NEAR, near_fields, near_refs)
    top = levels[0]

    def device(lat, lon):
        return {"lat": lat, "lon": lon}

    loads = []
    for k, ref in enumerate((forcing, surface)):
        for c in range(2):
            loads.append(pltpu.make_async_copy(ref.at[:, pl.ds(c * LANES, LANES)], in_f.at[k, c], in_sem))
    for k, ref in enumerate((sea, depth_levels)):
        for c in range(2):
            loads.append(pltpu.make_async_copy(ref.at[:, pl.ds(c * LANES, LANES)], in_i.at[k, c], in_sem))
    rims = [(dy, dx) for dy in (-1, 0, 1) for dx in (-1, 0, 1) if (dy, dx) != (0, 0)]
    hops = sorted(
        ((dx, dy) for dx in range(planes_x) for dy in range(planes_y) if (dx, dy) != (0, 0)),
        key=lambda d: -min(d[0], planes_x - d[0]) - min(d[1], planes_y - d[1]),
    )
    ring_steps = sorted(range(1, ring), key=lambda d: -min(d, ring - d))
    barrier = pltpu.get_barrier_semaphore()

    def greet(lat, lon):
        pl.semaphore_signal(barrier, inc=1, device_id=device(lat, lon), device_id_type=MESH)

    def beside(dy, dx):
        return la + dy, lax.rem(lo + dx + lon_count, lon_count)

    def ring_peer(step):
        return la, y * ring + lax.rem(z + step, ring)

    def plane_peer(dx, dy, other=0):
        return lax.rem(x + dx, planes_x) * CORES + (1 - core if other else core), lax.rem(y + dy, planes_y) * ring + z

    partner = (x * CORES + (1 - core), lo)
    inside = {-1: la > 0, 0: None, 1: la < lat_count - 1}

    def where_inside(dy, act):
        if dy == 0:
            act()
        else:
            pl.when(inside[dy])(act)

    for dx, dy in hops:
        greet(*plane_peer(dx, dy))
    for step in ring_steps:
        greet(*ring_peer(step))
    for dy, dx in sorted(rims, key=lambda d: (d[1] == 0, d[0] == 0)):
        where_inside(dy, lambda dy=dy, dx=dx: greet(*beside(dy, dx)))
    for load in loads:
        load.start()

    def clear(ref, col, row, count):
        ref[col, pl.ds(row, count), :] = jnp.zeros((count, LANES), ref.dtype)

    for base, group_of in ((fields, levels), (near_fields, near_levels)):
        for c in range(3):
            for k in range(3):
                clear(base.at[k], c, 0, PAD)
                clear(base.at[k], c, PAD + group_of[0].rows, PAD)
            for level in group_of:
                for ref in (level.north, level.va, level.vb):
                    clear(ref, c, 0, PAD)
                    clear(ref, c, PAD + level.rows, PAD)
    for ref in (faces.at[1], rhs, bottom.at[0], bottom.at[3], bottom.at[6]):
        for t in range(tiles):
            clear(ref, t, 0, PAD)
            clear(ref, t, PAD + lat_count * own_rows, PAD)
    for dy, row, near_row in ((-1, 0, 0), (1, RIM + ROWS, NEAR + ROWS)):

        @pl.when(jnp.logical_not(inside[dy]))
        def _(dy=dy, row=row, near_row=near_row):
            for k in range(3):
                for c in range(2):
                    clear(fields.at[k], c, PAD + row, RIM)
                    clear(near_fields.at[k], c, PAD + near_row, NEAR)
            for side in range(2):
                clear(near_corners.at[side], (dy + 1) // 2, 0, NEAR)
            east_rim[pl.ds(row, RIM), :] = jnp.zeros((RIM, LANES), jnp.float32)
            west_rim[pl.ds(row, RIM), :] = jnp.zeros((RIM, LANES), jnp.float32)

    first = la * ROWS - RIM
    for row in range(0, ROWS + 2 * RIM, CHUNK):
        number = (first + row + lax.broadcasted_iota(jnp.int32, (CHUNK, LANES), 0)).astype(jnp.float32)
        metric[0, pl.ds(row, CHUNK), :] = cosines(number + 0.5)
        metric[2, pl.ds(row, CHUNK), :] = 1.0 / metric[0, pl.ds(row, CHUNK), :]
        metric[1, pl.ds(row, CHUNK), :] = cosines(number + 1.0)

    for load in loads:
        load.wait()
    near_strips = [None, None]
    for row in range(0, ROWS, CHUNK):
        at = pl.ds(PAD + RIM + row, CHUNK)
        center = metric[0, pl.ds(RIM + row, CHUNK), :]
        own = pl.ds(row, CHUNK)
        lane = lane_of(CHUNK)
        values = []
        for c in range(2):
            sea_mask = in_i[0, c, own, :].astype(jnp.float32)
            layers = in_i[1, c, own, :].astype(jnp.float32)
            deep = sea_mask * ((layers + layers * (layers - 1.0) / 20.0) / 200.0)
            right = in_f[0, c, own, :] * sea_mask
            source = in_f[1, c, own, :] * center * sea_mask
            values.append((deep, right, source))
            for k in range(3):
                fields[k, c, at, :] = values[c][k]
                near_fields[k, c, pl.ds(PAD + NEAR + row, CHUNK), :] = values[c][k]
        packed_west, packed_east = values[0][0], values[1][0]
        for k in range(1, 3):
            part = (lane >= RIM * k) & (lane < RIM * (k + 1))
            packed_west = jnp.where(part, pltpu.roll(values[0][k], RIM * k, 1), packed_west)
            part = (lane < LANES - RIM * k) & (lane >= LANES - RIM * (k + 1))
            packed_east = jnp.where(part, pltpu.roll(values[1][k], LANES - RIM * k, 1), packed_east)
        west_pack[own, :] = packed_west
        east_pack[own, :] = packed_east
        for side in range(2):
            for k in range(3):
                place = row * 2 + NEAR * k
                moved = pltpu.roll(values[side][k], (place + NEAR * side) % LANES, 1)
                part = (lane >= place) & (lane < place + NEAR)
                near_strips[side] = moved if near_strips[side] is None else jnp.where(part, moved, near_strips[side])
    for side in range(2):
        near_packs[side] = near_strips[side]

    own3 = RIM >> 3
    lane = lane_of(own_rows)
    line_row = lax.broadcasted_iota(jnp.int32, (own_rows, LANES), 0)
    pick = (lane % 16) * 8
    low = (lane % 32) < 16

    def dense(west_tile, east_tile, last=0):
        return jnp.where(
            low, jnp.take_along_axis(west_tile, pick + last, axis=1), jnp.take_along_axis(east_tile, pick + last, axis=1)
        )

    def lane_sum(value):
        for shift in (1, 2, 4):
            value = pair_sum(value, shift, lane)
        return value

    def every8(k, c, row):
        return fields[k, c, pl.ds(PAD + RIM + row, own_rows, stride=8), :]

    sums = [[None, None] for _ in range(3)]
    for row in range(8):
        deep = [every8(0, c, row) for c in range(2)]
        east = east_of(deep, 1, lane)
        inverse = metric[2, pl.ds(RIM + row, own_rows, stride=8), :]
        for c in range(2):
            face, term = jnp.minimum(deep[c], east[c]) * inverse, every8(2, c, row)
            sums[0][c] = face if row == 0 else sums[0][c] + face
            sums[2][c] = term if row == 0 else sums[2][c] + term
    for c in range(2):
        above = pltpu.roll(every8(0, c, 0), own_rows - 1, 0)
        face = jnp.minimum(every8(0, c, 7), above) * metric[1, pl.ds(RIM + 7, own_rows, stride=8), :]
        sums[1][c] = lane_sum(face)
        sums[2][c] = lane_sum(sums[2][c])
    parts = [dense(*sums[0], last=7), dense(*sums[1]), dense(*sums[2])]
    face_slots[z] = jnp.where(lane < 32, parts[0], jnp.where(lane < 64, parts[1], parts[2]))

    greeted = 2 + (ring - 1) + len(hops)
    both = inside[-1].astype(jnp.int32) + inside[1].astype(jnp.int32)
    pl.semaphore_wait(barrier, greeted + 3 * both)

    def to_beside(source, target, k, dy, dx):
        return pltpu.make_async_remote_copy(
            source, target, rim_send.at[k], rim_recv.at[k],
            device_id=device(*beside(dy, dx)), device_id_type=MESH,
        )

    def rim_copy(dy, dx):
        k = 1 if dx == 0 else 2
        if dx == 0:
            source_row, target_row = (ROWS - RIM, 0) if dy > 0 else (0, RIM + ROWS)
            return to_beside(
                fields.at[:, pl.ds(0, 2), pl.ds(PAD + RIM + source_row, RIM), :],
                fields.at[:, pl.ds(0, 2), pl.ds(PAD + target_row, RIM), :], k, dy, dx,
            )
        source_row, target_row = {1: (ROWS - RIM, 0), -1: (0, RIM + ROWS), 0: (0, RIM)}[dy]
        count = ROWS if dy == 0 else RIM
        return to_beside(
            (east_pack if dx > 0 else west_pack).at[pl.ds(source_row, count), :],
            (west_rim if dx > 0 else east_rim).at[pl.ds(target_row, count), :], k, dy, dx,
        )

    def near_copy(dy, dx):
        k = 0
        if dx == 0:
            source_row, target_row = (ROWS - NEAR, 0) if dy > 0 else (0, NEAR + ROWS)
            return to_beside(
                near_fields.at[:, pl.ds(0, 2), pl.ds(PAD + NEAR + source_row, NEAR), :],
                near_fields.at[:, pl.ds(0, 2), pl.ds(PAD + target_row, NEAR), :], k, dy, dx,
            )
        side = (dx + 1) // 2
        if dy == 0:
            return to_beside(near_packs.at[side], near_rims.at[side], k, dy, dx)
        source_row = NEAR if dy > 0 else 0
        return to_beside(
            near_packs.at[side, pl.ds(source_row, NEAR), :], near_corners.at[side, (1 - dy) // 2], k, dy, dx
        )

    def all_rims(k, wait):
        per_side = ((6 + 2) * NEAR, 6 * RIM, 2 * RIM)[k]
        level_with = (ROWS, 0, 2 * ROWS)[k]
        between = jnp.logical_and(inside[-1], inside[1])
        for when, count in ((between, 2 * per_side + level_with), (jnp.logical_not(between), per_side + level_with)):

            @pl.when(when)
            def _(count=count):
                as_much = fields.at[pl.ds(0, 2), pl.ds(0, 2), pl.ds(0, count // 4), :]
                wait(to_beside(as_much, as_much, k, 0, 1))

    def slot_copy(slots, which, step):
        return pltpu.make_async_remote_copy(
            slots.at[z], slots.at[z], slot_send.at[which], slot_recv.at[which],
            device_id=device(*ring_peer(step)), device_id_type=MESH,
        )

    def all_slots(slots, which):
        return pltpu.make_async_remote_copy(
            slots.at[pl.ds(0, ring - 1)], slots.at[pl.ds(0, ring - 1)], slot_send.at[which], slot_recv.at[which],
            device_id=device(*ring_peer(1)), device_id_type=MESH,
        )

    def plane_block(which, lat, line):
        rows = pl.ds(pl.multiple_of(PAD + lat * own_rows, 8), own_rows)
        if which == 0:
            return faces.at[:, pl.ds(line * per_line, per_line), rows, :]
        if which == 1:
            return rhs.at[pl.ds(line * per_line, per_line), rows, :]
        return sides.at[line, rows, :]

    groups = [hops[0:5], hops[5:11], hops[11:]] if len(hops) == 15 else [hops]

    def plane_copy(which, dx, dy):
        block = plane_block(which, la, y)
        group_at = [g for g, group_hops in enumerate(groups) if (dx, dy) in group_hops][0]
        return pltpu.make_async_remote_copy(
            block, block, plane_send.at[which], plane_recv.at[which, group_at],
            device_id=device(*plane_peer(dx, dy)), device_id_type=MESH,
        )

    def all_planes(which):
        count = len(hops)
        lines, rows = (3, count // 3 * 8) if count % 3 == 0 else (1, count * 8)
        rows, of_tiles = pl.ds(0, rows), pl.ds(0, lines * per_line)
        block = (faces.at[:, of_tiles, rows, :], rhs.at[of_tiles, rows, :], sides.at[pl.ds(0, lines), rows, :])[which]
        return pltpu.make_async_remote_copy(
            block, block, plane_send.at[which], plane_recv.at[which, 0],
            device_id=device(*partner), device_id_type=MESH,
        )

    def pass_copy(which, lat, line):
        block = plane_block(which, lat, line)
        return pltpu.make_async_remote_copy(
            block, block, pass_send.at[which], pass_recv.at[which],
            device_id=device(*partner), device_id_type=MESH,
        )

    def all_passed(which):
        half = pl.ds(PAD, lat_count * own_rows // CORES)
        block = (faces.at[:, :, half, :], rhs.at[:, half, :], sides.at[:, half, :])[which]
        return pltpu.make_async_remote_copy(
            block, block, pass_send.at[which], pass_recv.at[which],
            device_id=device(*partner), device_id_type=MESH,
        )

    def send_plane(which):
        for dx, dy in hops:
            plane_copy(which, dx, dy).start()
        pass_copy(which, la, y).start()

    def sent(which):
        all_planes(which).wait_send()
        all_passed(which).wait_send()

    def take(which):
        for g, group_hops in enumerate(groups):
            rows = pl.ds(0, len(group_hops) * own_rows)
            line = pl.ds(0, per_line)
            block = (faces.at[:, line, rows, :], rhs.at[line, rows, :], sides.at[0, rows, :])[which]
            pltpu.make_async_remote_copy(
                block, block, plane_send.at[which], plane_recv.at[which, g],
                device_id=device(*partner), device_id_type=MESH,
            ).wait_recv()
            for dx, dy in group_hops:
                pass_copy(
                    which, lax.rem(x - dx + planes_x, planes_x) * CORES + core, lax.rem(y - dy + planes_y, planes_y)
                ).start()

    order = sorted(rims, key=lambda d: (d[1] == 0, d[0] == 0))
    for dy, dx in order:
        where_inside(dy, lambda dy=dy, dx=dx: near_copy(dy, dx).start())
    for step in ring_steps:
        slot_copy(face_slots, 0, step).start()
    for dy, dx in order:
        where_inside(dy, lambda dy=dy, dx=dx: rim_copy(dy, dx).start())

    def find_faces(some, base):
        first = some[0]
        n = first.chunk
        for row in first.chunks():
            deep = [first.load(base.at[0], c, row, n) for c in range(3)]
            east = east_of(deep, 1, lane_of(n))
            inverse = metric[2, pl.ds(RIM - first.rim + row, n), :]
            northern = metric[1, pl.ds(RIM - first.rim + row, n), :]
            for c in range(3):
                at = pl.ds(PAD + row, n)
                first.east[c, at, :] = jnp.minimum(deep[c], east[c]) * inverse
                first.north[c, at, :] = jnp.minimum(deep[c], first.load(base.at[0], c, row + 1, n)) * northern
        for fine, coarse in zip(some, some[1:]):
            for row in coarse.chunks():
                for c in range(3):
                    at = pl.ds(PAD + row, coarse.chunk)
                    coarse.east[c, at, :], coarse.north[c, at, :], coarse.source[c, at, :] = fine.coarse_faces(c, row, coarse.chunk)

    def descend(some):
        some[0].finish()
        some[0].descend()
        for fine, coarse in zip(some, some[1:]):
            for row in coarse.chunks():
                for c in range(3):
                    coarse.rhs[c, pl.ds(PAD + row, coarse.chunk), :] = fine.coarse_rhs(c, row, coarse.chunk)
            coarse.finish()
            coarse.descend()

    all_rims(0, lambda copy: copy.wait_recv())

    half_rows = ROWS // 2
    for row, count, quarter in (
        (0, NEAR, 1), (NEAR, half_rows, 0), (NEAR + half_rows, half_rows, 1), (NEAR + ROWS, NEAR, 0)
    ):
        wide_lane = lane_of(count)
        if count == NEAR:
            east, west = (near_corners[side, 0 if row == 0 else 1] for side in range(2))
        else:
            east, west = near_rims[0], near_rims[1]
        for k in range(3):
            place = quarter * (LANES // 2) + NEAR * k
            moved_east = pltpu.roll(east, LANES - place, 1) if place else east
            moved_west = pltpu.roll(west, LANES - NEAR - place, 1)
            near_fields[k, 2, pl.ds(PAD + row, count), :] = jnp.where(
                wide_lane < NEAR, moved_east, jnp.where(wide_lane >= LANES - NEAR, moved_west, 0.0)
            )

    find_faces(near_levels, near_fields)
    near3 = NEAR >> 3
    bottom_faces = [near_levels[2].coarse_faces(c, near3, own_rows) for c in range(2)]
    last = jnp.take_along_axis(bottom_faces[1][0], jnp.full_like(lane, LANES - 1), axis=1)
    last = jnp.where(lane % 8 == line_row, last, 0.0)
    for shift in (4, 2, 1):
        last = last + pltpu.roll(last, shift, 0)
    north = pltpu.roll(dense(bottom_faces[0][1], bottom_faces[1][1]), 1, 0)
    side_slots[z] = jnp.where(line_row == 0, north, last)[0:2]
    for step in ring_steps:
        slot_copy(side_slots, 2, step).start()
    descend(near_levels)

    bottom_rhs = [near_levels[2].coarse_rhs(c, near3, own_rows) for c in range(2)]
    packed = jnp.where(lane // 32 == line_row // 2, dense(*bottom_rhs), 0.0)
    for shift in (4, 2):
        packed = packed + pltpu.roll(packed, shift, 0)
    rhs_slots[z] = packed[0:2]
    for step in ring_steps:
        slot_copy(rhs_slots, 1, step).start()

    own_at = pl.ds(pl.multiple_of(PAD + la * own_rows, 8), own_rows)
    all_slots(face_slots, 0).wait_recv()
    for h in range(per_line):
        for k in range(3):
            value = None
            for j in range(group):
                slot = face_slots[h * group + j]
                shift = (32 * (j - k)) % LANES
                moved = pltpu.roll(slot, shift, 1) if shift else slot
                value = moved if value is None else jnp.where(lane // 32 == j, moved, value)
            faces[k, y * per_line + h, own_at, :] = value
    send_plane(0)

    def spread(ref, j, row):
        return jnp.broadcast_to(ref[j, pl.ds(row, 1), :], (own_rows, LANES))

    for k in (1, 2):
        all_rims(k, lambda copy: copy.wait_recv())
    for row in range(0, ROWS + 2 * RIM, CHUNK):
        wide_lane = lane_of(CHUNK)
        east, west = east_rim[pl.ds(row, CHUNK), :], west_rim[pl.ds(row, CHUNK), :]
        for k in range(3):
            moved_east = pltpu.roll(east, LANES - RIM * k, 1) if k else east
            moved_west = pltpu.roll(west, RIM * k, 1) if k else west
            fields[k, 2, pl.ds(PAD + row, CHUNK), :] = jnp.where(
                wide_lane < RIM, moved_east, jnp.where(wide_lane >= LANES - RIM, moved_west, 0.0)
            )
    find_faces(levels, fields)
    descend(levels)

    all_slots(side_slots, 2).wait_recv()
    side = None
    for j in range(ring):
        value = spread(side_slots, j, 1)
        side = value if side is None else jnp.where(lane // 8 == j, value, side)
    for h in range(per_line):
        for j in range(group):
            side = jnp.where((line_row == 7 - h) & (lane // 32 == j), spread(side_slots, h * group + j, 0), side)
    sides[y, own_at, :] = side
    send_plane(2)

    all_slots(rhs_slots, 1).wait_recv()
    unpick = 32 * (line_row // 2) + lane % 32
    for h in range(per_line):
        value = None
        for j in range(group):
            both_rows = jnp.where(line_row % 2 == 0, spread(rhs_slots, h * group + j, 0), spread(rhs_slots, h * group + j, 1))
            moved = jnp.take_along_axis(both_rows, unpick, axis=1)
            value = moved if value is None else jnp.where(lane // 32 == j, moved, value)
        rhs[y * per_line + h, own_at, :] = value
    send_plane(1)
    take(0)
    take(2)
    take(1)

    height = lat_count * own_rows
    everything = pl.ds(PAD, height)
    lane3 = lane_of(height)
    west_face, diagonal = bottom.at[1], bottom.at[2]
    rest_ref, image_ref, along_ref = bottom.at[0], bottom.at[3], bottom.at[4]
    image_image, far_ref = bottom.at[7], bottom.at[8]
    all_passed(0).wait_recv()
    all_passed(2).wait_recv()
    east_face, north_face = bottom.at[5], bottom.at[6]
    lane_lat = lane_of(lat_count)
    for t in range(tiles):
        h, line = t % per_line, t // per_line
        north_face[t, everything, :] = faces[1, t, everything, :]
        north_face[t, pl.ds(PAD + 7, lat_count, stride=8), :] = sides[line, pl.ds(PAD + 7 - h, lat_count, stride=8), :]
        east = sides[line, pl.ds(PAD, lat_count, stride=8), :]
        for row in range(own_rows):
            at = pl.ds(PAD + row, lat_count, stride=8)
            moved = jnp.take_along_axis(east, 8 * (h * group + lane_lat // 32) + row, axis=1)
            east_face[t, at, :] = jnp.where(lane_lat % 32 == 31, moved, faces[0, t, at, :])
    for t in range(tiles):
        east = east_face[t, everything, :]
        before = east_face[(t - 1) % tiles, everything, :]
        west = pltpu.roll(jnp.where(lane3 >= LANES - 1, before, east), 1, 1)
        west_face[t, everything, :] = west
        diagonal[t, everything, :] = (
            faces[2, t, everything, :] + east + west
            + north_face[t, everything, :] + north_face[t, pl.ds(PAD - 1, height), :]
        )
    all_passed(1).wait_recv()

    part = 16
    lane3 = lane_of(part)
    pieces = [(t, row) for t in range(tiles) for row in range(PAD, PAD + height, part)]

    def add(total, value):
        return value if total is None else total + value

    def operate(ref, target, sums):
        norm, product = None, None
        for t, row in pieces:
            at = pl.ds(row, part)
            value = ref[t, at, :]
            east = pltpu.roll(jnp.where(lane3 < 1, ref[(t + 1) % tiles, at, :], value), LANES - 1, 1)
            west = pltpu.roll(jnp.where(lane3 >= LANES - 1, ref[(t - 1) % tiles, at, :], value), 1, 1)
            image = diagonal[t, at, :] * value - (
                east_face[t, at, :] * east
                + west_face[t, at, :] * west
                + north_face[t, at, :] * ref[t, pl.ds(row + 1, part), :]
                + north_face[t, pl.ds(row - 1, part), :] * ref[t, pl.ds(row - 1, part), :]
            )
            target[t, at, :] = image
            if sums:
                norm, product = add(norm, value * value), add(product, value * image)
        if sums:
            return jnp.sum(norm, keepdims=True), jnp.sum(product, keepdims=True)

    own_tile = lo // group
    near_tiles = (lax.rem(own_tile - 1 + tiles, tiles), own_tile, lax.rem(own_tile + 1, tiles))
    near = pl.ds(pl.multiple_of(la * own_rows, 8), 2 * PAD + own_rows)
    solved = [None] * 3
    direction = [None] * 3
    norm, product = operate(rhs, image_ref, True)
    beta = None
    for iteration in range(BOTTOM_ITERS):
        final = iteration == BOTTOM_ITERS - 1
        current = rhs if iteration == 0 else rest_ref
        if not final:
            operate(image_ref, image_image, False)
        if iteration:
            beta = norm * inverse_norm
            product = product - beta * norm * inverse_alpha
        alpha = norm / product
        inverse_norm = 1.0 / norm
        inverse_alpha = product * inverse_norm
        for k in range(3):
            value = current[near_tiles[k], near, :]
            direction[k] = value if iteration == 0 else value + beta * direction[k]
            solved[k] = alpha * direction[k] if iteration == 0 else solved[k] + alpha * direction[k]
        if final:
            break
        norm, product = None, None
        for t, row in pieces:
            at = pl.ds(row, part)
            image = image_ref[t, at, :]
            along, far = image, image_image[t, at, :]
            if iteration:
                along = along + beta * along_ref[t, at, :]
                far = far + beta * far_ref[t, at, :]
            rest = current[t, at, :] - alpha * along
            image = image - alpha * far
            rest_ref[t, at, :] = rest
            if iteration < BOTTOM_ITERS - 2:
                along_ref[t, at, :] = along
                far_ref[t, at, :] = far
                image_ref[t, at, :] = image
            norm, product = add(norm, rest * rest), add(product, rest * image)
        norm, product = jnp.sum(norm, keepdims=True), jnp.sum(product, keepdims=True)

    quarter = (lo % group) * 32
    lane = lane_of(8)
    place = quarter + jnp.where(lane < LANES // 2, 32 + lane // 8, (lane - LANES) // 8)
    wrapped = place & (LANES - 1)
    for row in range(0, 2 * PAD + own_rows, 8):
        left, mine, right = (solved[k][row : row + 8] for k in range(3))
        piece[0, pl.ds(row, 8), :] = jnp.take_along_axis(mine, quarter + lane // 8, axis=1)
        piece[1, pl.ds(row, 8), :] = jnp.take_along_axis(mine, quarter + 16 + lane // 8, axis=1)
        piece[2, pl.ds(row, 8), :] = jnp.where(
            place < 0, jnp.take_along_axis(left, wrapped, axis=1),
            jnp.where(place >= LANES, jnp.take_along_axis(right, wrapped, axis=1), jnp.take_along_axis(mine, wrapped, axis=1)),
        )

    levels[2].rise(piece, PAD - own3, False)
    levels[1].rise(levels[2].va, PAD, False)
    levels[0].rise(levels[1].va, PAD, True)
    stores = []
    for c in range(2):
        stores.append(pltpu.make_async_copy(
            top.va.at[c, pl.ds(PAD + RIM, ROWS), :], solution_out.at[:, pl.ds(c * LANES, LANES)], out_sem))
        stores[-1].start()
    for row in range(RIM, RIM + ROWS, CHUNK):
        _, image = top.apply(top.va, row, CHUNK, cols=2)
        for c in range(2):
            top.tmp[c, pl.ds(PAD + row, CHUNK), :] = top.load(top.rhs, c, row, CHUNK) - image[c]
    for c in range(2):
        stores.append(pltpu.make_async_copy(
            top.tmp.at[c, pl.ds(PAD + RIM, ROWS), :], residual_out.at[:, pl.ds(c * LANES, LANES)], out_sem))
        stores[-1].start()

    for k in range(3):
        all_rims(k, lambda copy: copy.wait_send())
    for which, slots in enumerate((face_slots, rhs_slots, side_slots)):
        all_slots(slots, which).wait_send()
        sent(which)
    for store in stores:
        store.wait()


def put_out(solution_in, residual_in, solution_out, residual_out, sems):
    copies = [
        pltpu.make_async_copy(solution_in, solution_out, sems.at[0]),
        pltpu.make_async_copy(residual_in, residual_out, sems.at[1]),
    ]
    for copy in copies:
        copy.start()
    for copy in copies:
        copy.wait()


def solution(mesh, ring=RING):
    lat_count, lon_count = mesh.shape["lat"], mesh.shape["lon"]
    tiles = lon_count * (COLS >> 3) // LANES
    height = lat_count * (ROWS >> 3) + 2 * PAD
    f32 = jnp.float32

    def padded(level, rim=RIM):
        return pltpu.VMEM((3, ((ROWS + 2 * rim) >> level) + 2 * PAD, LANES), f32)

    rows = ROWS + 2 * RIM
    scratch = [
        pltpu.VMEM((2, 2, ROWS, LANES), f32),
        pltpu.VMEM((2, 2, ROWS, LANES), jnp.int32),
        pltpu.VMEM((3, 3, rows + 2 * PAD, LANES), f32),
        *[padded(0)] * 8,
        *[padded(1)] * 10,
        *[padded(2)] * 10,
        pltpu.VMEM((3, 3, ROWS + 2 * NEAR + 2 * PAD, LANES), f32),
        *[padded(0, NEAR)] * 8,
        *[padded(1, NEAR)] * 10,
        *[padded(2, NEAR)] * 10,
        pltpu.VMEM((ROWS, LANES), f32),
        pltpu.VMEM((ROWS, LANES), f32),
        pltpu.VMEM((rows, LANES), f32),
        pltpu.VMEM((rows, LANES), f32),
        pltpu.VMEM((2, ROWS // 2, LANES), f32),
        pltpu.VMEM((2, ROWS // 2, LANES), f32),
        pltpu.VMEM((2, 2, NEAR, LANES), f32),
        pltpu.VMEM((3, rows, LANES), f32),
        pltpu.VMEM((ring, 8, LANES), f32),
        pltpu.VMEM((ring, 2, LANES), f32),
        pltpu.VMEM((ring, 2, LANES), f32),
        pltpu.VMEM((3, tiles, height, LANES), f32),
        pltpu.VMEM((tiles, height, LANES), f32),
        pltpu.VMEM((lon_count // ring, height, LANES), f32),
        pltpu.VMEM((9, tiles, height, LANES), f32),
        pltpu.VMEM((3, 2 * PAD + (ROWS >> 3), LANES), f32),
        pltpu.SemaphoreType.DMA,
        pltpu.SemaphoreType.DMA,
        *[pltpu.SemaphoreType.DMA((3,))] * 5,
        pltpu.SemaphoreType.DMA((3, 3)),
        *[pltpu.SemaphoreType.DMA((3,))] * 2,
    ]

    def step(forcing, surface_term, sea_cells, levels):
        out = jax.ShapeDtypeStruct(forcing.shape, f32)
        results = pl.pallas_call(
            functools.partial(body, (lat_count, lon_count, ring)),
            out_shape=(out, out),
            in_specs=[pl.BlockSpec(memory_space=pltpu.HBM)] * 4,
            out_specs=[pl.BlockSpec(memory_space=pl.ANY)] * 2,
            scratch_shapes=scratch,
            compiler_params=pltpu.CompilerParams(
                collective_id=0, has_side_effects=True, vmem_limit_bytes=48 << 20
            ),
        )(*(pltpu.with_memory_space_constraint(v, pltpu.HBM) for v in (forcing, surface_term, sea_cells, levels)))
        return pl.pallas_call(
            put_out,
            out_shape=(out, out),
            in_specs=[pl.BlockSpec(memory_space=pltpu.VMEM)] * 2,
            out_specs=[pl.BlockSpec(memory_space=pltpu.HBM)] * 2,
            scratch_shapes=[pltpu.SemaphoreType.DMA((2,))],
        )(*(pltpu.with_memory_space_constraint(v, pltpu.VMEM) for v in results))

    return jax.shard_map(
        step,
        mesh=mesh,
        in_specs=(P("lat", "lon"),) * 4,
        out_specs=(P("lat", "lon"),) * 2,
        check_vma=False,
    )
```
